32 devices in a mesh: fsdp: 8 (over y, x, core), dp: 4 (over z).
Axes of the slice: x: 2, y: 2, z: 4, core: 2. Of those that a mesh axis runs over, the one named last changes fastest.
Arguments:
- inputs: bfloat16 [8, 1024, 2048], P(None, 'fsdp'), may hold values from -6 to 6
- cotangent: bfloat16 [8, 1024, 2048], P(None, 'fsdp'), may hold values from -6 to 6
- piece_start: int32 [8, 2], replicated, may hold values from 0 to 768, as said below
- piece_image: int32 [8, 2], replicated, may hold values from 0 to 1
- valid_mask: int32 [8, 1024], replicated, may hold values from 0 to 1, as said below
- query_weight: bfloat16 [2048, 2048], P('fsdp', 'dp'), may hold values from -0.125 to 0.125
- key_weight: bfloat16 [2048, 2048], P('fsdp', 'dp'), may hold values from -0.125 to 0.125
- value_weight: bfloat16 [2048, 2048], P('fsdp', 'dp'), may hold values from -0.125 to 0.125
- output_weight: bfloat16 [2048, 2048], P('dp', 'fsdp'), may hold values from -1.5 to 1.5
- attn_gain: bfloat16 [2048], P('fsdp'), may hold values from 0.5 to 1.5
- gate_weight: bfloat16 [2048, 8192], P('fsdp', 'dp'), may hold values from -0.125 to 0.125
- up_weight: bfloat16 [2048, 8192], P('fsdp', 'dp'), may hold values from -0.125 to 0.125
- down_weight: bfloat16 [8192, 2048], P('dp', 'fsdp'), may hold values from -0.0625 to 0.0625
- mlp_gain: bfloat16 [2048], P('fsdp'), may hold values from 0.5 to 1.5
Outputs:
- output: bfloat16 [8, 1024, 2048], P(None, 'fsdp')
- input_grad: bfloat16 [8, 1024, 2048], P(None, 'fsdp')
- query_grad: float32 [2048, 2048], P('fsdp', 'dp')
- key_grad: float32 [2048, 2048], P('fsdp', 'dp')
- value_grad: float32 [2048, 2048], P('fsdp', 'dp')
- output_weight_grad: float32 [2048, 2048], P('dp', 'fsdp')
- attn_gain_grad: float32 [2048], P('fsdp')
- gate_grad: float32 [2048, 8192], P('fsdp', 'dp')
- up_grad: float32 [2048, 8192], P('fsdp', 'dp')
- down_grad: float32 [8192, 2048], P('dp', 'fsdp')
- mlp_gain_grad: float32 [2048], P('fsdp')
- rms_residual: float32 [], replicated
- rms_attention: float32 [], replicated
- rms_mlp: float32 [], replicated
The draws below stay inside these ranges and needn't reach their ends.
Inputs may be any that keep to these rules, and one draw needn't show every extreme that they name: `piece_start`: the starts of a sequence are distinct multiples of 256, so its 2 pieces do not intersect. `piece_image`: pieces of one sequence with the same number belong to one image. `valid_mask`: in each sequence the valid slots form a prefix of 512 tokens or more.
All inputs are finite; a program needn't handle non-finite values.
Results may differ from the reference program's by a relative error of at most 0.024.
Values may be sent and summed in bfloat16 or wider, within the bound.
A program may use at most 384 MiB of HBM per device.

```python
import jax
import jax.numpy as jnp
from jax import lax

D = 2048
HEADS = 32
HD = 64
FF = 8192
LEN = 1024
PIECE = 256
PIECES = 2
SEQS = 8


def draw_piece_start(key, part):
    subkeys = jax.random.split(key, SEQS)

    def pick(subkey):
        return jax.random.permutation(subkey, LEN // PIECE)[:PIECES]
    return (jax.vmap(pick)(subkeys) * PIECE).astype(jnp.int32)


def draw_valid_mask(key, part):
    lengths = jax.random.randint(key, (SEQS, 1), LEN // 2, LEN + 1)
    places = jnp.arange(LEN, dtype=jnp.int32)[None, :]
    return (places < lengths).astype(jnp.int32)


def with_ends(drawn, stream_key, low, top_value):
    shape = drawn.shape
    spot = [jax.random.randint(jax.random.fold_in(stream_key, axis), (), 0, shape[axis]) for axis in range(len(shape))]
    drawn = drawn.at[tuple(spot)].set(low)
    longest = shape.index(max(shape))
    spot[longest] = (spot[longest] + 1) % shape[longest]
    return drawn.at[tuple(spot)].set(top_value)


def block_scale(key, extent, pieces, low, top_value):
    def one(axis_at, shards_of):
        heights = jax.random.uniform(jax.random.fold_in(jax.random.fold_in(key, 6), axis_at), (shards_of,), jnp.float32, low / len(pieces), top_value / len(pieces))
        return jnp.repeat(jnp.exp(heights), extent[axis_at] // shards_of).reshape((-1,) + (1,) * (len(extent) - axis_at - 1))

    level = one(*pieces[0])
    for cut in pieces[1:]:
        level = level * one(*cut)
    return level


def noise(key, shape, width, most, shards=(), held_as=jnp.bfloat16):
    loudness = block_scale(key, shape, shards, -0.22, 0.18) if shards else 1.0
    drawn = jax.random.normal(key, shape, jnp.float32) * width * loudness
    return jnp.minimum(jnp.maximum(drawn, -most), most).astype(held_as)


def setup_inputs(seed: int = 0) -> dict:
    key_of = jax.random.split(jax.random.key(seed), 15)
    return {
        "inputs": noise(key_of[0], (SEQS, LEN, D), 1.0, 6.0, ((1, 8),)),
        "cotangent": noise(key_of[1], (SEQS, LEN, D), 1.0, 6.0, ((1, 8),)),
        "piece_start": draw_piece_start(jax.random.fold_in(key_of[14], 71), 0),
        "piece_image": with_ends(jax.random.randint(key_of[3], (SEQS, PIECES), 0, PIECES), jax.random.fold_in(key_of[3], 1), 0, PIECES - 1).astype(jnp.int32),
        "valid_mask": draw_valid_mask(jax.random.fold_in(key_of[14], 71), 0),
        "query_weight": noise(key_of[5], (D, D), D ** -0.5, 0.125, ((0, 8), (1, 4))),
        "key_weight": noise(key_of[6], (D, D), D ** -0.5, 0.125, ((0, 8), (1, 4))),
        "value_weight": noise(key_of[7], (D, D), D ** -0.5, 0.125, ((0, 8), (1, 4))),
        "output_weight": noise(key_of[8], (D, D), (D // 128) ** -0.5, 1.5, ((0, 4), (1, 8))),
        "attn_gain": jnp.clip(1.0 + 0.1 * jax.random.normal(key_of[9], (D,), jnp.float32), 0.5, 1.5).astype(jnp.bfloat16),
        "gate_weight": noise(key_of[10], (D, FF), D ** -0.5, 0.125, ((0, 8), (1, 4))),
        "up_weight": noise(key_of[11], (D, FF), D ** -0.5, 0.125, ((0, 8), (1, 4))),
        "down_weight": noise(key_of[12], (FF, D), FF ** -0.5, 0.0625, ((0, 4), (1, 8))),
        "mlp_gain": jnp.clip(1.0 + 0.1 * jax.random.normal(key_of[13], (D,), jnp.float32), 0.5, 1.5).astype(jnp.bfloat16),
    }


EPS = 1e-05
THETA = 130000.0
NEG = -1e+30
HIGH = lax.Precision.HIGHEST

@jax.custom_vjp
def low(v):
    return lax.optimization_barrier(v.astype(jnp.bfloat16)).astype(jnp.float32)

@jax.custom_vjp
def low_back(v):
    return v

def low_keep(v):
    return (low(v), None)

def low_pass(kept, grad):
    return (grad,)

def back_keep(v):
    return (v, None)

def back_low(kept, grad):
    return (low(grad),)
low.defvjp(low_keep, low_pass)
low_back.defvjp(back_keep, back_low)

def rope_tables(positions, head_size):
    half = head_size // 2
    rates = THETA ** (-(jnp.arange(half, dtype=jnp.float32) * 2.0 / head_size))
    angle = positions.astype(jnp.float32)[:, None] * rates[None, :]
    cosine = jnp.concatenate([jnp.cos(angle), jnp.cos(angle)], axis=-1)
    sine = jnp.concatenate([jnp.sin(angle), jnp.sin(angle)], axis=-1)
    return (cosine, sine)

def rotate(values, cosine, sine):
    half = values.shape[-1] // 2
    turned = jnp.concatenate([-values[..., half:], values[..., :half]], axis=-1)
    return values * cosine[:, None, :] + turned * sine[:, None, :]

def image_of(positions, starts, images):
    inside = (positions[:, None] >= starts[None, :]) & (positions[:, None] < starts[None, :] + PIECE)
    return (lax.optimization_barrier(jnp.sum(jnp.where(inside, images[None, :] + 1, 0), axis=1)) - 1).astype(jnp.int32)

def allowed_mask(query_pos, key_pos, query_image, key_image, key_valid):
    causal = key_pos[None, :] <= query_pos[:, None]
    same = (query_image[:, None] >= 0) & (query_image[:, None] == key_image[None, :])
    return (causal | same) & (key_valid[None, :] > 0)

def dense(values, weight):
    return jnp.dot(values, weight, precision=HIGH, preferred_element_type=jnp.float32)

def layer_one(source, starts, images, valid_row, params):
    query_weight, key_weight, value_weight, output_weight, attn_gain, gate_weight, up_weight, down_weight, mlp_gain = params
    positions = jnp.arange(LEN, dtype=jnp.int32)
    cosine, sine = rope_tables(positions, HD)
    scale_one = lax.rsqrt(lax.optimization_barrier(jnp.mean(source * source, axis=1, keepdims=True)) + EPS)
    normed_one = low(source * scale_one * attn_gain)
    queries = low(rotate(low_back(dense(normed_one, query_weight)).reshape(LEN, HEADS, HD), cosine, sine))
    keys_all = low(rotate(low_back(dense(normed_one, key_weight)).reshape(LEN, HEADS, HD), cosine, sine))
    values_all = low(low_back(dense(normed_one, value_weight))).reshape(LEN, HEADS, HD)
    image_ids = image_of(positions, starts, images)
    allowed = allowed_mask(positions, positions, image_ids, image_ids, valid_row)
    raw = jnp.einsum('qhd,khd->hqk', queries, keys_all, precision=HIGH) * HD ** (-0.5)
    scores = jnp.where(allowed[None, :, :], low_back(raw), NEG)
    highest = lax.optimization_barrier(jnp.max(scores, axis=2, keepdims=True))
    log_total = highest + jnp.log(lax.optimization_barrier(jnp.sum(jnp.exp(scores - highest), axis=2, keepdims=True)))
    probs = low(jnp.exp(scores - log_total))
    mixed = jnp.einsum('hqk,khd->qhd', probs, values_all, precision=HIGH).reshape(LEN, D)
    mixed = low(low_back(mixed))
    attn_out = low_back(dense(mixed, output_weight))
    middle = source + attn_out
    scale_two = lax.rsqrt(lax.optimization_barrier(jnp.mean(middle * middle, axis=1, keepdims=True)) + EPS)
    normed_two = low(middle * scale_two * mlp_gain)
    gate = low_back(dense(normed_two, gate_weight))
    up = low_back(dense(normed_two, up_weight))
    activated = low(gate * jax.nn.sigmoid(gate) * up)
    mlp_out = low_back(dense(activated, down_weight))
    rows = valid_row.astype(jnp.float32)[:, None]
    stats = (jnp.sum(middle * middle * rows), jnp.sum(attn_out * attn_out * rows), jnp.sum(mlp_out * mlp_out * rows))
    return (middle + mlp_out, stats)

def reference(inputs, cotangent, piece_start, piece_image, valid_mask, query_weight, key_weight, value_weight, output_weight, attn_gain, gate_weight, up_weight, down_weight, mlp_gain):
    params = tuple((item.astype(jnp.float32) for item in (query_weight, key_weight, value_weight, output_weight, attn_gain, gate_weight, up_weight, down_weight, mlp_gain)))

    def forward(sources, weights):

        def one(totals, item):
            result, stats = jax.checkpoint(layer_one)(item[0], item[1], item[2], item[3], weights)
            return ((totals[0] + stats[0], totals[1] + stats[1], totals[2] + stats[2]), result)
        zero = jnp.zeros((), jnp.float32)
        totals, results = lax.scan(one, (zero, zero, zero), (sources, piece_start, piece_image, valid_mask))
        return (results, totals)
    results, pullback, totals = jax.vjp(forward, inputs.astype(jnp.float32), params, has_aux=True)
    input_grad, grads = pullback(cotangent.astype(jnp.float32))
    count = jnp.sum(valid_mask).astype(jnp.float32) * D
    return (results.astype(jnp.bfloat16), input_grad.astype(jnp.bfloat16), grads[0], grads[1], grads[2], grads[3], grads[4], grads[5], grads[6], grads[7], grads[8], jnp.sqrt(totals[0] / count), jnp.sqrt(totals[1] / count), jnp.sqrt(totals[2] / count))
```

```python
import functools

import jax
import jax.numpy as jnp
from jax import lax
from jax.experimental import pallas as pl
from jax.experimental.pallas import tpu as pltpu
from jax.sharding import PartitionSpec as P


HD = 64
PIECE = 256


EPS = 1e-05
THETA = 130000.0
NEG = -1e30


def rope_tables(positions, head_size):
    half = head_size // 2
    rates = THETA ** (-(jnp.arange(half, dtype=jnp.float32) * 2.0 / head_size))
    angle = positions.astype(jnp.float32)[:, None] * rates[None, :]
    cosine = jnp.concatenate([jnp.cos(angle), jnp.cos(angle)], axis=-1)
    sine = jnp.concatenate([jnp.sin(angle), jnp.sin(angle)], axis=-1)
    return (cosine, sine)


def rotate(values, cosine, sine):
    half = values.shape[-1] // 2
    turned = jnp.concatenate([-values[..., half:], values[..., :half]], axis=-1)
    return values * cosine[:, None, :] + turned * sine[:, None, :]


def unrotate(grads, cosine, sine):
    half = grads.shape[-1] // 2
    scaled = grads * sine[:, None, :]
    turned = jnp.concatenate([scaled[..., half:], -scaled[..., :half]], axis=-1)
    return grads * cosine[:, None, :] + turned


def image_of(positions, starts, images):
    inside = (positions[:, None] >= starts[None, :]) & (
        positions[:, None] < starts[None, :] + PIECE
    )
    return jnp.sum(jnp.where(inside, images[None, :] + 1, 0), axis=1) - 1


def allowed_mask(query_pos, key_pos, query_image, key_image, key_valid):
    causal = key_pos[None, :] <= query_pos[:, None]
    same = (query_image[:, None] >= 0) & (query_image[:, None] == key_image[None, :])
    return (causal | same) & (key_valid[None, :] > 0)


def project(values, weight):
    return jnp.einsum("std,de->ste", values, weight, preferred_element_type=jnp.float32)


def project_back(grads, weight):
    return jnp.einsum("ste,de->std", grads, weight, preferred_element_type=jnp.float32)


def weight_term(values, grads):
    return jnp.einsum("std,ste->de", values, grads, preferred_element_type=jnp.float32)


def masked_scores(queries, key_heads, allowed):
    raw = jnp.einsum(
        "qhd,khd->hqk", queries, key_heads, preferred_element_type=jnp.float32
    ) * HD ** (-0.5)
    return jnp.where(allowed[None, :, :], raw, NEG)


def norm_back(grad, source, scale, gain):
    scaled = grad * gain.astype(jnp.float32)
    inner = jnp.mean(scaled * source, axis=2, keepdims=True)
    return scale * (scaled - source * scale * scale * inner)


def blocked(step, items):
    total = items[0].shape[0]
    block_size = max((candidate for candidate in range(1, 9) if total % candidate == 0))
    groups = total // block_size
    shaped = tuple((item.reshape((groups, block_size) + item.shape[1:]) for item in items))
    results = lax.map(lambda group: jax.vmap(step)(*group), shaped)
    return jax.tree.map(
        lambda result: result.reshape((groups * block_size,) + result.shape[2:]), results
    )


def per_device_gather(
    inputs,
    cotangent,
    piece_start,
    piece_image,
    valid_mask,
    query_weight,
    key_weight,
    value_weight,
    output_weight,
    attn_gain,
    gate_weight,
    up_weight,
    down_weight,
    mlp_gain,
):
    seqs, local, width = inputs.shape
    length = valid_mask.shape[1]
    band = query_weight.shape[1]
    heads_here = band // HD
    offset = lax.axis_index("fsdp") * local
    positions = offset + jnp.arange(local, dtype=jnp.int32)
    key_places = jnp.arange(length, dtype=jnp.int32)
    cosine, sine = rope_tables(positions, HD)
    local_valid = lax.dynamic_slice_in_dim(valid_mask, offset, local, 1).astype(jnp.float32)

    def sequence_mask(starts, images, valid_row):
        query_image = image_of(positions, starts, images)
        key_image = image_of(key_places, starts, images)
        return allowed_mask(positions, key_places, query_image, key_image, valid_row)

    attn_set = (
        lax.all_gather(query_weight, "fsdp", axis=0, tiled=True),
        lax.all_gather(key_weight, "fsdp", axis=0, tiled=True),
        lax.all_gather(value_weight, "fsdp", axis=0, tiled=True),
        lax.all_gather(output_weight, "fsdp", axis=1, tiled=True),
        lax.all_gather(attn_gain, "fsdp", axis=0, tiled=True),
    )
    residual = inputs.astype(jnp.float32)
    scale_one = lax.rsqrt(jnp.mean(residual * residual, axis=2, keepdims=True) + EPS)
    normed_one = (residual * scale_one * attn_set[4].astype(jnp.float32)).astype(jnp.bfloat16)
    queries = rotate(
        project(normed_one, attn_set[0]).reshape(seqs, local, heads_here, HD), cosine, sine
    ).astype(jnp.bfloat16)
    keys_here = (
        rotate(project(normed_one, attn_set[1]).reshape(seqs, local, heads_here, HD), cosine, sine)
        .astype(jnp.bfloat16)
        .reshape(seqs, local, band)
    )
    values_here = project(normed_one, attn_set[2]).astype(jnp.bfloat16)
    keys_all, values_all = (
        lax.all_gather(keys_here, "fsdp", axis=1, tiled=True),
        lax.all_gather(values_here, "fsdp", axis=1, tiled=True),
    )

    def attend(query_one, key_one, value_one, starts, images, valid_row):
        allowed = sequence_mask(starts, images, valid_row)
        scores = masked_scores(query_one, key_one.reshape(length, heads_here, HD), allowed)
        highest = jnp.max(scores, axis=2, keepdims=True)
        log_total = highest + jnp.log(jnp.sum(jnp.exp(scores - highest), axis=2, keepdims=True))
        probs = jnp.exp(scores - log_total).astype(jnp.bfloat16)
        mixed_one = jnp.einsum(
            "hqk,khd->qhd",
            probs,
            value_one.reshape(length, heads_here, HD),
            preferred_element_type=jnp.float32,
        )
        return (mixed_one.reshape(local, band).astype(jnp.bfloat16), log_total)

    mixed, log_totals = blocked(
        attend, (queries, keys_all, values_all, piece_start, piece_image, valid_mask)
    )
    attn_out = lax.psum(project(mixed, attn_set[3]).astype(jnp.bfloat16), "dp").astype(jnp.float32)
    middle = residual + attn_out
    scale_two = lax.rsqrt(jnp.mean(middle * middle, axis=2, keepdims=True) + EPS)
    mlp_set = (
        lax.all_gather(gate_weight, "fsdp", axis=0, tiled=True),
        lax.all_gather(up_weight, "fsdp", axis=0, tiled=True),
        lax.all_gather(down_weight, "fsdp", axis=1, tiled=True),
        lax.all_gather(mlp_gain, "fsdp", axis=0, tiled=True),
    )
    normed_two = (middle * scale_two * mlp_set[3].astype(jnp.float32)).astype(jnp.bfloat16)
    gate = project(normed_two, mlp_set[0])
    up = project(normed_two, mlp_set[1])
    sigmoid_gate = jax.nn.sigmoid(gate)
    activated = (gate * sigmoid_gate * up).astype(jnp.bfloat16)
    mlp_out = lax.psum(project(activated, mlp_set[2]).astype(jnp.bfloat16), "dp").astype(
        jnp.float32
    )
    output = (middle + mlp_out).astype(jnp.bfloat16)
    row_weight = local_valid[:, :, None]
    totals = lax.psum(
        (
            jnp.sum(middle * middle * row_weight),
            jnp.sum(attn_out * attn_out * row_weight),
            jnp.sum(mlp_out * mlp_out * row_weight),
        ),
        "fsdp",
    )
    count = jnp.sum(valid_mask).astype(jnp.float32) * width
    mlp_back = (
        lax.all_gather(gate_weight, "fsdp", axis=0, tiled=True),
        lax.all_gather(up_weight, "fsdp", axis=0, tiled=True),
        lax.all_gather(down_weight, "fsdp", axis=1, tiled=True),
        lax.all_gather(mlp_gain, "fsdp", axis=0, tiled=True),
    )
    upstream = cotangent.astype(jnp.float32)
    act_grad = project_back(cotangent, mlp_back[2])
    gate_back = (
        act_grad * up * (sigmoid_gate + gate * sigmoid_gate * (1.0 - sigmoid_gate))
    ).astype(jnp.bfloat16)
    up_back = (act_grad * gate * sigmoid_gate).astype(jnp.bfloat16)
    normed_two_back = lax.psum(
        (project_back(gate_back, mlp_back[0]) + project_back(up_back, mlp_back[1])).astype(
            jnp.bfloat16
        ),
        "dp",
    ).astype(jnp.float32)
    middle_back = upstream + norm_back(normed_two_back, middle, scale_two, mlp_back[3])
    mlp_gain_term = jnp.sum(normed_two_back * middle * scale_two, axis=(0, 1))
    mlp_parts = lax.psum_scatter(
        jnp.concatenate(
            [
                weight_term(normed_two, gate_back),
                weight_term(normed_two, up_back),
                weight_term(cotangent, activated),
            ],
            axis=1,
        ).astype(jnp.bfloat16),
        "fsdp",
        scatter_dimension=0,
        tiled=True,
    ).astype(jnp.float32)
    feed = gate_weight.shape[1]
    gate_part = mlp_parts[:, :feed]
    up_part = mlp_parts[:, feed : 2 * feed]
    down_part = mlp_parts[:, 2 * feed :].T
    attn_back = (
        lax.all_gather(query_weight, "fsdp", axis=0, tiled=True),
        lax.all_gather(key_weight, "fsdp", axis=0, tiled=True),
        lax.all_gather(value_weight, "fsdp", axis=0, tiled=True),
        lax.all_gather(output_weight, "fsdp", axis=1, tiled=True),
        lax.all_gather(attn_gain, "fsdp", axis=0, tiled=True),
    )
    middle_low = middle_back.astype(jnp.bfloat16)
    mixed_back = project_back(middle_low, attn_back[3]).astype(jnp.bfloat16)

    def query_grads(query_one, key_heads, value_heads, grad_heads, log_total, allowed):
        scores = masked_scores(query_one, key_heads, allowed)
        weights = jnp.exp(scores - log_total)
        prob_back = jnp.einsum(
            "qhd,khd->hqk", grad_heads, value_heads, preferred_element_type=jnp.float32
        )
        inner = jnp.sum(weights * prob_back, axis=2, keepdims=True)
        score_back = (weights * (prob_back - inner)).astype(jnp.bfloat16)
        query_back = jnp.einsum(
            "hqk,khd->qhd", score_back, key_heads, preferred_element_type=jnp.float32
        ) * HD ** (-0.5)
        return (query_back, weights, score_back, inner)

    def attend_back(query_one, key_one, value_one, grad_one, log_total, starts, images, valid_row):
        allowed = sequence_mask(starts, images, valid_row)
        grad_heads = grad_one.reshape(local, heads_here, HD)
        query_back, weights, score_back, inner = query_grads(
            query_one,
            key_one.reshape(length, heads_here, HD),
            value_one.reshape(length, heads_here, HD),
            grad_heads,
            log_total,
            allowed,
        )
        key_back = jnp.einsum(
            "hqk,qhd->khd", score_back, query_one, preferred_element_type=jnp.float32
        ) * HD ** (-0.5)
        value_back = jnp.einsum(
            "hqk,qhd->khd",
            weights.astype(jnp.bfloat16),
            grad_heads,
            preferred_element_type=jnp.float32,
        )
        return (query_back, key_back.reshape(length, band), value_back.reshape(length, band))

    query_backs, key_parts, value_parts = blocked(
        attend_back,
        (
            queries,
            keys_all,
            values_all,
            mixed_back,
            log_totals,
            piece_start,
            piece_image,
            valid_mask,
        ),
    )
    key_backs, value_backs = (
        lax.psum_scatter(
            key_parts.astype(jnp.bfloat16), "fsdp", scatter_dimension=1, tiled=True
        ).astype(jnp.float32),
        lax.psum_scatter(
            value_parts.astype(jnp.bfloat16), "fsdp", scatter_dimension=1, tiled=True
        ).astype(jnp.float32),
    )
    query_low = unrotate(query_backs, cosine, sine).reshape(seqs, local, band).astype(jnp.bfloat16)
    key_low = (
        unrotate(key_backs.reshape(seqs, local, heads_here, HD), cosine, sine)
        .reshape(seqs, local, band)
        .astype(jnp.bfloat16)
    )
    value_low = value_backs.astype(jnp.bfloat16)
    partial_back = (
        project_back(query_low, attn_back[0])
        + project_back(key_low, attn_back[1])
        + project_back(value_low, attn_back[2])
    )
    normed_one_back = lax.psum(partial_back.astype(jnp.bfloat16), "dp").astype(jnp.float32)
    input_grad = (
        middle_back + norm_back(normed_one_back, residual, scale_one, attn_back[4])
    ).astype(jnp.bfloat16)
    query_part, key_part, value_part, output_term, attn_gain_part, mlp_gain_part = (
        lax.psum_scatter(
            weight_term(normed_one, query_low).astype(jnp.bfloat16),
            "fsdp",
            scatter_dimension=0,
            tiled=True,
        ).astype(jnp.float32),
        lax.psum_scatter(
            weight_term(normed_one, key_low).astype(jnp.bfloat16),
            "fsdp",
            scatter_dimension=0,
            tiled=True,
        ).astype(jnp.float32),
        lax.psum_scatter(
            weight_term(normed_one, value_low).astype(jnp.bfloat16),
            "fsdp",
            scatter_dimension=0,
            tiled=True,
        ).astype(jnp.float32),
        lax.psum_scatter(
            weight_term(middle_low, mixed).astype(jnp.bfloat16),
            "fsdp",
            scatter_dimension=0,
            tiled=True,
        ).astype(jnp.float32),
        lax.psum_scatter(
            jnp.sum(normed_one_back * residual * scale_one, axis=(0, 1)).astype(jnp.bfloat16),
            "fsdp",
            scatter_dimension=0,
            tiled=True,
        ).astype(jnp.float32),
        lax.psum_scatter(
            mlp_gain_term.astype(jnp.bfloat16), "fsdp", scatter_dimension=0, tiled=True
        ).astype(jnp.float32),
    )
    output_part = output_term.T
    return (
        output,
        input_grad,
        query_part,
        key_part,
        value_part,
        output_part,
        attn_gain_part,
        gate_part,
        up_part,
        down_part,
        mlp_gain_part,
        jnp.sqrt(totals[0] / count),
        jnp.sqrt(totals[1] / count),
        jnp.sqrt(totals[2] / count),
    )


VMEM_MOST = 66_000_000
MESH = pl.DeviceIdType.MESH
BF16 = jnp.bfloat16
F32 = jnp.float32
PAIR = 2 * HD
TILE = 256
STRIP = 64
HOP = 2

NT = (((1,), (1,)), ((), ()))
TN = (((0,), (0,)), ((), ()))


def mm(a, b):
    return jnp.dot(a, b, preferred_element_type=F32)


def mm_nt(a, b):
    return lax.dot_general(a, b, NT, preferred_element_type=F32)


def mm_tn(a, b):
    return lax.dot_general(a, b, TN, preferred_element_type=F32)


def half_swap(values):
    lane = lax.broadcasted_iota(jnp.int32, values.shape, 1) % HD
    ahead = pltpu.roll(values, PAIR - HD // 2, 1)
    behind = pltpu.roll(values, HD // 2, 1)
    return jnp.where(lane < HD // 2, ahead, behind)


def head_lanes(values, head):
    lane = lax.broadcasted_iota(jnp.int32, values.shape, 1) // HD
    return jnp.where(lane == head, values, jnp.zeros_like(values))


def diagonal_bias(is_piece):
    key = lax.broadcasted_iota(jnp.int32, (TILE, TILE), 0)
    query = lax.broadcasted_iota(jnp.int32, (TILE, TILE), 1)
    return jnp.where((key <= query) | is_piece, 0.0, NEG).astype(F32)


def attend_kernel(
    image_ref,
    q_in,
    k_in,
    v_in,
    cos_ref,
    sin_ref,
    bias_ref,
    q_ref,
    k_ref,
    v_ref,
    mixed_ref,
    lse_ref,
    top,
    total,
    acc,
    outs,
):
    length = q_in.shape[0]
    tiles = length // TILE
    cosine, sine = cos_ref[...], sin_ref[...]
    raw = q_in[...]
    q_ref[...] = ((raw * cosine + half_swap(raw) * sine) * HD ** (-0.5)).astype(BF16)
    raw = k_in[...]
    k_ref[...] = (raw * cosine + half_swap(raw) * sine).astype(BF16)
    v_ref[...] = v_in[...].astype(BF16)
    lse_ref[...] = jnp.zeros_like(lse_ref)
    for tile in range(tiles):
        here = slice(tile * TILE, (tile + 1) * TILE)
        upto = (tile + 1) * TILE
        corner = diagonal_bias(image_ref[tile] >= 0)
        for head in range(2):
            query = head_lanes(q_ref[here, :], head)
            scores = mm_nt(k_ref[:upto, :], query) + bias_ref[:upto, :]
            diag = scores[upto - TILE :, :] + corner
            highest = jnp.max(diag, axis=0, keepdims=True)
            if tile:
                before = scores[: upto - TILE, :]
                highest = jnp.maximum(highest, jnp.max(before, axis=0, keepdims=True))
                weight_low = jnp.exp(before - highest)
                weight_diag = jnp.exp(diag - highest)
                summed = jnp.sum(weight_low, axis=0, keepdims=True) + jnp.sum(
                    weight_diag, axis=0, keepdims=True
                )
                mixed = mm_tn(v_ref[: upto - TILE, :], weight_low.astype(BF16)) + mm_tn(
                    v_ref[upto - TILE : upto, :], weight_diag.astype(BF16)
                )
            else:
                weight_diag = jnp.exp(diag - highest)
                summed = jnp.sum(weight_diag, axis=0, keepdims=True)
                mixed = mm_tn(v_ref[:upto, :], weight_diag.astype(BF16))
            top[...] = highest
            total[...] = summed
            acc[...] = mixed
            for other in range(tile + 1, tiles):

                @pl.when((image_ref[tile] >= 0) & (image_ref[tile] == image_ref[other]))
                def _(other=other, query=query):
                    there = slice(other * TILE, (other + 1) * TILE)
                    extra = mm_nt(k_ref[there, :], query) + bias_ref[there, :]
                    newest = jnp.maximum(top[...], jnp.max(extra, axis=0, keepdims=True))
                    shrink = jnp.exp(top[...] - newest)
                    weight = jnp.exp(extra - newest)
                    total[...] = total[...] * shrink + jnp.sum(weight, axis=0, keepdims=True)
                    acc[...] = acc[...] * shrink + mm_tn(v_ref[there, :], weight.astype(BF16))
                    top[...] = newest

            rows = slice(head * HD, (head + 1) * HD)
            outs[rows, :] = acc[rows, :] / total[...]
            lse_ref[0, head : head + 1, here] = top[...] + jnp.log(total[...])
        mixed_ref[here, :] = outs[...].T.astype(BF16)


def attend(qkv, cosine, sine, bias, image):
    length, wide = qkv.shape
    band = wide // 3
    pairs = band // PAIR
    column = lambda shift: pl.BlockSpec((length, PAIR), lambda g, img: (0, g + shift))
    fixed = lambda cols: pl.BlockSpec((length, cols), lambda g, img: (0, 0))
    low = jax.ShapeDtypeStruct((length, band), BF16)
    return pl.pallas_call(
        attend_kernel,
        grid_spec=pltpu.PrefetchScalarGridSpec(
            num_scalar_prefetch=1,
            grid=(pairs,),
            in_specs=[
                column(0),
                column(pairs),
                column(2 * pairs),
                fixed(PAIR),
                fixed(PAIR),
                fixed(1),
            ],
            out_specs=[column(0)] * 4 + [pl.BlockSpec((1, 8, length), lambda g, img: (g, 0, 0))],
            scratch_shapes=[
                pltpu.VMEM((1, TILE), F32),
                pltpu.VMEM((1, TILE), F32),
                pltpu.VMEM((PAIR, TILE), F32),
                pltpu.VMEM((PAIR, TILE), F32),
            ],
        ),
        out_shape=[low] * 4 + [jax.ShapeDtypeStruct((pairs, 8, length), F32)],
        compiler_params=pltpu.CompilerParams(vmem_limit_bytes=VMEM_MOST),
        cost_estimate=pl.CostEstimate(
            flops=12_000_000_000, bytes_accessed=12_000_000, transcendentals=6_000_000
        ),
        name="attend",
    )(image, qkv, qkv, qkv, cosine, sine, bias)


def attend_back_kernel(
    image_ref,
    q_ref,
    k_ref,
    v_ref,
    g_ref,
    mixed_ref,
    lse_ref,
    cos_ref,
    sin_ref,
    bias_ref,
    dq_ref,
    dk_ref,
    dv_ref,
    dk_acc,
    dv_acc,
    dq_acc,
):
    length = q_ref.shape[0]
    tiles = length // TILE
    dk_acc[...] = jnp.zeros_like(dk_acc)
    dv_acc[...] = jnp.zeros_like(dv_acc)
    pick_row = lax.broadcasted_iota(jnp.int32, (8, PAIR), 0)
    pick_lane = lax.broadcasted_iota(jnp.int32, (8, PAIR), 1) // HD
    picker = (pick_row == pick_lane).astype(F32)
    for tile in range(tiles):
        here = slice(tile * TILE, (tile + 1) * TILE)
        corner = diagonal_bias(image_ref[tile] >= 0)
        product = mixed_ref[here, :].astype(F32) * g_ref[here, :].astype(F32)
        inners = lax.dot_general(
            picker, product, NT, precision=lax.Precision.HIGHEST, preferred_element_type=F32
        )
        for head in range(2):
            query = head_lanes(q_ref[here, :], head)
            grad = head_lanes(g_ref[here, :], head)
            inner = inners[head : head + 1, :]
            lse = lse_ref[0, head : head + 1, here]
            rows = slice(head * HD, (head + 1) * HD)

            def block(there, extra, first):
                scores = mm_nt(k_ref[there, :], query) + bias_ref[there, :]
                if extra is not None:
                    scores = scores + extra
                weight = jnp.exp(scores - lse)
                back = mm_nt(v_ref[there, :], grad)
                score_back = (weight * (back - inner)).astype(BF16)
                dv_acc[there, :] += mm(weight.astype(BF16), grad)
                dk_acc[there, :] += mm(score_back, query)
                part = mm_tn(k_ref[there, :], score_back)
                if first:
                    dq_acc[rows, :] = part[rows, :]
                else:
                    dq_acc[rows, :] += part[rows, :]

            block(here, corner, True)
            for other in range(tile):
                block(slice(other * TILE, (other + 1) * TILE), None, False)
            for other in range(tile + 1, tiles):

                @pl.when((image_ref[tile] >= 0) & (image_ref[tile] == image_ref[other]))
                def _(other=other):
                    block(slice(other * TILE, (other + 1) * TILE), None, False)

        turned = dq_acc[...].T * HD ** (-0.5)
        dq_ref[here, :] = (
            turned * cos_ref[here, :] - half_swap(turned) * sin_ref[here, :]
        ).astype(BF16)
    turned = dk_acc[...]
    dk_ref[...] = (turned * cos_ref[...] - half_swap(turned) * sin_ref[...]).astype(BF16)
    dv_ref[...] = dv_acc[...].astype(BF16)


def attend_back(queries, keys, values, grads, mixed, lse, cosine, sine, bias, image):
    length, band = queries.shape
    pairs = band // PAIR
    column = pl.BlockSpec((length, PAIR), lambda g, img: (0, g))
    fixed = lambda cols: pl.BlockSpec((length, cols), lambda g, img: (0, 0))
    low = jax.ShapeDtypeStruct((length, band), BF16)
    return pl.pallas_call(
        attend_back_kernel,
        grid_spec=pltpu.PrefetchScalarGridSpec(
            num_scalar_prefetch=1,
            grid=(pairs,),
            in_specs=[column] * 5
            + [
                pl.BlockSpec((1, 8, length), lambda g, img: (g, 0, 0)),
                fixed(PAIR),
                fixed(PAIR),
                fixed(1),
            ],
            out_specs=[column] * 3,
            scratch_shapes=[
                pltpu.VMEM((length, PAIR), F32),
                pltpu.VMEM((length, PAIR), F32),
                pltpu.VMEM((PAIR, TILE), F32),
            ],
        ),
        out_shape=[low] * 3,
        compiler_params=pltpu.CompilerParams(vmem_limit_bytes=VMEM_MOST),
        cost_estimate=pl.CostEstimate(
            flops=30_000_000_000, bytes_accessed=12_000_000, transcendentals=6_000_000
        ),
        name="attend_back",
    )(image, queries, keys, values, grads, mixed, lse, cosine, sine, bias)


def line_sum(n, own, flows, make, finish):
    from_low, from_high, to_high, to_low, sems = flows
    send_high, send_low, got_low, got_high = (sems.at[k] for k in range(4))
    rank = lax.axis_index("dp")
    strips = own.shape[0] // STRIP
    has_low, has_high = rank > 0, rank < n - 1
    higher, lower = lax.rem(rank + 1, n), lax.rem(rank + n - 1, n)

    barrier = pltpu.get_barrier_semaphore()

    @pl.when(has_low)
    def _():
        pl.semaphore_signal(barrier, inc=1, device_id={"dp": lower}, device_id_type=MESH)

    @pl.when(has_high)
    def _():
        pl.semaphore_signal(barrier, inc=1, device_id={"dp": higher}, device_id_type=MESH)

    pl.semaphore_wait(barrier, has_low.astype(jnp.int32) + has_high.astype(jnp.int32))

    def rows_of(strip):
        return pl.ds(pl.multiple_of(strip * STRIP, STRIP), STRIP)

    def up(strip):
        rows = rows_of(strip)
        return pltpu.make_async_remote_copy(
            src_ref=to_high.at[rows],
            dst_ref=from_low.at[rows],
            send_sem=send_high.at[strip],
            recv_sem=got_low.at[strip],
            device_id={"dp": higher},
            device_id_type=MESH,
        )

    def down(strip):
        rows = rows_of(strip)
        return pltpu.make_async_remote_copy(
            src_ref=to_low.at[rows],
            dst_ref=from_high.at[rows],
            send_sem=send_low.at[strip],
            recv_sem=got_high.at[strip],
            device_id={"dp": lower},
            device_id_type=MESH,
        )

    @pl.when(jnp.logical_not(has_low))
    def _():
        from_low[...] = jnp.zeros_like(from_low)

    @pl.when(jnp.logical_not(has_high))
    def _():
        from_high[...] = jnp.zeros_like(from_high)

    late = jnp.maximum(rank, n - 1 - rank)

    def step(s, carry):
        @pl.when(s < strips)
        def _():
            make(s, rows_of(s))

        a = s - rank * HOP

        @pl.when((a >= 0) & (a < strips))
        def _():
            @pl.when(has_low)
            def _():
                up(a).wait_recv()

            @pl.when(has_high)
            def _():
                rows = rows_of(a)
                to_high[rows, :] = (
                    own[rows, :].astype(F32) + from_low[rows, :].astype(F32)
                ).astype(BF16)
                up(a).start()

        b = s - (n - 1 - rank) * HOP

        @pl.when((b >= 0) & (b < strips))
        def _():
            @pl.when(has_high)
            def _():
                down(b).wait_recv()

            @pl.when(has_low)
            def _():
                rows = rows_of(b)
                to_low[rows, :] = (
                    own[rows, :].astype(F32) + from_high[rows, :].astype(F32)
                ).astype(BF16)
                down(b).start()

        c = s - late * HOP

        @pl.when((c >= 0) & (c < strips))
        def _():
            rows = rows_of(c)
            finish(
                c,
                rows,
                own[rows, :].astype(F32)
                + from_low[rows, :].astype(F32)
                + from_high[rows, :].astype(F32),
            )

        return carry

    lax.fori_loop(0, strips + (n - 1) * HOP, step, 0)

    def drain(s, carry):
        @pl.when(has_high)
        def _():
            up(s).wait_send()

        @pl.when(has_low)
        def _():
            down(s).wait_send()

        return carry

    lax.fori_loop(0, strips, drain, 0)


def flow_scratch(length, width):
    whole = pltpu.VMEM((length, width), BF16)
    return [whole] * 4 + [pltpu.SemaphoreType.DMA((4, length // STRIP))]


VM = pl.BlockSpec(memory_space=pltpu.VMEM)
ANY = pl.BlockSpec(memory_space=pl.ANY)


def row_mean(values):
    return jnp.mean(values, axis=1, keepdims=True)


def col_sum(values):
    return jnp.sum(values, axis=0, keepdims=True)


def line_call(kernel, n, name, collective_id, args, out_shape, scratch, specs, flops=10**9):
    return pl.pallas_call(
        functools.partial(kernel, n),
        in_specs=specs,
        out_specs=[VM] * len(out_shape),
        out_shape=out_shape,
        scratch_shapes=scratch,
        compiler_params=pltpu.CompilerParams(
            collective_id=collective_id, has_side_effects=True, vmem_limit_bytes=VMEM_MOST
        ),
        cost_estimate=pl.CostEstimate(
            flops=flops, bytes_accessed=200_000_000, transcendentals=0
        ),
        name=name,
    )(*args)


def middle_kernel(
    n,
    mixed_ref,
    out_weight,
    source,
    gain,
    valid,
    middle_ref,
    normed_ref,
    stats_ref,
    own,
    weight,
    weight_sem,
    *flows,
):
    band = weight.shape[1]
    load = pltpu.make_async_copy(
        out_weight.at[:, pl.ds(out_weight.shape[1] - band, band)], weight, weight_sem
    )
    load.start()
    stats_ref[...] = jnp.zeros_like(stats_ref)
    load.wait()

    def make(strip, rows):
        own[rows, :] = mm_nt(mixed_ref[rows, :], weight[...]).astype(BF16)

    def finish(strip, rows, total):
        middle = source[rows, :].astype(F32) + total
        middle_ref[rows, :] = middle
        square = middle * middle
        scale = lax.rsqrt(row_mean(square) + EPS)
        normed_ref[rows, :] = (middle * scale * gain[...]).astype(BF16)
        stats_ref[0:1, :] += col_sum(square * valid[rows, :])
        stats_ref[1:2, :] += col_sum(total * total * valid[rows, :])

    line_sum(n, own, flows, make, finish)


def middle_sum(n, mixed, gathered, source, gain, valid):
    length, width = source.shape
    band = mixed.shape[1]
    return line_call(
        middle_kernel,
        n,
        "middle_sum",
        1,
        (mixed, gathered, source, gain, valid),
        [
            jax.ShapeDtypeStruct((length, width), F32),
            jax.ShapeDtypeStruct((length, width), BF16),
            jax.ShapeDtypeStruct((8, width), F32),
        ],
        [
            pltpu.VMEM((length, width), BF16),
            pltpu.VMEM((width, band), BF16),
            pltpu.SemaphoreType.DMA,
        ]
        + flow_scratch(length, width),
        [VM, ANY, VM, VM, VM],
    )


def middle_back_kernel(n, own, cotangent, middle_ref, gain, back_ref, low_ref, gain_ref, *flows):
    gain_ref[...] = jnp.zeros_like(gain_ref)

    def make(strip, rows):
        pass

    def finish(strip, rows, total):
        middle = middle_ref[rows, :]
        scale = lax.rsqrt(row_mean(middle * middle) + EPS)
        scaled = total * gain[...]
        inner = row_mean(scaled * middle)
        back = cotangent[rows, :].astype(F32) + scale * (scaled - middle * (scale * scale * inner))
        back_ref[rows, :] = back
        low_ref[rows, :] = back.astype(BF16)
        gain_ref[0:1, :] += col_sum(total * middle * scale)

    line_sum(n, own, flows, make, finish)


def middle_back_sum(n, part, cotangent, middle, gain):
    length, width = part.shape
    return line_call(
        middle_back_kernel,
        n,
        "middle_back_sum",
        2,
        (part, cotangent, middle, gain),
        [
            jax.ShapeDtypeStruct((length, width), F32),
            jax.ShapeDtypeStruct((length, width), BF16),
            jax.ShapeDtypeStruct((8, width), F32),
        ],
        flow_scratch(length, width),
        [VM] * 4,
    )


def output_kernel(n, own, middle_ref, valid, out_ref, stats_ref, *flows):
    stats_ref[...] = jnp.zeros_like(stats_ref)

    def make(strip, rows):
        pass

    def finish(strip, rows, total):
        out_ref[rows, :] = (middle_ref[rows, :] + total).astype(BF16)
        stats_ref[0:1, :] += col_sum(total * total * valid[rows, :])

    line_sum(n, own, flows, make, finish)


def output_sum(n, part, middle, valid):
    length, width = part.shape
    return line_call(
        output_kernel,
        n,
        "output_sum",
        3,
        (part, middle, valid),
        [
            jax.ShapeDtypeStruct((length, width), BF16),
            jax.ShapeDtypeStruct((8, width), F32),
        ],
        flow_scratch(length, width),
        [VM] * 3,
    )


def input_kernel(n, own, source_ref, back_ref, gain, grad_ref, gain_ref, *flows):
    gain_ref[...] = jnp.zeros_like(gain_ref)

    def make(strip, rows):
        pass

    def finish(strip, rows, total):
        source = source_ref[rows, :].astype(F32)
        scale = lax.rsqrt(row_mean(source * source) + EPS)
        scaled = total * gain[...]
        inner = row_mean(scaled * source)
        grad_ref[rows, :] = (
            back_ref[rows, :] + scale * (scaled - source * (scale * scale * inner))
        ).astype(BF16)
        gain_ref[0:1, :] += col_sum(total * source * scale)

    line_sum(n, own, flows, make, finish)


def input_sum(n, part, source, back, gain):
    length, width = part.shape
    return line_call(
        input_kernel,
        n,
        "input_sum",
        4,
        (part, source, back, gain),
        [
            jax.ShapeDtypeStruct((length, width), BF16),
            jax.ShapeDtypeStruct((8, width), F32),
        ],
        flow_scratch(length, width),
        [VM] * 4,
    )


def per_device(
    mesh_sizes,
    inputs,
    cotangent,
    piece_start,
    piece_image,
    valid_mask,
    query_weight,
    key_weight,
    value_weight,
    output_weight,
    attn_gain,
    gate_weight,
    up_weight,
    down_weight,
    mlp_gain,
):
    spread, line = mesh_sizes
    seqs, local, width = inputs.shape
    length = valid_mask.shape[1]
    band = query_weight.shape[1]
    feed = gate_weight.shape[1]
    mine = lax.axis_index("fsdp")

    def swap(values):
        return lax.all_to_all(values, "fsdp", split_axis=0, concat_axis=0, tiled=True)

    attn_w = lax.all_gather(
        jnp.concatenate([query_weight, key_weight, value_weight, output_weight.T], axis=1),
        "fsdp",
        axis=0,
        tiled=True,
    )
    gains = lax.all_gather(jnp.stack([attn_gain, mlp_gain]), "fsdp", axis=1, tiled=True).astype(F32)
    attn_g, mlp_g = gains[0:1], gains[1:2]
    mlp_w = lax.all_gather(
        jnp.concatenate([gate_weight, up_weight, down_weight.T], axis=1),
        "fsdp",
        axis=0,
        tiled=True,
    )
    source = swap(inputs).reshape(length, width)
    upstream = swap(cotangent).reshape(length, width)

    places = jnp.arange(length, dtype=jnp.int32)
    cosine, sine = rope_tables(places, HD)
    signs = jnp.where(jnp.arange(HD) < HD // 2, -1.0, 1.0).astype(F32)
    cosine = jnp.concatenate([cosine, cosine], axis=1)
    sine = jnp.concatenate([sine * signs, sine * signs], axis=1)
    valid_row = lax.dynamic_index_in_dim(valid_mask, mine, 0, keepdims=False)
    valid = valid_row.astype(F32)[:, None]
    bias = jnp.where(valid_row > 0, 0.0, NEG).astype(F32)[:, None]
    starts = lax.dynamic_index_in_dim(piece_start, mine, 0, keepdims=False)
    images = lax.dynamic_index_in_dim(piece_image, mine, 0, keepdims=False)
    image = image_of(jnp.arange(length // TILE, dtype=jnp.int32) * TILE, starts, images).astype(
        jnp.int32
    )

    residual = source.astype(F32)
    scale_one = lax.rsqrt(jnp.mean(residual * residual, axis=1, keepdims=True) + EPS)
    normed_one = (residual * scale_one * attn_g).astype(BF16)
    qkv = mm(normed_one, attn_w[:, : 3 * band])
    queries, keys, values, mixed, lse = attend(qkv, cosine, sine, bias, image)
    middle, normed_two, stats = middle_sum(line, mixed, attn_w, source, mlp_g, valid)

    gate = mm(normed_two, mlp_w[:, :feed])
    up = mm(normed_two, mlp_w[:, feed : 2 * feed])
    sig = jax.nn.sigmoid(gate)
    activated = (gate * sig * up).astype(BF16)
    act_grad = mm(upstream, mlp_w[:, 2 * feed :])
    gate_back = (act_grad * up * (sig + gate * sig * (1.0 - sig))).astype(BF16)
    up_back = (act_grad * gate * sig).astype(BF16)
    back_part = (
        mm_nt(gate_back, mlp_w[:, :feed]) + mm_nt(up_back, mlp_w[:, feed : 2 * feed])
    ).astype(BF16)
    middle_back, middle_low, mlp_gain_sum = middle_back_sum(
        line, back_part, upstream, middle, mlp_g
    )
    mlp_grads = lax.psum_scatter(
        jnp.concatenate(
            [
                mm_tn(normed_two, gate_back).astype(BF16),
                mm_tn(normed_two, up_back).astype(BF16),
                mm_tn(upstream, activated).astype(BF16),
            ],
            axis=1,
        ),
        "fsdp",
        scatter_dimension=0,
        tiled=True,
    ).astype(F32)
    mixed_back = mm(middle_low, attn_w[:, 3 * band :]).astype(BF16)
    dq, dk, dv = attend_back(
        queries, keys, values, mixed_back, mixed, lse, cosine, sine, bias, image
    )
    mlp_part = mm_nt(activated, mlp_w[:, 2 * feed :]).astype(BF16)
    result, mlp_stats = output_sum(line, mlp_part, middle, valid)
    output = swap(result.reshape(seqs, local, width))
    front_part = mm_nt(jnp.concatenate([dq, dk, dv], axis=1), attn_w[:, : 3 * band]).astype(BF16)
    source_grad, attn_gain_sum = input_sum(line, front_part, source, middle_back, attn_g)
    input_grad = swap(source_grad.reshape(seqs, local, width))
    attn_grads = lax.psum_scatter(
        jnp.concatenate(
            [
                mm_tn(normed_one, dq).astype(BF16),
                mm_tn(normed_one, dk).astype(BF16),
                mm_tn(normed_one, dv).astype(BF16),
                mm_tn(middle_low, mixed).astype(BF16),
            ],
            axis=1,
        ),
        "fsdp",
        scatter_dimension=0,
        tiled=True,
    ).astype(F32)
    sums = jnp.stack([jnp.sum(stats[0]), jnp.sum(stats[1]), jnp.sum(mlp_stats[0])])
    small = lax.psum(
        jnp.concatenate([attn_gain_sum[0], mlp_gain_sum[0], sums]), "fsdp"
    )
    share = width // spread
    attn_gain_part = lax.dynamic_slice_in_dim(small, mine * share, share)
    mlp_gain_part = lax.dynamic_slice_in_dim(small, width + mine * share, share)
    count = jnp.sum(valid_mask).astype(F32) * width
    roots = jnp.sqrt(small[2 * width :] / count)
    return (
        output,
        input_grad,
        attn_grads[:, :band],
        attn_grads[:, band : 2 * band],
        attn_grads[:, 2 * band : 3 * band],
        attn_grads[:, 3 * band :].T,
        attn_gain_part,
        mlp_grads[:, :feed],
        mlp_grads[:, feed : 2 * feed],
        mlp_grads[:, 2 * feed :].T,
        mlp_gain_part,
        roots[0],
        roots[1],
        roots[2],
    )


def solution(mesh):
    placed = (
        P(None, "fsdp", None),
        P(None, "fsdp", None),
        P(),
        P(),
        P(),
        P("fsdp", "dp"),
        P("fsdp", "dp"),
        P("fsdp", "dp"),
        P("dp", "fsdp"),
        P("fsdp"),
        P("fsdp", "dp"),
        P("fsdp", "dp"),
        P("dp", "fsdp"),
        P("fsdp"),
    )
    spread, line = mesh.shape["fsdp"], mesh.shape["dp"]

    def whole(*arrays):
        seqs, length, _ = arrays[0].shape
        own_sequence = seqs == spread and length % (2 * TILE) == 0 and line > 1
        each = functools.partial(per_device, (spread, line)) if own_sequence else per_device_gather
        return jax.shard_map(
            each,
            mesh=mesh,
            in_specs=placed,
            out_specs=(
                P(None, "fsdp", None),
                P(None, "fsdp", None),
                P("fsdp", "dp"),
                P("fsdp", "dp"),
                P("fsdp", "dp"),
                P("dp", "fsdp"),
                P("fsdp"),
                P("fsdp", "dp"),
                P("fsdp", "dp"),
                P("dp", "fsdp"),
                P("fsdp"),
                P(),
                P(),
                P(),
            ),
            check_vma=False,
        )(*arrays)

    return whole
```

```python
import functools

import jax
import jax.numpy as jnp
from jax import lax
from jax.experimental import pallas as pl
from jax.experimental.pallas import tpu as pltpu
from jax.sharding import PartitionSpec as P


HD = 64
PIECE = 256


EPS = 1e-05
THETA = 130000.0
NEG = -1e30


def rope_tables(positions, head_size):
    half = head_size // 2
    rates = THETA ** (-(jnp.arange(half, dtype=jnp.float32) * 2.0 / head_size))
    angle = positions.astype(jnp.float32)[:, None] * rates[None, :]
    cosine = jnp.concatenate([jnp.cos(angle), jnp.cos(angle)], axis=-1)
    sine = jnp.concatenate([jnp.sin(angle), jnp.sin(angle)], axis=-1)
    return (cosine, sine)


def rotate(values, cosine, sine):
    half = values.shape[-1] // 2
    turned = jnp.concatenate([-values[..., half:], values[..., :half]], axis=-1)
    return values * cosine[:, None, :] + turned * sine[:, None, :]


def unrotate(grads, cosine, sine):
    half = grads.shape[-1] // 2
    scaled = grads * sine[:, None, :]
    turned = jnp.concatenate([scaled[..., half:], -scaled[..., :half]], axis=-1)
    return grads * cosine[:, None, :] + turned


def image_of(positions, starts, images):
    inside = (positions[:, None] >= starts[None, :]) & (
        positions[:, None] < starts[None, :] + PIECE
    )
    return jnp.sum(jnp.where(inside, images[None, :] + 1, 0), axis=1) - 1


def allowed_mask(query_pos, key_pos, query_image, key_image, key_valid):
    causal = key_pos[None, :] <= query_pos[:, None]
    same = (query_image[:, None] >= 0) & (query_image[:, None] == key_image[None, :])
    return (causal | same) & (key_valid[None, :] > 0)


def project(values, weight):
    return jnp.einsum("std,de->ste", values, weight, preferred_element_type=jnp.float32)


def project_back(grads, weight):
    return jnp.einsum("ste,de->std", grads, weight, preferred_element_type=jnp.float32)


def weight_term(values, grads):
    return jnp.einsum("std,ste->de", values, grads, preferred_element_type=jnp.float32)


def masked_scores(queries, key_heads, allowed):
    raw = jnp.einsum(
        "qhd,khd->hqk", queries, key_heads, preferred_element_type=jnp.float32
    ) * HD ** (-0.5)
    return jnp.where(allowed[None, :, :], raw, NEG)


def norm_back(grad, source, scale, gain):
    scaled = grad * gain.astype(jnp.float32)
    inner = jnp.mean(scaled * source, axis=2, keepdims=True)
    return scale * (scaled - source * scale * scale * inner)


def blocked(step, items):
    total = items[0].shape[0]
    block_size = max((candidate for candidate in range(1, 9) if total % candidate == 0))
    groups = total // block_size
    shaped = tuple((item.reshape((groups, block_size) + item.shape[1:]) for item in items))
    results = lax.map(lambda group: jax.vmap(step)(*group), shaped)
    return jax.tree.map(
        lambda result: result.reshape((groups * block_size,) + result.shape[2:]), results
    )


def per_device_gather(
    inputs,
    cotangent,
    piece_start,
    piece_image,
    valid_mask,
    query_weight,
    key_weight,
    value_weight,
    output_weight,
    attn_gain,
    gate_weight,
    up_weight,
    down_weight,
    mlp_gain,
):
    seqs, local, width = inputs.shape
    length = valid_mask.shape[1]
    band = query_weight.shape[1]
    heads_here = band // HD
    offset = lax.axis_index("fsdp") * local
    positions = offset + jnp.arange(local, dtype=jnp.int32)
    key_places = jnp.arange(length, dtype=jnp.int32)
    cosine, sine = rope_tables(positions, HD)
    local_valid = lax.dynamic_slice_in_dim(valid_mask, offset, local, 1).astype(jnp.float32)

    def sequence_mask(starts, images, valid_row):
        query_image = image_of(positions, starts, images)
        key_image = image_of(key_places, starts, images)
        return allowed_mask(positions, key_places, query_image, key_image, valid_row)

    attn_set = (
        lax.all_gather(query_weight, "fsdp", axis=0, tiled=True),
        lax.all_gather(key_weight, "fsdp", axis=0, tiled=True),
        lax.all_gather(value_weight, "fsdp", axis=0, tiled=True),
        lax.all_gather(output_weight, "fsdp", axis=1, tiled=True),
        lax.all_gather(attn_gain, "fsdp", axis=0, tiled=True),
    )
    residual = inputs.astype(jnp.float32)
    scale_one = lax.rsqrt(jnp.mean(residual * residual, axis=2, keepdims=True) + EPS)
    normed_one = (residual * scale_one * attn_set[4].astype(jnp.float32)).astype(jnp.bfloat16)
    queries = rotate(
        project(normed_one, attn_set[0]).reshape(seqs, local, heads_here, HD), cosine, sine
    ).astype(jnp.bfloat16)
    keys_here = (
        rotate(project(normed_one, attn_set[1]).reshape(seqs, local, heads_here, HD), cosine, sine)
        .astype(jnp.bfloat16)
        .reshape(seqs, local, band)
    )
    values_here = project(normed_one, attn_set[2]).astype(jnp.bfloat16)
    keys_all, values_all = (
        lax.all_gather(keys_here, "fsdp", axis=1, tiled=True),
        lax.all_gather(values_here, "fsdp", axis=1, tiled=True),
    )

    def attend(query_one, key_one, value_one, starts, images, valid_row):
        allowed = sequence_mask(starts, images, valid_row)
        scores = masked_scores(query_one, key_one.reshape(length, heads_here, HD), allowed)
        highest = jnp.max(scores, axis=2, keepdims=True)
        log_total = highest + jnp.log(jnp.sum(jnp.exp(scores - highest), axis=2, keepdims=True))
        probs = jnp.exp(scores - log_total).astype(jnp.bfloat16)
        mixed_one = jnp.einsum(
            "hqk,khd->qhd",
            probs,
            value_one.reshape(length, heads_here, HD),
            preferred_element_type=jnp.float32,
        )
        return (mixed_one.reshape(local, band).astype(jnp.bfloat16), log_total)

    mixed, log_totals = blocked(
        attend, (queries, keys_all, values_all, piece_start, piece_image, valid_mask)
    )
    attn_out = lax.psum(project(mixed, attn_set[3]).astype(jnp.bfloat16), "dp").astype(jnp.float32)
    middle = residual + attn_out
    scale_two = lax.rsqrt(jnp.mean(middle * middle, axis=2, keepdims=True) + EPS)
    mlp_set = (
        lax.all_gather(gate_weight, "fsdp", axis=0, tiled=True),
        lax.all_gather(up_weight, "fsdp", axis=0, tiled=True),
        lax.all_gather(down_weight, "fsdp", axis=1, tiled=True),
        lax.all_gather(mlp_gain, "fsdp", axis=0, tiled=True),
    )
    normed_two = (middle * scale_two * mlp_set[3].astype(jnp.float32)).astype(jnp.bfloat16)
    gate = project(normed_two, mlp_set[0])
    up = project(normed_two, mlp_set[1])
    sigmoid_gate = jax.nn.sigmoid(gate)
    activated = (gate * sigmoid_gate * up).astype(jnp.bfloat16)
    mlp_out = lax.psum(project(activated, mlp_set[2]).astype(jnp.bfloat16), "dp").astype(
        jnp.float32
    )
    output = (middle + mlp_out).astype(jnp.bfloat16)
    row_weight = local_valid[:, :, None]
    totals = lax.psum(
        (
            jnp.sum(middle * middle * row_weight),
            jnp.sum(attn_out * attn_out * row_weight),
            jnp.sum(mlp_out * mlp_out * row_weight),
        ),
        "fsdp",
    )
    count = jnp.sum(valid_mask).astype(jnp.float32) * width
    mlp_back = (
        lax.all_gather(gate_weight, "fsdp", axis=0, tiled=True),
        lax.all_gather(up_weight, "fsdp", axis=0, tiled=True),
        lax.all_gather(down_weight, "fsdp", axis=1, tiled=True),
        lax.all_gather(mlp_gain, "fsdp", axis=0, tiled=True),
    )
    upstream = cotangent.astype(jnp.float32)
    act_grad = project_back(cotangent, mlp_back[2])
    gate_back = (
        act_grad * up * (sigmoid_gate + gate * sigmoid_gate * (1.0 - sigmoid_gate))
    ).astype(jnp.bfloat16)
    up_back = (act_grad * gate * sigmoid_gate).astype(jnp.bfloat16)
    normed_two_back = lax.psum(
        (project_back(gate_back, mlp_back[0]) + project_back(up_back, mlp_back[1])).astype(
            jnp.bfloat16
        ),
        "dp",
    ).astype(jnp.float32)
    middle_back = upstream + norm_back(normed_two_back, middle, scale_two, mlp_back[3])
    mlp_gain_term = jnp.sum(normed_two_back * middle * scale_two, axis=(0, 1))
    mlp_parts = lax.psum_scatter(
        jnp.concatenate(
            [
                weight_term(normed_two, gate_back),
                weight_term(normed_two, up_back),
                weight_term(cotangent, activated),
            ],
            axis=1,
        ).astype(jnp.bfloat16),
        "fsdp",
        scatter_dimension=0,
        tiled=True,
    ).astype(jnp.float32)
    feed = gate_weight.shape[1]
    gate_part = mlp_parts[:, :feed]
    up_part = mlp_parts[:, feed : 2 * feed]
    down_part = mlp_parts[:, 2 * feed :].T
    attn_back = (
        lax.all_gather(query_weight, "fsdp", axis=0, tiled=True),
        lax.all_gather(key_weight, "fsdp", axis=0, tiled=True),
        lax.all_gather(value_weight, "fsdp", axis=0, tiled=True),
        lax.all_gather(output_weight, "fsdp", axis=1, tiled=True),
        lax.all_gather(attn_gain, "fsdp", axis=0, tiled=True),
    )
    middle_low = middle_back.astype(jnp.bfloat16)
    mixed_back = project_back(middle_low, attn_back[3]).astype(jnp.bfloat16)

    def query_grads(query_one, key_heads, value_heads, grad_heads, log_total, allowed):
        scores = masked_scores(query_one, key_heads, allowed)
        weights = jnp.exp(scores - log_total)
        prob_back = jnp.einsum(
            "qhd,khd->hqk", grad_heads, value_heads, preferred_element_type=jnp.float32
        )
        inner = jnp.sum(weights * prob_back, axis=2, keepdims=True)
        score_back = (weights * (prob_back - inner)).astype(jnp.bfloat16)
        query_back = jnp.einsum(
            "hqk,khd->qhd", score_back, key_heads, preferred_element_type=jnp.float32
        ) * HD ** (-0.5)
        return (query_back, weights, score_back, inner)

    def attend_back(query_one, key_one, value_one, grad_one, log_total, starts, images, valid_row):
        allowed = sequence_mask(starts, images, valid_row)
        grad_heads = grad_one.reshape(local, heads_here, HD)
        query_back, weights, score_back, inner = query_grads(
            query_one,
            key_one.reshape(length, heads_here, HD),
            value_one.reshape(length, heads_here, HD),
            grad_heads,
            log_total,
            allowed,
        )
        key_back = jnp.einsum(
            "hqk,qhd->khd", score_back, query_one, preferred_element_type=jnp.float32
        ) * HD ** (-0.5)
        value_back = jnp.einsum(
            "hqk,qhd->khd",
            weights.astype(jnp.bfloat16),
            grad_heads,
            preferred_element_type=jnp.float32,
        )
        return (query_back, key_back.reshape(length, band), value_back.reshape(length, band))

    query_backs, key_parts, value_parts = blocked(
        attend_back,
        (
            queries,
            keys_all,
            values_all,
            mixed_back,
            log_totals,
            piece_start,
            piece_image,
            valid_mask,
        ),
    )
    key_backs, value_backs = (
        lax.psum_scatter(
            key_parts.astype(jnp.bfloat16), "fsdp", scatter_dimension=1, tiled=True
        ).astype(jnp.float32),
        lax.psum_scatter(
            value_parts.astype(jnp.bfloat16), "fsdp", scatter_dimension=1, tiled=True
        ).astype(jnp.float32),
    )
    query_low = unrotate(query_backs, cosine, sine).reshape(seqs, local, band).astype(jnp.bfloat16)
    key_low = (
        unrotate(key_backs.reshape(seqs, local, heads_here, HD), cosine, sine)
        .reshape(seqs, local, band)
        .astype(jnp.bfloat16)
    )
    value_low = value_backs.astype(jnp.bfloat16)
    partial_back = (
        project_back(query_low, attn_back[0])
        + project_back(key_low, attn_back[1])
        + project_back(value_low, attn_back[2])
    )
    normed_one_back = lax.psum(partial_back.astype(jnp.bfloat16), "dp").astype(jnp.float32)
    input_grad = (
        middle_back + norm_back(normed_one_back, residual, scale_one, attn_back[4])
    ).astype(jnp.bfloat16)
    query_part, key_part, value_part, output_term, attn_gain_part, mlp_gain_part = (
        lax.psum_scatter(
            weight_term(normed_one, query_low).astype(jnp.bfloat16),
            "fsdp",
            scatter_dimension=0,
            tiled=True,
        ).astype(jnp.float32),
        lax.psum_scatter(
            weight_term(normed_one, key_low).astype(jnp.bfloat16),
            "fsdp",
            scatter_dimension=0,
            tiled=True,
        ).astype(jnp.float32),
        lax.psum_scatter(
            weight_term(normed_one, value_low).astype(jnp.bfloat16),
            "fsdp",
            scatter_dimension=0,
            tiled=True,
        ).astype(jnp.float32),
        lax.psum_scatter(
            weight_term(middle_low, mixed).astype(jnp.bfloat16),
            "fsdp",
            scatter_dimension=0,
            tiled=True,
        ).astype(jnp.float32),
        lax.psum_scatter(
            jnp.sum(normed_one_back * residual * scale_one, axis=(0, 1)).astype(jnp.bfloat16),
            "fsdp",
            scatter_dimension=0,
            tiled=True,
        ).astype(jnp.float32),
        lax.psum_scatter(
            mlp_gain_term.astype(jnp.bfloat16), "fsdp", scatter_dimension=0, tiled=True
        ).astype(jnp.float32),
    )
    output_part = output_term.T
    return (
        output,
        input_grad,
        query_part,
        key_part,
        value_part,
        output_part,
        attn_gain_part,
        gate_part,
        up_part,
        down_part,
        mlp_gain_part,
        jnp.sqrt(totals[0] / count),
        jnp.sqrt(totals[1] / count),
        jnp.sqrt(totals[2] / count),
    )


VMEM_MOST = 66_000_000
MESH = pl.DeviceIdType.MESH
BF16 = jnp.bfloat16
F32 = jnp.float32
PAIR = 2 * HD
TILE = 256
STRIP = 32
SLAB = 512
HOP = 2

NT = (((1,), (1,)), ((), ()))
TN = (((0,), (0,)), ((), ()))


def mm(a, b):
    return jnp.dot(a, b, preferred_element_type=F32)


def mm_nt(a, b):
    return lax.dot_general(a, b, NT, preferred_element_type=F32)


def mm_tn(a, b):
    return lax.dot_general(a, b, TN, preferred_element_type=F32)


def half_swap(values):
    lane = lax.broadcasted_iota(jnp.int32, values.shape, 1) % HD
    ahead = pltpu.roll(values, PAIR - HD // 2, 1)
    behind = pltpu.roll(values, HD // 2, 1)
    return jnp.where(lane < HD // 2, ahead, behind)


def head_lanes(values, head):
    lane = lax.broadcasted_iota(jnp.int32, values.shape, 1) // HD
    return jnp.where(lane == head, values, jnp.zeros_like(values))


def diagonal_bias(is_piece):
    key = lax.broadcasted_iota(jnp.int32, (TILE, TILE), 0)
    query = lax.broadcasted_iota(jnp.int32, (TILE, TILE), 1)
    return jnp.where((key <= query) | is_piece, 0.0, NEG).astype(F32)


def attend_kernel(
    image_ref,
    q_in,
    k_in,
    v_in,
    cos_ref,
    sin_ref,
    bias_ref,
    q_ref,
    k_ref,
    v_ref,
    mixed_ref,
    lse_ref,
    top,
    total,
    acc,
    outs,
):
    length = q_in.shape[0]
    tiles = length // TILE
    cosine, sine = cos_ref[...], sin_ref[...]
    raw = q_in[...]
    q_ref[...] = ((raw * cosine + half_swap(raw) * sine) * HD ** (-0.5)).astype(BF16)
    raw = k_in[...]
    k_ref[...] = (raw * cosine + half_swap(raw) * sine).astype(BF16)
    v_ref[...] = v_in[...].astype(BF16)
    lse_ref[...] = jnp.zeros_like(lse_ref)
    for tile in range(tiles):
        here = slice(tile * TILE, (tile + 1) * TILE)
        upto = (tile + 1) * TILE
        corner = diagonal_bias(image_ref[tile] >= 0)
        for head in range(2):
            query = head_lanes(q_ref[here, :], head)
            scores = mm_nt(k_ref[:upto, :], query) + bias_ref[:upto, :]
            diag = scores[upto - TILE :, :] + corner
            highest = jnp.max(diag, axis=0, keepdims=True)
            if tile:
                before = scores[: upto - TILE, :]
                highest = jnp.maximum(highest, jnp.max(before, axis=0, keepdims=True))
                weight_low = jnp.exp(before - highest)
                weight_diag = jnp.exp(diag - highest)
                summed = jnp.sum(weight_low, axis=0, keepdims=True) + jnp.sum(
                    weight_diag, axis=0, keepdims=True
                )
                mixed = mm_tn(v_ref[: upto - TILE, :], weight_low.astype(BF16)) + mm_tn(
                    v_ref[upto - TILE : upto, :], weight_diag.astype(BF16)
                )
            else:
                weight_diag = jnp.exp(diag - highest)
                summed = jnp.sum(weight_diag, axis=0, keepdims=True)
                mixed = mm_tn(v_ref[:upto, :], weight_diag.astype(BF16))
            top[...] = highest
            total[...] = summed
            acc[...] = mixed
            for other in range(tile + 1, tiles):

                @pl.when((image_ref[tile] >= 0) & (image_ref[tile] == image_ref[other]))
                def _(other=other, query=query):
                    there = slice(other * TILE, (other + 1) * TILE)
                    extra = mm_nt(k_ref[there, :], query) + bias_ref[there, :]
                    newest = jnp.maximum(top[...], jnp.max(extra, axis=0, keepdims=True))
                    shrink = jnp.exp(top[...] - newest)
                    weight = jnp.exp(extra - newest)
                    total[...] = total[...] * shrink + jnp.sum(weight, axis=0, keepdims=True)
                    acc[...] = acc[...] * shrink + mm_tn(v_ref[there, :], weight.astype(BF16))
                    top[...] = newest

            rows = slice(head * HD, (head + 1) * HD)
            outs[rows, :] = acc[rows, :] / total[...]
            lse_ref[0, head : head + 1, here] = top[...] + jnp.log(total[...])
        mixed_ref[here, :] = outs[...].T.astype(BF16)


def attend(qkv, cosine, sine, bias, image):
    length, wide = qkv.shape
    band = wide // 3
    pairs = band // PAIR
    column = lambda shift: pl.BlockSpec((length, PAIR), lambda g, img: (0, g + shift))
    fixed = lambda cols: pl.BlockSpec((length, cols), lambda g, img: (0, 0))
    low = jax.ShapeDtypeStruct((length, band), BF16)
    return pl.pallas_call(
        attend_kernel,
        grid_spec=pltpu.PrefetchScalarGridSpec(
            num_scalar_prefetch=1,
            grid=(pairs,),
            in_specs=[
                column(0),
                column(pairs),
                column(2 * pairs),
                fixed(PAIR),
                fixed(PAIR),
                fixed(1),
            ],
            out_specs=[column(0)] * 4 + [pl.BlockSpec((1, 8, length), lambda g, img: (g, 0, 0))],
            scratch_shapes=[
                pltpu.VMEM((1, TILE), F32),
                pltpu.VMEM((1, TILE), F32),
                pltpu.VMEM((PAIR, TILE), F32),
                pltpu.VMEM((PAIR, TILE), F32),
            ],
        ),
        out_shape=[low] * 4 + [jax.ShapeDtypeStruct((pairs, 8, length), F32)],
        compiler_params=pltpu.CompilerParams(vmem_limit_bytes=VMEM_MOST),
        cost_estimate=pl.CostEstimate(
            flops=12_000_000_000, bytes_accessed=12_000_000, transcendentals=6_000_000
        ),
        name="attend",
    )(image, qkv, qkv, qkv, cosine, sine, bias)


def attend_back_kernel(
    image_ref,
    q_ref,
    k_ref,
    v_ref,
    g_ref,
    mixed_ref,
    lse_ref,
    cos_ref,
    sin_ref,
    bias_ref,
    dq_ref,
    dk_ref,
    dv_ref,
    dk_acc,
    dv_acc,
    dq_acc,
):
    length = q_ref.shape[0]
    tiles = length // TILE
    dk_acc[...] = jnp.zeros_like(dk_acc)
    dv_acc[...] = jnp.zeros_like(dv_acc)
    pick_row = lax.broadcasted_iota(jnp.int32, (8, PAIR), 0)
    pick_lane = lax.broadcasted_iota(jnp.int32, (8, PAIR), 1) // HD
    picker = (pick_row == pick_lane).astype(F32)
    for tile in range(tiles):
        here = slice(tile * TILE, (tile + 1) * TILE)
        corner = diagonal_bias(image_ref[tile] >= 0)
        product = mixed_ref[here, :].astype(F32) * g_ref[here, :].astype(F32)
        inners = lax.dot_general(
            picker, product, NT, precision=lax.Precision.HIGHEST, preferred_element_type=F32
        )
        for head in range(2):
            query = head_lanes(q_ref[here, :], head)
            grad = head_lanes(g_ref[here, :], head)
            inner = inners[head : head + 1, :]
            lse = lse_ref[0, head : head + 1, here]
            rows = slice(head * HD, (head + 1) * HD)

            def block(there, extra, first):
                scores = mm_nt(k_ref[there, :], query) + bias_ref[there, :]
                if extra is not None:
                    scores = scores + extra
                weight = jnp.exp(scores - lse)
                back = mm_nt(v_ref[there, :], grad)
                score_back = (weight * (back - inner)).astype(BF16)
                dv_acc[there, :] += mm(weight.astype(BF16), grad)
                dk_acc[there, :] += mm(score_back, query)
                part = mm_tn(k_ref[there, :], score_back)
                if first:
                    dq_acc[rows, :] = part[rows, :]
                else:
                    dq_acc[rows, :] += part[rows, :]

            block(here, corner, True)
            for other in range(tile):
                block(slice(other * TILE, (other + 1) * TILE), None, False)
            for other in range(tile + 1, tiles):

                @pl.when((image_ref[tile] >= 0) & (image_ref[tile] == image_ref[other]))
                def _(other=other):
                    block(slice(other * TILE, (other + 1) * TILE), None, False)

        turned = dq_acc[...].T * HD ** (-0.5)
        dq_ref[here, :] = (
            turned * cos_ref[here, :] - half_swap(turned) * sin_ref[here, :]
        ).astype(BF16)
    turned = dk_acc[...]
    dk_ref[...] = (turned * cos_ref[...] - half_swap(turned) * sin_ref[...]).astype(BF16)
    dv_ref[...] = dv_acc[...].astype(BF16)


def attend_back(queries, keys, values, grads, mixed, lse, cosine, sine, bias, image):
    length, band = queries.shape
    pairs = band // PAIR
    column = pl.BlockSpec((length, PAIR), lambda g, img: (0, g))
    fixed = lambda cols: pl.BlockSpec((length, cols), lambda g, img: (0, 0))
    low = jax.ShapeDtypeStruct((length, band), BF16)
    return pl.pallas_call(
        attend_back_kernel,
        grid_spec=pltpu.PrefetchScalarGridSpec(
            num_scalar_prefetch=1,
            grid=(pairs,),
            in_specs=[column] * 5
            + [
                pl.BlockSpec((1, 8, length), lambda g, img: (g, 0, 0)),
                fixed(PAIR),
                fixed(PAIR),
                fixed(1),
            ],
            out_specs=[column] * 3,
            scratch_shapes=[
                pltpu.VMEM((length, PAIR), F32),
                pltpu.VMEM((length, PAIR), F32),
                pltpu.VMEM((PAIR, TILE), F32),
            ],
        ),
        out_shape=[low] * 3,
        compiler_params=pltpu.CompilerParams(vmem_limit_bytes=VMEM_MOST),
        cost_estimate=pl.CostEstimate(
            flops=30_000_000_000, bytes_accessed=12_000_000, transcendentals=6_000_000
        ),
        name="attend_back",
    )(image, queries, keys, values, grads, mixed, lse, cosine, sine, bias)


VM = pl.BlockSpec(memory_space=pltpu.VMEM)
ANY = pl.BlockSpec(memory_space=pl.ANY)


def row_mean(values):
    return jnp.mean(values, axis=1, keepdims=True)


def col_sum(values):
    return jnp.sum(values, axis=0, keepdims=True)


def greet(n, peers=0):
    rank = lax.axis_index("dp")
    has_low, has_high = rank > 0, rank < n - 1
    barrier = pltpu.get_barrier_semaphore()

    @pl.when(has_low)
    def _():
        pl.semaphore_signal(
            barrier, inc=1, device_id={"dp": lax.rem(rank + n - 1, n)}, device_id_type=MESH
        )

    @pl.when(has_high)
    def _():
        pl.semaphore_signal(
            barrier, inc=1, device_id={"dp": lax.rem(rank + 1, n)}, device_id_type=MESH
        )

    mine = lax.axis_index("fsdp")
    for ahead in range(1, peers):
        pl.semaphore_signal(
            barrier, inc=1, device_id={"fsdp": lax.rem(mine + ahead, peers)}, device_id_type=MESH
        )
    both = has_low.astype(jnp.int32) + has_high.astype(jnp.int32)
    pl.semaphore_wait(barrier, both + max(peers - 1, 0))


def line_sum(n, own, flows, work, finish, shift=0):
    prefix, suffix, sems = flows
    send_high, send_low, got_low, got_high = (sems.at[k] for k in range(4))
    rank = lax.axis_index("dp")
    strips = own.shape[0] // STRIP
    has_low, has_high = rank > 0, rank < n - 1
    higher, lower = lax.rem(rank + 1, n), lax.rem(rank + n - 1, n)

    def rows_of(strip):
        at = strip if isinstance(shift, int) else lax.rem(strip + shift, strips)
        return pl.ds(pl.multiple_of(at * STRIP, STRIP), STRIP)

    def up(strip):
        rows = rows_of(strip)
        return pltpu.make_async_remote_copy(
            src_ref=prefix.at[rows],
            dst_ref=prefix.at[rows],
            send_sem=send_high.at[strip],
            recv_sem=got_low.at[strip],
            device_id={"dp": higher},
            device_id_type=MESH,
        )

    def down(strip):
        rows = rows_of(strip)
        return pltpu.make_async_remote_copy(
            src_ref=suffix.at[rows],
            dst_ref=suffix.at[rows],
            send_sem=send_low.at[strip],
            recv_sem=got_high.at[strip],
            device_id={"dp": lower},
            device_id_type=MESH,
        )

    late = jnp.maximum(rank, n - 1 - rank)

    def step(s, carry):
        work(s)
        a = s - rank * HOP

        @pl.when((a >= 0) & (a < strips))
        def _():
            rows = rows_of(a)

            @pl.when(has_low)
            def _():
                up(a).wait_recv()
                prefix[rows, :] = (
                    own[rows, :].astype(F32) + prefix[rows, :].astype(F32)
                ).astype(BF16)

            @pl.when(jnp.logical_not(has_low))
            def _():
                prefix[rows, :] = own[rows, :]

            @pl.when(has_high)
            def _():
                up(a).start()

        b = s - (n - 1 - rank) * HOP

        @pl.when((b >= 0) & (b < strips))
        def _():
            rows = rows_of(b)

            @pl.when(has_high)
            def _():
                down(b).wait_recv()
                suffix[rows, :] = (
                    own[rows, :].astype(F32) + suffix[rows, :].astype(F32)
                ).astype(BF16)

            @pl.when(jnp.logical_not(has_high))
            def _():
                suffix[rows, :] = own[rows, :]

            @pl.when(has_low)
            def _():
                down(b).start()

        c = s - late * HOP

        @pl.when((c >= 0) & (c < strips))
        def _():
            rows = rows_of(c)
            finish(
                c,
                rows,
                prefix[rows, :].astype(F32)
                + suffix[rows, :].astype(F32)
                - own[rows, :].astype(F32),
            )

        return carry

    lax.fori_loop(0, strips + (n - 1) * HOP, step, 0)

    def drain(s, carry):
        @pl.when(has_high)
        def _():
            up(s).wait_send()

        @pl.when(has_low)
        def _():
            down(s).wait_send()

        return carry

    lax.fori_loop(0, strips, drain, 0)


def flow_scratch(length, width):
    whole = pltpu.VMEM((length, width), BF16)
    return [whole] * 2 + [pltpu.SemaphoreType.DMA((4, length // STRIP))]


def line_call(kernel, n, name, collective_id, args, specs, outs, out_specs, scratch, flops):
    return pl.pallas_call(
        functools.partial(kernel, n),
        in_specs=specs,
        out_specs=out_specs,
        out_shape=outs,
        scratch_shapes=scratch,
        compiler_params=pltpu.CompilerParams(
            collective_id=collective_id, has_side_effects=True, vmem_limit_bytes=VMEM_MOST
        ),
        cost_estimate=pl.CostEstimate(
            flops=flops, bytes_accessed=300_000_000, transcendentals=0
        ),
        name=name,
    )(*args)


def wide_rows(group):
    return pl.ds(pl.multiple_of(group * TILE, TILE), TILE)


def product_nt(own, rows, pairs):
    width = own.shape[1]

    def piece(p, carry):
        cols = pl.ds(pl.multiple_of(p * SLAB, SLAB), SLAB)
        total = None
        for left, right in pairs:
            term = mm_nt(left(rows), right(cols))
            total = term if total is None else total + term
        own[rows, cols] = total.astype(BF16)
        return carry

    lax.fori_loop(0, width // SLAB, piece, 0)


def on_groups(s, length, make):
    per = TILE // STRIP

    @pl.when((lax.rem(s, per) == 0) & (s < length // STRIP))
    def _():
        make(lax.div(s, per))


def middle_kernel(
    n,
    mixed_ref,
    out_weight,
    source_hbm,
    gain,
    valid,
    middle_ref,
    normed_ref,
    stats_ref,
    weight,
    source,
    own,
    load_sems,
    *flows,
):
    band = weight.shape[1]
    length = own.shape[0]
    loads = [
        pltpu.make_async_copy(
            out_weight.at[:, pl.ds(out_weight.shape[1] - band, band)], weight, load_sems.at[0]
        ),
        pltpu.make_async_copy(source_hbm, source, load_sems.at[1]),
    ]
    for load in loads:
        load.start()
    greet(n)
    stats_ref[...] = jnp.zeros_like(stats_ref)
    for load in loads:
        load.wait()

    def make(group):
        product_nt(
            own,
            wide_rows(group),
            [(lambda rows: mixed_ref[rows, :], lambda cols: weight[cols, :])],
        )

    def finish(strip, rows, total):
        middle = source[rows, :].astype(F32) + total
        middle_ref[rows, :] = middle.astype(BF16)
        square = middle * middle
        scale = lax.rsqrt(row_mean(square) + EPS)
        normed_ref[rows, :] = (middle * scale * gain[...]).astype(BF16)
        stats_ref[0:1, :] += col_sum(square * valid[rows, :])
        stats_ref[1:2, :] += col_sum(total * total * valid[rows, :])

    line_sum(n, own, flows, lambda s: on_groups(s, length, make), finish)


def middle_sum(n, mixed, gathered, source, gain, valid):
    length, width = source.shape
    band = mixed.shape[1]
    rows = pltpu.VMEM((length, width), BF16)
    return line_call(
        middle_kernel,
        n,
        "middle_sum",
        1,
        (mixed, gathered, source, gain, valid),
        [VM, ANY, ANY, VM, VM],
        [
            jax.ShapeDtypeStruct((length, width), BF16),
            jax.ShapeDtypeStruct((length, width), BF16),
            jax.ShapeDtypeStruct((8, width), F32),
        ],
        [VM] * 3,
        [
            pltpu.VMEM((width, band), BF16),
            rows,
            rows,
            pltpu.SemaphoreType.DMA((2,)),
        ]
        + flow_scratch(length, width),
        50_000_000_000,
    )
def mlp_kernel(
    n,
    normed_hbm,
    upstream_hbm,
    middle_hbm,
    gain,
    weight_hbm,
    act_hbm,
    gate_back_hbm,
    up_back_hbm,
    low_ref,
    gain_ref,
    weight,
    normed,
    upstream,
    middle_in,
    own,
    acc,
    stage,
    load_sems,
    weight_sems,
    stage_sems,
    *flows,
):
    width, feed = weight.shape[0], weight.shape[1] // 3
    length = own.shape[0]
    blocks = feed // SLAB
    chunks = length // TILE
    loads = [
        pltpu.make_async_copy(normed_hbm, normed, load_sems.at[0]),
        pltpu.make_async_copy(upstream_hbm, upstream, load_sems.at[1]),
        pltpu.make_async_copy(middle_hbm, middle_in, load_sems.at[2]),
    ]

    def columns(kind, block):
        return pl.ds(pl.multiple_of(kind * feed + block * SLAB, SLAB), SLAB)

    def weight_load(kind, block):
        return pltpu.make_async_copy(
            weight_hbm.at[:, columns(kind, block)],
            weight.at[:, columns(kind, block)],
            weight_sems.at[kind, block],
        )

    loads[0].start()
    for kind in range(3):
        weight_load(kind, 0).start()
    loads[1].start()
    for block in range(1, blocks):
        for kind in range(3):
            weight_load(kind, block).start()
    loads[2].start()
    greet(n)
    gain_ref[...] = jnp.zeros_like(gain_ref)
    loads[0].wait()
    loads[1].wait()
    backs = (act_hbm, gate_back_hbm, up_back_hbm)

    def store(kind, unit):
        slot = lax.rem(unit, 2)
        rows = pl.ds(pl.multiple_of(lax.div(unit, blocks) * TILE, TILE), TILE)
        cols = pl.ds(pl.multiple_of(lax.rem(unit, blocks) * SLAB, SLAB), SLAB)
        return pltpu.make_async_copy(
            stage.at[slot, kind], backs[kind].at[rows, cols], stage_sems.at[slot, kind]
        )

    def unit_work(unit):
        block = lax.rem(unit, blocks)
        rows = pl.ds(pl.multiple_of(lax.div(unit, blocks) * TILE, TILE), TILE)
        slot = lax.rem(unit, 2)

        @pl.when(unit < blocks)
        def _():
            for kind in range(3):
                weight_load(kind, block).wait()

        @pl.when(unit >= 2)
        def _():
            for kind in range(3):
                store(kind, unit - 2).wait()

        here = normed[rows, :]
        gate_w = weight[:, columns(0, block)]
        up_w = weight[:, columns(1, block)]
        gate = mm(here, gate_w)
        up = mm(here, up_w)
        act_grad = mm(upstream[rows, :], weight[:, columns(2, block)])
        sig = jax.nn.sigmoid(gate)
        gate_sig = gate * sig
        stage[slot, 0] = (gate_sig * up).astype(BF16)
        gate_back = (act_grad * up * (sig + gate_sig * (1.0 - sig))).astype(BF16)
        up_back = (act_grad * gate_sig).astype(BF16)
        stage[slot, 1] = gate_back
        stage[slot, 2] = up_back
        for kind in range(3):
            store(kind, unit).start()
        part = mm_nt(gate_back, gate_w) + mm_nt(up_back, up_w)

        @pl.when(block == 0)
        def _():
            acc[...] = part

        @pl.when(block > 0)
        def _():
            acc[...] += part

        @pl.when(block == blocks - 1)
        def _():
            own[rows, :] = acc[...].astype(BF16)

    units = chunks * blocks

    def first(unit, carry):
        unit_work(unit)
        return carry

    lax.fori_loop(0, blocks, first, 0)
    loads[2].wait()
    per = (length // STRIP) // chunks

    def work(s):
        for k in range(max(1, blocks // per)):
            stride = max(1, per // blocks)
            unit = blocks + (s * max(1, blocks // per) + k if per <= blocks else lax.div(s, stride))

            @pl.when((unit < units) & (lax.rem(s, stride) == 0))
            def _(unit=unit):
                unit_work(unit)

    def finish(strip, rows, total):
        middle = middle_in[rows, :].astype(F32)
        scale = lax.rsqrt(row_mean(middle * middle) + EPS)
        scaled = total * gain[...]
        inner = row_mean(scaled * middle)
        back = upstream[rows, :].astype(F32) + scale * (scaled - middle * (scale * scale * inner))
        low_ref[rows, :] = back.astype(BF16)
        gain_ref[0:1, :] += col_sum(total * middle * scale)

    line_sum(n, own, flows, work, finish)
    for kind in range(3):
        store(kind, units - 2).wait()
        store(kind, units - 1).wait()


def mlp_sum(n, normed, upstream, middle, gain, weights):
    length, width = normed.shape
    feed = weights.shape[1] // 3
    rows = pltpu.VMEM((length, width), BF16)
    low = jax.ShapeDtypeStruct((length, feed), BF16)
    return line_call(
        mlp_kernel,
        n,
        "mlp_sum",
        2,
        (normed, upstream, middle, gain, weights),
        [ANY, ANY, ANY, VM, ANY],
        [low] * 3
        + [
            jax.ShapeDtypeStruct((length, width), BF16),
            jax.ShapeDtypeStruct((8, width), F32),
        ],
        [ANY] * 3 + [VM] * 2,
        [
            pltpu.VMEM((width, 3 * feed), BF16),
            rows,
            rows,
            rows,
            rows,
            pltpu.VMEM((TILE, width), F32),
            pltpu.VMEM((2, 3, TILE, SLAB), BF16),
            pltpu.SemaphoreType.DMA((3,)),
            pltpu.SemaphoreType.DMA((3, feed // SLAB)),
            pltpu.SemaphoreType.DMA((2, 3)),
        ]
        + flow_scratch(length, width),
        60_000_000_000,
    )
TURN = 128
GRAD = 256


def output_kernel(
    n,
    act_hbm,
    weight_hbm,
    middle_hbm,
    normed_hbm,
    upstream_hbm,
    gate_back_hbm,
    up_back_hbm,
    valid,
    out_ref,
    stats_ref,
    grads_hbm,
    act,
    down,
    middle,
    normed_t,
    upstream_t,
    gate_back,
    up_back,
    own,
    slices,
    stage,
    load_sems,
    slice_sems,
    stage_sems,
    *flows,
):
    length, width = own.shape
    feed = act.shape[1]
    loads = [
        pltpu.make_async_copy(act_hbm, act, load_sems.at[0]),
        pltpu.make_async_copy(weight_hbm.at[:, pl.ds(2 * feed, feed)], down, load_sems.at[1]),
        pltpu.make_async_copy(middle_hbm, middle, load_sems.at[2]),
        pltpu.make_async_copy(gate_back_hbm, gate_back, load_sems.at[3]),
        pltpu.make_async_copy(up_back_hbm, up_back, load_sems.at[4]),
    ]
    turns = length // TURN

    def slice_load(kind, turn):
        rows = pl.ds(pl.multiple_of(turn * TURN, TURN), TURN)
        slot = lax.rem(turn, 2)
        return pltpu.make_async_copy(
            (normed_hbm, upstream_hbm)[kind].at[rows],
            slices.at[slot, kind],
            slice_sems.at[slot, kind],
        )

    loads[0].start()
    loads[1].start()
    for turn in range(2):
        for kind in range(2):
            slice_load(kind, turn).start()
    for load in loads[2:]:
        load.start()
    greet(n)
    stats_ref[...] = jnp.zeros_like(stats_ref)
    loads[0].wait()
    loads[1].wait()

    def make(group):
        product_nt(
            own, wide_rows(group), [(lambda rows: act[rows, :], lambda cols: down[cols, :])]
        )

    blocks = feed // GRAD
    units = 3 * blocks

    def store(unit):
        cols = pl.ds(pl.multiple_of(unit * GRAD, GRAD), GRAD)
        slot = lax.rem(unit, 2)
        return pltpu.make_async_copy(stage.at[slot], grads_hbm.at[:, cols], stage_sems.at[slot])

    def grad_unit(unit):
        slot = lax.rem(unit, 2)

        @pl.when(unit >= 2)
        def _():
            store(unit - 2).wait()

        cols = pl.ds(pl.multiple_of(lax.rem(unit, blocks) * GRAD, GRAD), GRAD)
        for kind, (left, right) in enumerate(
            ((normed_t, gate_back), (normed_t, up_back), (upstream_t, act))
        ):

            @pl.when(lax.div(unit, blocks) == kind)
            def _(left=left, right=right):
                def piece(p, carry):
                    rows = pl.ds(pl.multiple_of(p * SLAB, SLAB), SLAB)
                    stage[slot, rows, :] = mm(left[rows, :], right[:, cols]).astype(BF16)
                    return carry

                lax.fori_loop(0, width // SLAB, piece, 0)

        store(unit).start()

    def work(s):
        on_groups(s, length, make)

        @pl.when(s < turns)
        def _():
            slot = lax.rem(s, 2)
            cols = pl.ds(pl.multiple_of(s * TURN, TURN), TURN)
            for kind, turned in enumerate((normed_t, upstream_t)):
                slice_load(kind, s).wait()
                turned[:, cols] = slices[slot, kind].T

                @pl.when(s + 2 < turns)
                def _(kind=kind):
                    slice_load(kind, s + 2).start()

        @pl.when(s == turns)
        def _():
            loads[3].wait()
            loads[4].wait()

        @pl.when((s >= turns) & (s < turns + units))
        def _():
            grad_unit(s - turns)

        @pl.when(s == 0)
        def _():
            loads[2].wait()

    def finish(strip, rows, total):
        out_ref[rows, :] = (middle[rows, :].astype(F32) + total).astype(BF16)
        stats_ref[0:1, :] += col_sum(total * total * valid[rows, :])

    line_sum(n, own, flows, work, finish)
    store(units - 2).wait()
    store(units - 1).wait()


def output_sum(n, act, weights, middle, normed, upstream, gate_back, up_back, valid):
    length, width = middle.shape
    feed = act.shape[1]
    rows = pltpu.VMEM((length, width), BF16)
    wide = pltpu.VMEM((length, feed), BF16)
    turned = pltpu.VMEM((width, length), BF16)
    return line_call(
        output_kernel,
        n,
        "output_sum",
        3,
        (act, weights, middle, normed, upstream, gate_back, up_back, valid),
        [ANY] * 7 + [VM],
        [
            jax.ShapeDtypeStruct((length, width), BF16),
            jax.ShapeDtypeStruct((8, width), F32),
            jax.ShapeDtypeStruct((width, 3 * feed), BF16),
        ],
        [VM, VM, ANY],
        [
            wide,
            pltpu.VMEM((width, feed), BF16),
            rows,
            turned,
            turned,
            wide,
            wide,
            rows,
            pltpu.VMEM((2, 2, TURN, width), BF16),
            pltpu.VMEM((2, width, GRAD), BF16),
            pltpu.SemaphoreType.DMA((5,)),
            pltpu.SemaphoreType.DMA((2, 2)),
            pltpu.SemaphoreType.DMA((2,)),
        ]
        + flow_scratch(length, width),
        60_000_000_000,
    )


def input_kernel(
    n,
    peers,
    dq_ref,
    dk_ref,
    dv_ref,
    weight_hbm,
    source_hbm,
    back_hbm,
    gain,
    rows_ref,
    out_hbm,
    small_ref,
    weight,
    source,
    back,
    own,
    result,
    small_own,
    small_got,
    load_sems,
    send_sems,
    recv_sems,
    home_sem,
    small_send,
    small_recv,
    *flows,
):
    length, width = own.shape
    band = dq_ref.shape[1]
    mine = lax.axis_index("fsdp")
    local = length // peers
    share = width // peers
    strips = length // STRIP
    per = local // STRIP
    loads = [
        pltpu.make_async_copy(weight_hbm.at[:, pl.ds(0, 3 * band)], weight, load_sems.at[0]),
        pltpu.make_async_copy(source_hbm, source, load_sems.at[1]),
        pltpu.make_async_copy(back_hbm, back, load_sems.at[2]),
    ]
    for load in loads:
        load.start()
    greet(n, peers)
    small_own[...] = rows_ref[...]
    small_own[0:1, :] = jnp.zeros((1, width), F32)
    loads[0].wait()
    halves = [
        (lambda rows, ref=ref: ref[rows, :], lambda cols, k=k: weight[cols, k * band : (k + 1) * band])
        for k, ref in enumerate((dq_ref, dk_ref, dv_ref))
    ]
    shift = mine * per

    def make(group):
        product_nt(own, wide_rows(group), halves)

    def work(s):
        full = TILE // STRIP
        base = lax.rem(s + shift, strips)

        @pl.when((s == 0) | ((lax.rem(base, full) == 0) & (s <= strips - full)))
        def _():
            make(lax.div(base, full))

        @pl.when(s == 0)
        def _():
            loads[1].wait()
            loads[2].wait()

    def place(strip):
        at = lax.rem(strip + shift, strips)
        owner = lax.div(at, per)
        inside = pl.ds(pl.multiple_of(lax.rem(at, per) * STRIP, STRIP), STRIP)
        rows = pl.ds(pl.multiple_of(at * STRIP, STRIP), STRIP)
        return owner, rows, inside

    def away(strip):
        owner, rows, inside = place(strip)
        return pltpu.make_async_remote_copy(
            src_ref=result.at[rows],
            dst_ref=out_hbm.at[mine, inside],
            send_sem=send_sems.at[strip],
            recv_sem=recv_sems.at[mine],
            device_id={"fsdp": owner},
            device_id_type=MESH,
        )

    def home(strip):
        owner, rows, inside = place(strip)
        return pltpu.make_async_copy(
            result.at[rows], out_hbm.at[mine, inside], home_sem.at[lax.rem(strip, per)]
        )

    def finish(strip, rows, total):
        here = source[rows, :].astype(F32)
        scale = lax.rsqrt(row_mean(here * here) + EPS)
        scaled = total * gain[...]
        inner = row_mean(scaled * here)
        result[rows, :] = (
            back[rows, :].astype(F32) + scale * (scaled - here * (scale * scale * inner))
        ).astype(BF16)
        small_own[0:1, :] += col_sum(total * here * scale)

        @pl.when(strip < per)
        def _():
            home(strip).start()

        @pl.when(strip >= per)
        def _():
            away(strip).start()

    line_sum(n, own, flows, work, finish, shift)

    def small(ahead):
        peer = lax.rem(mine + ahead, peers)
        cols = pl.ds(pl.multiple_of(peer * share, share), share)
        return pltpu.make_async_remote_copy(
            src_ref=small_own.at[:, cols],
            dst_ref=small_got.at[mine],
            send_sem=small_send.at[ahead],
            recv_sem=small_recv.at[mine],
            device_id={"fsdp": peer},
            device_id_type=MESH,
        )

    for ahead in range(1, peers):
        small(ahead).start()
    for strip in range(per):
        home(strip).wait()

    def drain(strip, carry):
        away(strip).wait_send()
        return carry

    lax.fori_loop(per, strips, drain, 0)
    total = small_own[:, pl.ds(pl.multiple_of(mine * share, share), share)]
    for ahead in range(1, peers):
        peer = lax.rem(mine + ahead, peers)
        pltpu.make_async_remote_copy(
            src_ref=small_own.at[:, pl.ds(0, share)],
            dst_ref=small_got.at[peer],
            send_sem=small_send.at[ahead],
            recv_sem=small_recv.at[peer],
            device_id={"fsdp": peer},
            device_id_type=MESH,
        ).wait_recv()
        total = total + small_got[peer]
        small(ahead).wait_send()
        pltpu.make_async_remote_copy(
            src_ref=result.at[pl.ds(0, local)],
            dst_ref=out_hbm.at[peer],
            send_sem=send_sems.at[0],
            recv_sem=recv_sems.at[peer],
            device_id={"fsdp": peer},
            device_id_type=MESH,
        ).wait_recv()
    small_ref[...] = total


def input_sum(n, peers, dq, dk, dv, weights, source, back, gain, small_rows):
    length, width = source.shape
    band = dq.shape[1]
    rows = pltpu.VMEM((length, width), BF16)
    share = width // peers
    return line_call(
        lambda count, *refs: input_kernel(count, peers, *refs),
        n,
        "input_sum",
        4,
        (dq, dk, dv, weights, source, back, gain, small_rows),
        [VM, VM, VM, ANY, ANY, ANY, VM, VM],
        [
            jax.ShapeDtypeStruct((peers, length // peers, width), BF16),
            jax.ShapeDtypeStruct((8, share), F32),
        ],
        [ANY, VM],
        [
            pltpu.VMEM((width, 3 * band), BF16),
            rows,
            rows,
            rows,
            rows,
            pltpu.VMEM((8, width), F32),
            pltpu.VMEM((peers, 8, share), F32),
            pltpu.SemaphoreType.DMA((3,)),
            pltpu.SemaphoreType.DMA((length // STRIP,)),
            pltpu.SemaphoreType.DMA((peers,)),
            pltpu.SemaphoreType.DMA((length // peers // STRIP,)),
            pltpu.SemaphoreType.DMA((peers,)),
            pltpu.SemaphoreType.DMA((peers,)),
        ]
        + flow_scratch(length, width),
        50_000_000_000,
    )
def per_device(
    mesh_sizes,
    inputs,
    cotangent,
    piece_start,
    piece_image,
    valid_mask,
    query_weight,
    key_weight,
    value_weight,
    output_weight,
    attn_gain,
    gate_weight,
    up_weight,
    down_weight,
    mlp_gain,
):
    spread, line = mesh_sizes
    seqs, local, width = inputs.shape
    length = valid_mask.shape[1]
    band = query_weight.shape[1]
    feed = gate_weight.shape[1]
    mine = lax.axis_index("fsdp")

    def swap(values):
        return lax.all_to_all(values, "fsdp", split_axis=0, concat_axis=0, tiled=True)

    gains = lax.all_gather(jnp.stack([attn_gain, mlp_gain]), "fsdp", axis=1, tiled=True)
    gains, inputs = lax.optimization_barrier((gains, inputs))
    gains = gains.astype(F32)
    attn_g, mlp_g = gains[0:1], gains[1:2]
    attn_w = lax.all_gather(
        jnp.concatenate([query_weight, key_weight, value_weight, output_weight.T], axis=1),
        "fsdp",
        axis=0,
        tiled=True,
    )
    mlp_w = lax.all_gather(
        jnp.concatenate([gate_weight, up_weight, down_weight.T], axis=1),
        "fsdp",
        axis=0,
        tiled=True,
    )
    source = swap(inputs).reshape(length, width)
    source, cotangent = lax.optimization_barrier((source, cotangent))
    upstream = swap(cotangent).reshape(length, width)

    places = jnp.arange(length, dtype=jnp.int32)
    cosine, sine = rope_tables(places, HD)
    signs = jnp.where(jnp.arange(HD) < HD // 2, -1.0, 1.0).astype(F32)
    cosine = jnp.concatenate([cosine, cosine], axis=1)
    sine = jnp.concatenate([sine * signs, sine * signs], axis=1)
    valid_row = lax.dynamic_index_in_dim(valid_mask, mine, 0, keepdims=False)
    valid = valid_row.astype(F32)[:, None]
    bias = jnp.where(valid_row > 0, 0.0, NEG).astype(F32)[:, None]
    starts = lax.dynamic_index_in_dim(piece_start, mine, 0, keepdims=False)
    images = lax.dynamic_index_in_dim(piece_image, mine, 0, keepdims=False)
    image = image_of(jnp.arange(length // TILE, dtype=jnp.int32) * TILE, starts, images).astype(
        jnp.int32
    )

    residual = source.astype(F32)
    scale_one = lax.rsqrt(jnp.mean(residual * residual, axis=1, keepdims=True) + EPS)
    normed_one = (residual * scale_one * attn_g).astype(BF16)
    qkv = mm(normed_one, attn_w[:, : 3 * band])
    queries, keys, values, mixed, lse = attend(qkv, cosine, sine, bias, image)
    middle, normed_two, stats = middle_sum(line, mixed, attn_w, source, mlp_g, valid)
    act, gate_back, up_back, middle_low, mlp_gain_sum = mlp_sum(
        line, normed_two, upstream, middle, mlp_g, mlp_w
    )
    result, mlp_stats, mlp_grads = output_sum(
        line, act, mlp_w, middle, normed_two, upstream, gate_back, up_back, valid
    )
    output = swap(result.reshape(seqs, local, width))
    mlp_grads = lax.psum_scatter(mlp_grads, "fsdp", scatter_dimension=0, tiled=True).astype(F32)

    mixed_back = mm(middle_low, attn_w[:, 3 * band :]).astype(BF16)
    dq, dk, dv = attend_back(
        queries, keys, values, mixed_back, mixed, lse, cosine, sine, bias, image
    )
    attn_terms = jnp.concatenate(
        [
            mm_tn(normed_one, dq).astype(BF16),
            mm_tn(normed_one, dk).astype(BF16),
            mm_tn(normed_one, dv).astype(BF16),
            mm_tn(middle_low, mixed).astype(BF16),
        ],
        axis=1,
    )
    sums = jnp.stack([jnp.sum(stats[0]), jnp.sum(stats[1]), jnp.sum(mlp_stats[0])])
    small_rows = jnp.concatenate(
        [
            jnp.zeros((1, width), F32),
            mlp_gain_sum[0:1],
            jnp.broadcast_to(sums[:, None], (3, width)),
            jnp.zeros((3, width), F32),
        ]
    )
    input_grad, small = input_sum(
        line, spread, dq, dk, dv, attn_w, source, middle_low, attn_g, small_rows
    )
    attn_grads = lax.psum_scatter(attn_terms, "fsdp", scatter_dimension=0, tiled=True).astype(F32)
    count = jnp.sum(valid_mask).astype(F32) * width
    roots = jnp.sqrt(small[2:5, 0] / count)
    return (
        output,
        input_grad,
        attn_grads[:, :band],
        attn_grads[:, band : 2 * band],
        attn_grads[:, 2 * band : 3 * band],
        attn_grads[:, 3 * band :].T,
        small[0],
        mlp_grads[:, :feed],
        mlp_grads[:, feed : 2 * feed],
        mlp_grads[:, 2 * feed :].T,
        small[1],
        roots[0],
        roots[1],
        roots[2],
    )


def solution(mesh):
    placed = (
        P(None, "fsdp", None),
        P(None, "fsdp", None),
        P(),
        P(),
        P(),
        P("fsdp", "dp"),
        P("fsdp", "dp"),
        P("fsdp", "dp"),
        P("dp", "fsdp"),
        P("fsdp"),
        P("fsdp", "dp"),
        P("fsdp", "dp"),
        P("dp", "fsdp"),
        P("fsdp"),
    )
    spread, line = mesh.shape["fsdp"], mesh.shape["dp"]

    def whole(*arrays):
        seqs, length, _ = arrays[0].shape
        own_sequence = seqs == spread and length % (2 * TILE) == 0 and line > 1
        each = functools.partial(per_device, (spread, line)) if own_sequence else per_device_gather
        return jax.shard_map(
            each,
            mesh=mesh,
            in_specs=placed,
            out_specs=(
                P(None, "fsdp", None),
                P(None, "fsdp", None),
                P("fsdp", "dp"),
                P("fsdp", "dp"),
                P("fsdp", "dp"),
                P("dp", "fsdp"),
                P("fsdp"),
                P("fsdp", "dp"),
                P("fsdp", "dp"),
                P("dp", "fsdp"),
                P("fsdp"),
                P(),
                P(),
                P(),
            ),
            check_vma=False,
        )(*arrays)

    return whole
```

```python
import functools

import jax
import jax.numpy as jnp
from jax import lax
from jax.experimental import pallas as pl
from jax.experimental.pallas import tpu as pltpu
from jax.sharding import PartitionSpec as P


HD = 64
PIECE = 256


EPS = 1e-05
THETA = 130000.0
NEG = -1e30


def rope_tables(positions, head_size):
    half = head_size // 2
    rates = THETA ** (-(jnp.arange(half, dtype=jnp.float32) * 2.0 / head_size))
    angle = positions.astype(jnp.float32)[:, None] * rates[None, :]
    cosine = jnp.concatenate([jnp.cos(angle), jnp.cos(angle)], axis=-1)
    sine = jnp.concatenate([jnp.sin(angle), jnp.sin(angle)], axis=-1)
    return (cosine, sine)


def rotate(values, cosine, sine):
    half = values.shape[-1] // 2
    turned = jnp.concatenate([-values[..., half:], values[..., :half]], axis=-1)
    return values * cosine[:, None, :] + turned * sine[:, None, :]


def unrotate(grads, cosine, sine):
    half = grads.shape[-1] // 2
    scaled = grads * sine[:, None, :]
    turned = jnp.concatenate([scaled[..., half:], -scaled[..., :half]], axis=-1)
    return grads * cosine[:, None, :] + turned


def image_of(positions, starts, images):
    inside = (positions[:, None] >= starts[None, :]) & (
        positions[:, None] < starts[None, :] + PIECE
    )
    return jnp.sum(jnp.where(inside, images[None, :] + 1, 0), axis=1) - 1


def allowed_mask(query_pos, key_pos, query_image, key_image, key_valid):
    causal = key_pos[None, :] <= query_pos[:, None]
    same = (query_image[:, None] >= 0) & (query_image[:, None] == key_image[None, :])
    return (causal | same) & (key_valid[None, :] > 0)


def project(values, weight):
    return jnp.einsum("std,de->ste", values, weight, preferred_element_type=jnp.float32)


def project_back(grads, weight):
    return jnp.einsum("ste,de->std", grads, weight, preferred_element_type=jnp.float32)


def weight_term(values, grads):
    return jnp.einsum("std,ste->de", values, grads, preferred_element_type=jnp.float32)


def masked_scores(queries, key_heads, allowed):
    raw = jnp.einsum(
        "qhd,khd->hqk", queries, key_heads, preferred_element_type=jnp.float32
    ) * HD ** (-0.5)
    return jnp.where(allowed[None, :, :], raw, NEG)


def norm_back(grad, source, scale, gain):
    scaled = grad * gain.astype(jnp.float32)
    inner = jnp.mean(scaled * source, axis=2, keepdims=True)
    return scale * (scaled - source * scale * scale * inner)


def blocked(step, items):
    total = items[0].shape[0]
    block_size = max((candidate for candidate in range(1, 9) if total % candidate == 0))
    groups = total // block_size
    shaped = tuple((item.reshape((groups, block_size) + item.shape[1:]) for item in items))
    results = lax.map(lambda group: jax.vmap(step)(*group), shaped)
    return jax.tree.map(
        lambda result: result.reshape((groups * block_size,) + result.shape[2:]), results
    )


def per_device_gather(
    inputs,
    cotangent,
    piece_start,
    piece_image,
    valid_mask,
    query_weight,
    key_weight,
    value_weight,
    output_weight,
    attn_gain,
    gate_weight,
    up_weight,
    down_weight,
    mlp_gain,
):
    seqs, local, width = inputs.shape
    length = valid_mask.shape[1]
    band = query_weight.shape[1]
    heads_here = band // HD
    offset = lax.axis_index("fsdp") * local
    positions = offset + jnp.arange(local, dtype=jnp.int32)
    key_places = jnp.arange(length, dtype=jnp.int32)
    cosine, sine = rope_tables(positions, HD)
    local_valid = lax.dynamic_slice_in_dim(valid_mask, offset, local, 1).astype(jnp.float32)

    def sequence_mask(starts, images, valid_row):
        query_image = image_of(positions, starts, images)
        key_image = image_of(key_places, starts, images)
        return allowed_mask(positions, key_places, query_image, key_image, valid_row)

    attn_set = (
        lax.all_gather(query_weight, "fsdp", axis=0, tiled=True),
        lax.all_gather(key_weight, "fsdp", axis=0, tiled=True),
        lax.all_gather(value_weight, "fsdp", axis=0, tiled=True),
        lax.all_gather(output_weight, "fsdp", axis=1, tiled=True),
        lax.all_gather(attn_gain, "fsdp", axis=0, tiled=True),
    )
    residual = inputs.astype(jnp.float32)
    scale_one = lax.rsqrt(jnp.mean(residual * residual, axis=2, keepdims=True) + EPS)
    normed_one = (residual * scale_one * attn_set[4].astype(jnp.float32)).astype(jnp.bfloat16)
    queries = rotate(
        project(normed_one, attn_set[0]).reshape(seqs, local, heads_here, HD), cosine, sine
    ).astype(jnp.bfloat16)
    keys_here = (
        rotate(project(normed_one, attn_set[1]).reshape(seqs, local, heads_here, HD), cosine, sine)
        .astype(jnp.bfloat16)
        .reshape(seqs, local, band)
    )
    values_here = project(normed_one, attn_set[2]).astype(jnp.bfloat16)
    keys_all, values_all = (
        lax.all_gather(keys_here, "fsdp", axis=1, tiled=True),
        lax.all_gather(values_here, "fsdp", axis=1, tiled=True),
    )

    def attend(query_one, key_one, value_one, starts, images, valid_row):
        allowed = sequence_mask(starts, images, valid_row)
        scores = masked_scores(query_one, key_one.reshape(length, heads_here, HD), allowed)
        highest = jnp.max(scores, axis=2, keepdims=True)
        log_total = highest + jnp.log(jnp.sum(jnp.exp(scores - highest), axis=2, keepdims=True))
        probs = jnp.exp(scores - log_total).astype(jnp.bfloat16)
        mixed_one = jnp.einsum(
            "hqk,khd->qhd",
            probs,
            value_one.reshape(length, heads_here, HD),
            preferred_element_type=jnp.float32,
        )
        return (mixed_one.reshape(local, band).astype(jnp.bfloat16), log_total)

    mixed, log_totals = blocked(
        attend, (queries, keys_all, values_all, piece_start, piece_image, valid_mask)
    )
    attn_out = lax.psum(project(mixed, attn_set[3]).astype(jnp.bfloat16), "dp").astype(jnp.float32)
    middle = residual + attn_out
    scale_two = lax.rsqrt(jnp.mean(middle * middle, axis=2, keepdims=True) + EPS)
    mlp_set = (
        lax.all_gather(gate_weight, "fsdp", axis=0, tiled=True),
        lax.all_gather(up_weight, "fsdp", axis=0, tiled=True),
        lax.all_gather(down_weight, "fsdp", axis=1, tiled=True),
        lax.all_gather(mlp_gain, "fsdp", axis=0, tiled=True),
    )
    normed_two = (middle * scale_two * mlp_set[3].astype(jnp.float32)).astype(jnp.bfloat16)
    gate = project(normed_two, mlp_set[0])
    up = project(normed_two, mlp_set[1])
    sigmoid_gate = jax.nn.sigmoid(gate)
    activated = (gate * sigmoid_gate * up).astype(jnp.bfloat16)
    mlp_out = lax.psum(project(activated, mlp_set[2]).astype(jnp.bfloat16), "dp").astype(
        jnp.float32
    )
    output = (middle + mlp_out).astype(jnp.bfloat16)
    row_weight = local_valid[:, :, None]
    totals = lax.psum(
        (
            jnp.sum(middle * middle * row_weight),
            jnp.sum(attn_out * attn_out * row_weight),
            jnp.sum(mlp_out * mlp_out * row_weight),
        ),
        "fsdp",
    )
    count = jnp.sum(valid_mask).astype(jnp.float32) * width
    mlp_back = (
        lax.all_gather(gate_weight, "fsdp", axis=0, tiled=True),
        lax.all_gather(up_weight, "fsdp", axis=0, tiled=True),
        lax.all_gather(down_weight, "fsdp", axis=1, tiled=True),
        lax.all_gather(mlp_gain, "fsdp", axis=0, tiled=True),
    )
    upstream = cotangent.astype(jnp.float32)
    act_grad = project_back(cotangent, mlp_back[2])
    gate_back = (
        act_grad * up * (sigmoid_gate + gate * sigmoid_gate * (1.0 - sigmoid_gate))
    ).astype(jnp.bfloat16)
    up_back = (act_grad * gate * sigmoid_gate).astype(jnp.bfloat16)
    normed_two_back = lax.psum(
        (project_back(gate_back, mlp_back[0]) + project_back(up_back, mlp_back[1])).astype(
            jnp.bfloat16
        ),
        "dp",
    ).astype(jnp.float32)
    middle_back = upstream + norm_back(normed_two_back, middle, scale_two, mlp_back[3])
    mlp_gain_term = jnp.sum(normed_two_back * middle * scale_two, axis=(0, 1))
    mlp_parts = lax.psum_scatter(
        jnp.concatenate(
            [
                weight_term(normed_two, gate_back),
                weight_term(normed_two, up_back),
                weight_term(cotangent, activated),
            ],
            axis=1,
        ).astype(jnp.bfloat16),
        "fsdp",
        scatter_dimension=0,
        tiled=True,
    ).astype(jnp.float32)
    feed = gate_weight.shape[1]
    gate_part = mlp_parts[:, :feed]
    up_part = mlp_parts[:, feed : 2 * feed]
    down_part = mlp_parts[:, 2 * feed :].T
    attn_back = (
        lax.all_gather(query_weight, "fsdp", axis=0, tiled=True),
        lax.all_gather(key_weight, "fsdp", axis=0, tiled=True),
        lax.all_gather(value_weight, "fsdp", axis=0, tiled=True),
        lax.all_gather(output_weight, "fsdp", axis=1, tiled=True),
        lax.all_gather(attn_gain, "fsdp", axis=0, tiled=True),
    )
    middle_low = middle_back.astype(jnp.bfloat16)
    mixed_back = project_back(middle_low, attn_back[3]).astype(jnp.bfloat16)

    def query_grads(query_one, key_heads, value_heads, grad_heads, log_total, allowed):
        scores = masked_scores(query_one, key_heads, allowed)
        weights = jnp.exp(scores - log_total)
        prob_back = jnp.einsum(
            "qhd,khd->hqk", grad_heads, value_heads, preferred_element_type=jnp.float32
        )
        inner = jnp.sum(weights * prob_back, axis=2, keepdims=True)
        score_back = (weights * (prob_back - inner)).astype(jnp.bfloat16)
        query_back = jnp.einsum(
            "hqk,khd->qhd", score_back, key_heads, preferred_element_type=jnp.float32
        ) * HD ** (-0.5)
        return (query_back, weights, score_back, inner)

    def attend_back(query_one, key_one, value_one, grad_one, log_total, starts, images, valid_row):
        allowed = sequence_mask(starts, images, valid_row)
        grad_heads = grad_one.reshape(local, heads_here, HD)
        query_back, weights, score_back, inner = query_grads(
            query_one,
            key_one.reshape(length, heads_here, HD),
            value_one.reshape(length, heads_here, HD),
            grad_heads,
            log_total,
            allowed,
        )
        key_back = jnp.einsum(
            "hqk,qhd->khd", score_back, query_one, preferred_element_type=jnp.float32
        ) * HD ** (-0.5)
        value_back = jnp.einsum(
            "hqk,qhd->khd",
            weights.astype(jnp.bfloat16),
            grad_heads,
            preferred_element_type=jnp.float32,
        )
        return (query_back, key_back.reshape(length, band), value_back.reshape(length, band))

    query_backs, key_parts, value_parts = blocked(
        attend_back,
        (
            queries,
            keys_all,
            values_all,
            mixed_back,
            log_totals,
            piece_start,
            piece_image,
            valid_mask,
        ),
    )
    key_backs, value_backs = (
        lax.psum_scatter(
            key_parts.astype(jnp.bfloat16), "fsdp", scatter_dimension=1, tiled=True
        ).astype(jnp.float32),
        lax.psum_scatter(
            value_parts.astype(jnp.bfloat16), "fsdp", scatter_dimension=1, tiled=True
        ).astype(jnp.float32),
    )
    query_low = unrotate(query_backs, cosine, sine).reshape(seqs, local, band).astype(jnp.bfloat16)
    key_low = (
        unrotate(key_backs.reshape(seqs, local, heads_here, HD), cosine, sine)
        .reshape(seqs, local, band)
        .astype(jnp.bfloat16)
    )
    value_low = value_backs.astype(jnp.bfloat16)
    partial_back = (
        project_back(query_low, attn_back[0])
        + project_back(key_low, attn_back[1])
        + project_back(value_low, attn_back[2])
    )
    normed_one_back = lax.psum(partial_back.astype(jnp.bfloat16), "dp").astype(jnp.float32)
    input_grad = (
        middle_back + norm_back(normed_one_back, residual, scale_one, attn_back[4])
    ).astype(jnp.bfloat16)
    query_part, key_part, value_part, output_term, attn_gain_part, mlp_gain_part = (
        lax.psum_scatter(
            weight_term(normed_one, query_low).astype(jnp.bfloat16),
            "fsdp",
            scatter_dimension=0,
            tiled=True,
        ).astype(jnp.float32),
        lax.psum_scatter(
            weight_term(normed_one, key_low).astype(jnp.bfloat16),
            "fsdp",
            scatter_dimension=0,
            tiled=True,
        ).astype(jnp.float32),
        lax.psum_scatter(
            weight_term(normed_one, value_low).astype(jnp.bfloat16),
            "fsdp",
            scatter_dimension=0,
            tiled=True,
        ).astype(jnp.float32),
        lax.psum_scatter(
            weight_term(middle_low, mixed).astype(jnp.bfloat16),
            "fsdp",
            scatter_dimension=0,
            tiled=True,
        ).astype(jnp.float32),
        lax.psum_scatter(
            jnp.sum(normed_one_back * residual * scale_one, axis=(0, 1)).astype(jnp.bfloat16),
            "fsdp",
            scatter_dimension=0,
            tiled=True,
        ).astype(jnp.float32),
        lax.psum_scatter(
            mlp_gain_term.astype(jnp.bfloat16), "fsdp", scatter_dimension=0, tiled=True
        ).astype(jnp.float32),
    )
    output_part = output_term.T
    return (
        output,
        input_grad,
        query_part,
        key_part,
        value_part,
        output_part,
        attn_gain_part,
        gate_part,
        up_part,
        down_part,
        mlp_gain_part,
        jnp.sqrt(totals[0] / count),
        jnp.sqrt(totals[1] / count),
        jnp.sqrt(totals[2] / count),
    )


VMEM_MOST = 66_000_000
MESH = pl.DeviceIdType.MESH
BF16 = jnp.bfloat16
F32 = jnp.float32
PAIR = 2 * HD
TILE = 256
STRIP = 32
SLAB = 512
HOP = 2

NT = (((1,), (1,)), ((), ()))
TN = (((0,), (0,)), ((), ()))


def mm(a, b):
    return jnp.dot(a, b, preferred_element_type=F32)


def mm_nt(a, b):
    return lax.dot_general(a, b, NT, preferred_element_type=F32)


def mm_tn(a, b):
    return lax.dot_general(a, b, TN, preferred_element_type=F32)


def half_swap(values):
    lane = lax.broadcasted_iota(jnp.int32, values.shape, 1) % HD
    ahead = pltpu.roll(values, PAIR - HD // 2, 1)
    behind = pltpu.roll(values, HD // 2, 1)
    return jnp.where(lane < HD // 2, ahead, behind)


def head_lanes(values, head):
    lane = lax.broadcasted_iota(jnp.int32, values.shape, 1) // HD
    return jnp.where(lane == head, values, jnp.zeros_like(values))


def diagonal_bias(is_piece):
    key = lax.broadcasted_iota(jnp.int32, (TILE, TILE), 0)
    query = lax.broadcasted_iota(jnp.int32, (TILE, TILE), 1)
    return jnp.where((key <= query) | is_piece, 0.0, NEG).astype(F32)


def attend_kernel(
    image_ref,
    q_in,
    k_in,
    v_in,
    cos_ref,
    sin_ref,
    bias_ref,
    q_ref,
    k_ref,
    v_ref,
    mixed_ref,
    lse_ref,
    top,
    total,
    acc,
    outs,
):
    length = q_in.shape[0]
    tiles = length // TILE
    cosine, sine = cos_ref[...], sin_ref[...]
    raw = q_in[...]
    q_ref[...] = ((raw * cosine + half_swap(raw) * sine) * HD ** (-0.5)).astype(BF16)
    raw = k_in[...]
    k_ref[...] = (raw * cosine + half_swap(raw) * sine).astype(BF16)
    v_ref[...] = v_in[...].astype(BF16)
    lse_ref[...] = jnp.zeros_like(lse_ref)
    for tile in range(tiles):
        here = slice(tile * TILE, (tile + 1) * TILE)
        upto = (tile + 1) * TILE
        corner = diagonal_bias(image_ref[tile] >= 0)
        for head in range(2):
            query = head_lanes(q_ref[here, :], head)
            scores = mm_nt(k_ref[:upto, :], query) + bias_ref[:upto, :]
            diag = scores[upto - TILE :, :] + corner
            highest = jnp.max(diag, axis=0, keepdims=True)
            if tile:
                before = scores[: upto - TILE, :]
                highest = jnp.maximum(highest, jnp.max(before, axis=0, keepdims=True))
                weight_low = jnp.exp(before - highest)
                weight_diag = jnp.exp(diag - highest)
                summed = jnp.sum(weight_low, axis=0, keepdims=True) + jnp.sum(
                    weight_diag, axis=0, keepdims=True
                )
                mixed = mm_tn(v_ref[: upto - TILE, :], weight_low.astype(BF16)) + mm_tn(
                    v_ref[upto - TILE : upto, :], weight_diag.astype(BF16)
                )
            else:
                weight_diag = jnp.exp(diag - highest)
                summed = jnp.sum(weight_diag, axis=0, keepdims=True)
                mixed = mm_tn(v_ref[:upto, :], weight_diag.astype(BF16))
            top[...] = highest
            total[...] = summed
            acc[...] = mixed
            for other in range(tile + 1, tiles):

                @pl.when((image_ref[tile] >= 0) & (image_ref[tile] == image_ref[other]))
                def _(other=other, query=query):
                    there = slice(other * TILE, (other + 1) * TILE)
                    extra = mm_nt(k_ref[there, :], query) + bias_ref[there, :]
                    newest = jnp.maximum(top[...], jnp.max(extra, axis=0, keepdims=True))
                    shrink = jnp.exp(top[...] - newest)
                    weight = jnp.exp(extra - newest)
                    total[...] = total[...] * shrink + jnp.sum(weight, axis=0, keepdims=True)
                    acc[...] = acc[...] * shrink + mm_tn(v_ref[there, :], weight.astype(BF16))
                    top[...] = newest

            rows = slice(head * HD, (head + 1) * HD)
            outs[rows, :] = acc[rows, :] / total[...]
            lse_ref[0, head : head + 1, here] = top[...] + jnp.log(total[...])
        mixed_ref[here, :] = outs[...].T.astype(BF16)


def attend(qkv, cosine, sine, bias, image):
    length, wide = qkv.shape
    band = wide // 3
    pairs = band // PAIR
    column = lambda shift: pl.BlockSpec((length, PAIR), lambda g, img: (0, g + shift))
    fixed = lambda cols: pl.BlockSpec((length, cols), lambda g, img: (0, 0))
    low = jax.ShapeDtypeStruct((length, band), BF16)
    return pl.pallas_call(
        attend_kernel,
        grid_spec=pltpu.PrefetchScalarGridSpec(
            num_scalar_prefetch=1,
            grid=(pairs,),
            in_specs=[
                column(0),
                column(pairs),
                column(2 * pairs),
                fixed(PAIR),
                fixed(PAIR),
                fixed(1),
            ],
            out_specs=[column(0)] * 4 + [pl.BlockSpec((1, 8, length), lambda g, img: (g, 0, 0))],
            scratch_shapes=[
                pltpu.VMEM((1, TILE), F32),
                pltpu.VMEM((1, TILE), F32),
                pltpu.VMEM((PAIR, TILE), F32),
                pltpu.VMEM((PAIR, TILE), F32),
            ],
        ),
        out_shape=[low] * 4 + [jax.ShapeDtypeStruct((pairs, 8, length), F32)],
        compiler_params=pltpu.CompilerParams(vmem_limit_bytes=VMEM_MOST),
        cost_estimate=pl.CostEstimate(
            flops=12_000_000_000, bytes_accessed=12_000_000, transcendentals=6_000_000
        ),
        name="attend",
    )(image, qkv, qkv, qkv, cosine, sine, bias)


def attend_back_kernel(
    image_ref,
    q_ref,
    k_ref,
    v_ref,
    g_ref,
    mixed_ref,
    lse_ref,
    cos_ref,
    sin_ref,
    bias_ref,
    dq_ref,
    dk_ref,
    dv_ref,
    dk_acc,
    dv_acc,
    dq_acc,
):
    length = q_ref.shape[0]
    tiles = length // TILE
    dk_acc[...] = jnp.zeros_like(dk_acc)
    dv_acc[...] = jnp.zeros_like(dv_acc)
    pick_row = lax.broadcasted_iota(jnp.int32, (8, PAIR), 0)
    pick_lane = lax.broadcasted_iota(jnp.int32, (8, PAIR), 1) // HD
    picker = (pick_row == pick_lane).astype(F32)
    for tile in range(tiles):
        here = slice(tile * TILE, (tile + 1) * TILE)
        corner = diagonal_bias(image_ref[tile] >= 0)
        product = mixed_ref[here, :].astype(F32) * g_ref[here, :].astype(F32)
        inners = lax.dot_general(
            picker, product, NT, precision=lax.Precision.HIGHEST, preferred_element_type=F32
        )
        for head in range(2):
            query = head_lanes(q_ref[here, :], head)
            grad = head_lanes(g_ref[here, :], head)
            inner = inners[head : head + 1, :]
            lse = lse_ref[0, head : head + 1, here]
            rows = slice(head * HD, (head + 1) * HD)

            def block(there, extra, first):
                scores = mm_nt(k_ref[there, :], query) + bias_ref[there, :]
                if extra is not None:
                    scores = scores + extra
                weight = jnp.exp(scores - lse)
                back = mm_nt(v_ref[there, :], grad)
                score_back = (weight * (back - inner)).astype(BF16)
                dv_acc[there, :] += mm(weight.astype(BF16), grad)
                dk_acc[there, :] += mm(score_back, query)
                part = mm_tn(k_ref[there, :], score_back)
                if first:
                    dq_acc[rows, :] = part[rows, :]
                else:
                    dq_acc[rows, :] += part[rows, :]

            block(here, corner, True)
            for other in range(tile):
                block(slice(other * TILE, (other + 1) * TILE), None, False)
            for other in range(tile + 1, tiles):

                @pl.when((image_ref[tile] >= 0) & (image_ref[tile] == image_ref[other]))
                def _(other=other):
                    block(slice(other * TILE, (other + 1) * TILE), None, False)

        turned = dq_acc[...].T * HD ** (-0.5)
        dq_ref[here, :] = (
            turned * cos_ref[here, :] - half_swap(turned) * sin_ref[here, :]
        ).astype(BF16)
    turned = dk_acc[...]
    dk_ref[...] = (turned * cos_ref[...] - half_swap(turned) * sin_ref[...]).astype(BF16)
    dv_ref[...] = dv_acc[...].astype(BF16)


def attend_back(queries, keys, values, grads, mixed, lse, cosine, sine, bias, image):
    length, band = queries.shape
    pairs = band // PAIR
    column = pl.BlockSpec((length, PAIR), lambda g, img: (0, g))
    fixed = lambda cols: pl.BlockSpec((length, cols), lambda g, img: (0, 0))
    low = jax.ShapeDtypeStruct((length, band), BF16)
    return pl.pallas_call(
        attend_back_kernel,
        grid_spec=pltpu.PrefetchScalarGridSpec(
            num_scalar_prefetch=1,
            grid=(pairs,),
            in_specs=[column] * 5
            + [
                pl.BlockSpec((1, 8, length), lambda g, img: (g, 0, 0)),
                fixed(PAIR),
                fixed(PAIR),
                fixed(1),
            ],
            out_specs=[column] * 3,
            scratch_shapes=[
                pltpu.VMEM((length, PAIR), F32),
                pltpu.VMEM((length, PAIR), F32),
                pltpu.VMEM((PAIR, TILE), F32),
            ],
        ),
        out_shape=[low] * 3,
        compiler_params=pltpu.CompilerParams(vmem_limit_bytes=VMEM_MOST),
        cost_estimate=pl.CostEstimate(
            flops=30_000_000_000, bytes_accessed=12_000_000, transcendentals=6_000_000
        ),
        name="attend_back",
    )(image, queries, keys, values, grads, mixed, lse, cosine, sine, bias)


VM = pl.BlockSpec(memory_space=pltpu.VMEM)
ANY = pl.BlockSpec(memory_space=pl.ANY)


def row_mean(values):
    return jnp.mean(values, axis=1, keepdims=True)


def col_sum(values):
    return jnp.sum(values, axis=0, keepdims=True)


def greet(n, peers=0):
    rank = lax.axis_index("dp")
    has_low, has_high = rank > 0, rank < n - 1
    barrier = pltpu.get_barrier_semaphore()

    @pl.when(has_low)
    def _():
        pl.semaphore_signal(
            barrier, inc=1, device_id={"dp": lax.rem(rank + n - 1, n)}, device_id_type=MESH
        )

    @pl.when(has_high)
    def _():
        pl.semaphore_signal(
            barrier, inc=1, device_id={"dp": lax.rem(rank + 1, n)}, device_id_type=MESH
        )

    mine = lax.axis_index("fsdp")
    for ahead in range(1, peers):
        pl.semaphore_signal(
            barrier, inc=1, device_id={"fsdp": lax.rem(mine + ahead, peers)}, device_id_type=MESH
        )
    both = has_low.astype(jnp.int32) + has_high.astype(jnp.int32)
    pl.semaphore_wait(barrier, both + max(peers - 1, 0))


def line_sum(n, own, flows, work, finish, shift=0):
    prefix, suffix, sems = flows
    send_high, send_low, got_low, got_high = (sems.at[k] for k in range(4))
    rank = lax.axis_index("dp")
    strips = own.shape[0] // STRIP
    has_low, has_high = rank > 0, rank < n - 1
    higher, lower = lax.rem(rank + 1, n), lax.rem(rank + n - 1, n)

    def rows_of(strip):
        at = strip if isinstance(shift, int) else lax.rem(strip + shift, strips)
        return pl.ds(pl.multiple_of(at * STRIP, STRIP), STRIP)

    def up(strip):
        rows = rows_of(strip)
        return pltpu.make_async_remote_copy(
            src_ref=prefix.at[rows],
            dst_ref=prefix.at[rows],
            send_sem=send_high.at[strip],
            recv_sem=got_low.at[strip],
            device_id={"dp": higher},
            device_id_type=MESH,
        )

    def down(strip):
        rows = rows_of(strip)
        return pltpu.make_async_remote_copy(
            src_ref=suffix.at[rows],
            dst_ref=suffix.at[rows],
            send_sem=send_low.at[strip],
            recv_sem=got_high.at[strip],
            device_id={"dp": lower},
            device_id_type=MESH,
        )

    late = jnp.maximum(rank, n - 1 - rank)

    def step(s, carry):
        work(s)
        a = s - rank * HOP

        @pl.when((a >= 0) & (a < strips))
        def _():
            rows = rows_of(a)

            @pl.when(has_low)
            def _():
                up(a).wait_recv()
                prefix[rows, :] = (
                    own[rows, :].astype(F32) + prefix[rows, :].astype(F32)
                ).astype(BF16)

            @pl.when(jnp.logical_not(has_low))
            def _():
                prefix[rows, :] = own[rows, :]

            @pl.when(has_high)
            def _():
                up(a).start()

        b = s - (n - 1 - rank) * HOP

        @pl.when((b >= 0) & (b < strips))
        def _():
            rows = rows_of(b)

            @pl.when(has_high)
            def _():
                down(b).wait_recv()
                suffix[rows, :] = (
                    own[rows, :].astype(F32) + suffix[rows, :].astype(F32)
                ).astype(BF16)

            @pl.when(jnp.logical_not(has_high))
            def _():
                suffix[rows, :] = own[rows, :]

            @pl.when(has_low)
            def _():
                down(b).start()

        c = s - late * HOP

        @pl.when((c >= 0) & (c < strips))
        def _():
            rows = rows_of(c)
            finish(
                c,
                rows,
                prefix[rows, :].astype(F32)
                + suffix[rows, :].astype(F32)
                - own[rows, :].astype(F32),
            )

        return carry

    lax.fori_loop(0, strips + (n - 1) * HOP, step, 0)

    def drain(s, carry):
        @pl.when(has_high)
        def _():
            up(s).wait_send()

        @pl.when(has_low)
        def _():
            down(s).wait_send()

        return carry

    lax.fori_loop(0, strips, drain, 0)


def flow_scratch(length, width):
    whole = pltpu.VMEM((length, width), BF16)
    return [whole] * 2 + [pltpu.SemaphoreType.DMA((4, length // STRIP))]


def line_call(kernel, n, name, collective_id, args, specs, outs, out_specs, scratch, flops):
    return pl.pallas_call(
        functools.partial(kernel, n),
        in_specs=specs,
        out_specs=out_specs,
        out_shape=outs,
        scratch_shapes=scratch,
        compiler_params=pltpu.CompilerParams(
            collective_id=collective_id, has_side_effects=True, vmem_limit_bytes=VMEM_MOST
        ),
        cost_estimate=pl.CostEstimate(
            flops=flops, bytes_accessed=300_000_000, transcendentals=0
        ),
        name=name,
    )(*args)


def wide_rows(group):
    return pl.ds(pl.multiple_of(group * TILE, TILE), TILE)


def product_nt(own, rows, pairs):
    width = own.shape[1]

    def piece(p, carry):
        cols = pl.ds(pl.multiple_of(p * SLAB, SLAB), SLAB)
        total = None
        for left, right in pairs:
            term = mm_nt(left(rows), right(cols))
            total = term if total is None else total + term
        own[rows, cols] = total.astype(BF16)
        return carry

    lax.fori_loop(0, width // SLAB, piece, 0)


def on_groups(s, length, make):
    per = TILE // STRIP

    @pl.when((lax.rem(s, per) == 0) & (s < length // STRIP))
    def _():
        make(lax.div(s, per))


def middle_kernel(
    n,
    mixed_ref,
    out_weight,
    source_hbm,
    gain,
    valid,
    middle_ref,
    normed_ref,
    stats_ref,
    weight,
    source,
    own,
    load_sems,
    *flows,
):
    band = weight.shape[1]
    length = own.shape[0]
    loads = [
        pltpu.make_async_copy(
            out_weight.at[:, pl.ds(out_weight.shape[1] - band, band)], weight, load_sems.at[0]
        ),
        pltpu.make_async_copy(source_hbm, source, load_sems.at[1]),
    ]
    for load in loads:
        load.start()
    greet(n)
    stats_ref[...] = jnp.zeros_like(stats_ref)
    for load in loads:
        load.wait()

    def make(group):
        product_nt(
            own,
            wide_rows(group),
            [(lambda rows: mixed_ref[rows, :], lambda cols: weight[cols, :])],
        )

    def finish(strip, rows, total):
        middle = source[rows, :].astype(F32) + total
        middle_ref[rows, :] = middle.astype(BF16)
        square = middle * middle
        scale = lax.rsqrt(row_mean(square) + EPS)
        normed_ref[rows, :] = (middle * scale * gain[...]).astype(BF16)
        stats_ref[0:1, :] += col_sum(square * valid[rows, :])
        stats_ref[1:2, :] += col_sum(total * total * valid[rows, :])

    line_sum(n, own, flows, lambda s: on_groups(s, length, make), finish)


def middle_sum(n, mixed, gathered, source, gain, valid):
    length, width = source.shape
    band = mixed.shape[1]
    rows = pltpu.VMEM((length, width), BF16)
    return line_call(
        middle_kernel,
        n,
        "middle_sum",
        1,
        (mixed, gathered, source, gain, valid),
        [VM, ANY, ANY, VM, VM],
        [
            jax.ShapeDtypeStruct((length, width), BF16),
            jax.ShapeDtypeStruct((length, width), BF16),
            jax.ShapeDtypeStruct((8, width), F32),
        ],
        [VM] * 3,
        [
            pltpu.VMEM((width, band), BF16),
            rows,
            rows,
            pltpu.SemaphoreType.DMA((2,)),
        ]
        + flow_scratch(length, width),
        50_000_000_000,
    )
TURN = 128
GRAD = 256


def mlp_kernel(
    n,
    normed_hbm,
    upstream_hbm,
    middle_hbm,
    gain,
    weight_hbm,
    act_hbm,
    gate_back_hbm,
    up_back_hbm,
    grads_hbm,
    low_ref,
    gain_ref,
    weight,
    normed,
    upstream,
    middle_in,
    own,
    acc,
    stage,
    load_sems,
    weight_sems,
    stage_sems,
    right_sems,
    grad_sems,
    *flows,
):
    width, feed = weight.shape[0], weight.shape[1] // 3
    length = own.shape[0]
    blocks = feed // SLAB
    chunks = length // TILE
    loads = [
        pltpu.make_async_copy(normed_hbm, normed, load_sems.at[0]),
        pltpu.make_async_copy(upstream_hbm, upstream, load_sems.at[1]),
        pltpu.make_async_copy(middle_hbm, middle_in, load_sems.at[2]),
    ]

    def columns(kind, block):
        return pl.ds(pl.multiple_of(kind * feed + block * SLAB, SLAB), SLAB)

    def weight_load(kind, block):
        return pltpu.make_async_copy(
            weight_hbm.at[:, columns(kind, block)],
            weight.at[:, columns(kind, block)],
            weight_sems.at[kind, block],
        )

    loads[0].start()
    for kind in range(3):
        weight_load(kind, 0).start()
    loads[1].start()
    for block in range(1, blocks):
        for kind in range(3):
            weight_load(kind, block).start()
    loads[2].start()
    greet(n)
    gain_ref[...] = jnp.zeros_like(gain_ref)
    loads[0].wait()
    loads[1].wait()
    backs = (act_hbm, gate_back_hbm, up_back_hbm)

    def store(kind, unit):
        slot = lax.rem(unit, 2)
        rows = pl.ds(pl.multiple_of(lax.div(unit, blocks) * TILE, TILE), TILE)
        cols = pl.ds(pl.multiple_of(lax.rem(unit, blocks) * SLAB, SLAB), SLAB)
        return pltpu.make_async_copy(
            stage.at[slot, kind], backs[kind].at[rows, cols], stage_sems.at[slot, kind]
        )

    def unit_work(unit):
        block = lax.rem(unit, blocks)
        rows = pl.ds(pl.multiple_of(lax.div(unit, blocks) * TILE, TILE), TILE)
        slot = lax.rem(unit, 2)

        @pl.when(unit < blocks)
        def _():
            for kind in range(3):
                weight_load(kind, block).wait()

        @pl.when(unit >= 2)
        def _():
            for kind in range(3):
                store(kind, unit - 2).wait()

        here = normed[rows, :]
        gate_w = weight[:, columns(0, block)]
        up_w = weight[:, columns(1, block)]
        gate = mm(here, gate_w)
        up = mm(here, up_w)
        act_grad = mm(upstream[rows, :], weight[:, columns(2, block)])
        sig = jax.nn.sigmoid(gate)
        gate_sig = gate * sig
        stage[slot, 0] = (gate_sig * up).astype(BF16)
        gate_back = (act_grad * up * (sig + gate_sig * (1.0 - sig))).astype(BF16)
        up_back = (act_grad * gate_sig).astype(BF16)
        stage[slot, 1] = gate_back
        stage[slot, 2] = up_back
        for kind in range(3):
            store(kind, unit).start()
        part = mm_nt(gate_back, gate_w) + mm_nt(up_back, up_w)

        @pl.when(block == 0)
        def _():
            acc[...] = part

        @pl.when(block > 0)
        def _():
            acc[...] += part

        @pl.when(block == blocks - 1)
        def _():
            own[rows, :] = acc[...].astype(BF16)

    units = chunks * blocks

    def first(unit, carry):
        unit_work(unit)
        return carry

    lax.fori_loop(0, blocks, first, 0)
    loads[2].wait()
    per = (length // STRIP) // chunks
    stride = per // blocks
    last = (units - blocks - 1) * stride

    turned = weight.at[:, pl.ds(0, length)]
    each = feed // GRAD
    grads = 2 * each
    turn_steps = 4
    turns = length // TURN // turn_steps
    begin = last + 1 + turn_steps
    at_once = -(-grads // (length // STRIP + (n - 1) * HOP - begin))

    def right(unit):
        return weight.at[
            pl.ds(0, length),
            pl.ds(pl.multiple_of(length + lax.rem(unit, 2) * GRAD, GRAD), GRAD),
        ]

    def made(unit):
        return weight.at[
            :, pl.ds(pl.multiple_of(length + (2 + lax.rem(unit, 2)) * GRAD, GRAD), GRAD)
        ]

    def right_load(unit, kind):
        cols = pl.ds(pl.multiple_of(lax.rem(unit, each) * GRAD, GRAD), GRAD)
        return pltpu.make_async_copy(
            backs[1 + kind].at[:, cols], right(unit), right_sems.at[lax.rem(unit, 2)]
        )

    def fetch(unit):
        for kind in range(2):

            @pl.when(lax.div(unit, each) == kind)
            def _(kind=kind):
                right_load(unit, kind).start()

    def grad_store(unit):
        cols = pl.ds(pl.multiple_of(unit * GRAD, GRAD), GRAD)
        return pltpu.make_async_copy(
            made(unit), grads_hbm.at[:, cols], grad_sems.at[lax.rem(unit, 2)]
        )

    def grad_work(unit):
        right_load(unit, 0).wait()

        @pl.when(unit >= 2)
        def _():
            grad_store(unit - 2).wait()

        here, there = right(unit), made(unit)

        def piece(p, carry):
            rows = pl.ds(pl.multiple_of(p * SLAB, SLAB), SLAB)
            there[rows, :] = mm(turned[rows, :], here[...]).astype(BF16)
            return carry

        lax.fori_loop(0, width // SLAB, piece, 0)
        grad_store(unit).start()

        @pl.when(unit + 2 < grads)
        def _():
            fetch(unit + 2)

    def work(s):
        @pl.when((s <= last) & (lax.rem(s, stride) == 0))
        def _():
            unit_work(blocks + lax.div(s, stride))

        @pl.when(s == last + 1)
        def _():
            for kind in range(3):
                store(kind, units - 2).wait()
                store(kind, units - 1).wait()
            fetch(0)
            fetch(1)

        @pl.when((s > last) & (s < begin))
        def _():
            for k in range(turns):
                at = pl.multiple_of(((s - last - 1) * turns + k) * TURN, TURN)
                turned[:, pl.ds(at, TURN)] = normed[pl.ds(at, TURN), :].T

        @pl.when(s >= begin)
        def _():
            def some(k, carry):
                unit = (s - begin) * at_once + k

                @pl.when(unit < grads)
                def _():
                    grad_work(unit)

                return carry

            lax.fori_loop(0, at_once, some, 0)

    def finish(strip, rows, total):
        middle = middle_in[rows, :].astype(F32)
        scale = lax.rsqrt(row_mean(middle * middle) + EPS)
        scaled = total * gain[...]
        inner = row_mean(scaled * middle)
        back = upstream[rows, :].astype(F32) + scale * (scaled - middle * (scale * scale * inner))
        low_ref[rows, :] = back.astype(BF16)
        gain_ref[0:1, :] += col_sum(total * middle * scale)

    line_sum(n, own, flows, work, finish)
    grad_store(grads - 2).wait()
    grad_store(grads - 1).wait()


def mlp_sum(n, normed, upstream, middle, gain, weights):
    length, width = normed.shape
    feed = weights.shape[1] // 3
    rows = pltpu.VMEM((length, width), BF16)
    low = jax.ShapeDtypeStruct((length, feed), BF16)
    return line_call(
        mlp_kernel,
        n,
        "mlp_sum",
        2,
        (normed, upstream, middle, gain, weights),
        [ANY, ANY, ANY, VM, ANY],
        [low] * 3
        + [
            jax.ShapeDtypeStruct((width, 2 * feed), BF16),
            jax.ShapeDtypeStruct((length, width), BF16),
            jax.ShapeDtypeStruct((8, width), F32),
        ],
        [ANY] * 4 + [VM] * 2,
        [
            pltpu.VMEM((width, 3 * feed), BF16),
            rows,
            rows,
            rows,
            rows,
            pltpu.VMEM((TILE, width), F32),
            pltpu.VMEM((2, 3, TILE, SLAB), BF16),
            pltpu.SemaphoreType.DMA((3,)),
            pltpu.SemaphoreType.DMA((3, feed // SLAB)),
            pltpu.SemaphoreType.DMA((2, 3)),
            pltpu.SemaphoreType.DMA((2,)),
            pltpu.SemaphoreType.DMA((2,)),
        ]
        + flow_scratch(length, width),
        60_000_000_000,
    )
def scatter(length, peers, result, out_hbm, sems):
    send_sems, recv_sems, home_sems = sems
    mine = lax.axis_index("fsdp")
    strips, local = length // STRIP, length // peers
    per = local // STRIP
    shift = mine * per

    def place(strip):
        at = lax.rem(strip + shift, strips)
        inside = pl.ds(pl.multiple_of(lax.rem(at, per) * STRIP, STRIP), STRIP)
        rows = pl.ds(pl.multiple_of(at * STRIP, STRIP), STRIP)
        return lax.div(at, per), rows, inside

    def away(strip):
        owner, rows, inside = place(strip)
        return pltpu.make_async_remote_copy(
            src_ref=result.at[rows],
            dst_ref=out_hbm.at[mine, inside],
            send_sem=send_sems.at[strip],
            recv_sem=recv_sems.at[mine],
            device_id={"fsdp": owner},
            device_id_type=MESH,
        )

    def home(strip):
        _, rows, inside = place(strip)
        return pltpu.make_async_copy(
            result.at[rows], out_hbm.at[mine, inside], home_sems.at[lax.rem(strip, per)]
        )

    def send(strip):
        @pl.when(strip < per)
        def _():
            home(strip).start()

        @pl.when(strip >= per)
        def _():
            away(strip).start()

    def drain():
        for strip in range(per):
            home(strip).wait()

        def sent(strip, carry):
            away(strip).wait_send()
            return carry

        lax.fori_loop(per, strips, sent, 0)
        for ahead in range(1, peers):
            peer = lax.rem(mine + ahead, peers)
            pltpu.make_async_remote_copy(
                src_ref=result.at[pl.ds(0, local)],
                dst_ref=out_hbm.at[peer],
                send_sem=send_sems.at[0],
                recv_sem=recv_sems.at[peer],
                device_id={"fsdp": peer},
                device_id_type=MESH,
            ).wait_recv()

    return send, drain, shift


def scatter_scratch(length, peers):
    return [
        pltpu.SemaphoreType.DMA((length // STRIP,)),
        pltpu.SemaphoreType.DMA((peers,)),
        pltpu.SemaphoreType.DMA((length // peers // STRIP,)),
    ]


def on_shifted_groups(s, shift, strips, make):
    full = TILE // STRIP
    base = lax.rem(s + shift, strips)

    @pl.when((s == 0) | ((lax.rem(base, full) == 0) & (s <= strips - full)))
    def _():
        make(lax.div(base, full))


def output_kernel(
    n,
    peers,
    act_hbm,
    weight_hbm,
    middle_hbm,
    upstream_hbm,
    normed_hbm,
    low_hbm,
    dq_hbm,
    dk_hbm,
    dv_hbm,
    mixed_hbm,
    valid,
    out_hbm,
    stats_ref,
    grads_hbm,
    result,
    act,
    down,
    middle,
    upstream_t,
    normed_t,
    low_t,
    rights,
    own,
    slices,
    stage,
    load_sems,
    slice_sems,
    stage_sems,
    send_sems,
    recv_sems,
    home_sems,
    *flows,
):
    length, width = own.shape
    feed = act.shape[1]
    loads = [
        pltpu.make_async_copy(act_hbm, act, load_sems.at[0]),
        pltpu.make_async_copy(weight_hbm.at[:, pl.ds(2 * feed, feed)], down, load_sems.at[1]),
        pltpu.make_async_copy(middle_hbm, middle, load_sems.at[2]),
    ]
    band = dq_hbm.shape[1]
    for k, ref in enumerate((dq_hbm, dk_hbm, dv_hbm, mixed_hbm)):
        loads.append(
            pltpu.make_async_copy(
                ref, rights.at[:, k * band : (k + 1) * band], load_sems.at[3 + k]
            )
        )
    turned = (upstream_t, normed_t, low_t)
    turns = length // TURN

    def slice_load(kind, turn):
        rows = pl.ds(pl.multiple_of(turn * TURN, TURN), TURN)
        slot = lax.rem(turn, 2)
        return pltpu.make_async_copy(
            (upstream_hbm, normed_hbm, low_hbm)[kind].at[rows],
            slices.at[slot, kind],
            slice_sems.at[slot, kind],
        )

    loads[0].start()
    loads[1].start()
    for turn in range(2):
        for kind in range(3):
            slice_load(kind, turn).start()
    for load in loads[2:]:
        load.start()
    greet(n, peers)
    stats_ref[...] = jnp.zeros_like(stats_ref)
    loads[0].wait()
    loads[1].wait()

    def make(group):
        product_nt(
            own, wide_rows(group), [(lambda rows: act[rows, :], lambda cols: down[cols, :])]
        )

    edges = (0, feed // GRAD, (feed + 3 * band) // GRAD, (feed + 4 * band) // GRAD)
    units = edges[3]

    def store(unit):
        cols = pl.ds(pl.multiple_of(unit * GRAD, GRAD), GRAD)
        slot = lax.rem(unit, 2)
        return pltpu.make_async_copy(stage.at[slot], grads_hbm.at[:, cols], stage_sems.at[slot])

    def grad_unit(unit):
        slot = lax.rem(unit, 2)

        @pl.when(unit >= 2)
        def _():
            store(unit - 2).wait()

        for kind, (left, right) in enumerate(
            ((upstream_t, act), (normed_t, rights), (low_t, rights))
        ):
            first = 0 if kind == 0 else edges[1]

            @pl.when((unit >= edges[kind]) & (unit < edges[kind + 1]))
            def _(left=left, right=right, first=first):
                cols = pl.ds(pl.multiple_of((unit - first) * GRAD, GRAD), GRAD)

                def piece(p, carry):
                    rows = pl.ds(pl.multiple_of(p * SLAB, SLAB), SLAB)
                    stage[slot, rows, :] = mm(left[rows, :], right[:, cols]).astype(BF16)
                    return carry

                lax.fori_loop(0, width // SLAB, piece, 0)

        store(unit).start()

    send, drain, shift = scatter(
        length, peers, result, out_hbm, (send_sems, recv_sems, home_sems)
    )

    def work(s):
        on_shifted_groups(s, shift, length // STRIP, make)

        @pl.when(s < turns)
        def _():
            slot = lax.rem(s, 2)
            cols = pl.ds(pl.multiple_of(s * TURN, TURN), TURN)
            for kind in range(3):
                slice_load(kind, s).wait()
                turned[kind][:, cols] = slices[slot, kind].T

                @pl.when(s + 2 < turns)
                def _(kind=kind):
                    slice_load(kind, s + 2).start()

        @pl.when(s == turns)
        def _():
            for load in loads[3:]:
                load.wait()

        @pl.when((s >= turns) & (s < turns + units))
        def _():
            grad_unit(s - turns)

        @pl.when(s == 0)
        def _():
            loads[2].wait()

    def finish(strip, rows, total):
        result[rows, :] = (middle[rows, :].astype(F32) + total).astype(BF16)
        send(strip)
        stats_ref[0:1, :] += col_sum(total * total * valid[rows, :])

    line_sum(n, own, flows, work, finish, shift)
    drain()
    store(units - 2).wait()
    store(units - 1).wait()


def output_sum(
    n, peers, act, weights, middle, upstream, normed, low, dq, dk, dv, mixed, valid
):
    length, width = middle.shape
    feed = act.shape[1]
    rows = pltpu.VMEM((length, width), BF16)
    wide = pltpu.VMEM((length, feed), BF16)
    turned = pltpu.VMEM((width, length), BF16)
    return line_call(
        lambda count, *refs: output_kernel(count, peers, *refs),
        n,
        "output_sum",
        3,
        (act, weights, middle, upstream, normed, low, dq, dk, dv, mixed, valid),
        [ANY] * 10 + [VM],
        [
            jax.ShapeDtypeStruct((peers, length // peers, width), BF16),
            jax.ShapeDtypeStruct((8, width), F32),
            jax.ShapeDtypeStruct((width, feed + 4 * dq.shape[1]), BF16),
        ],
        [ANY, VM, ANY],
        [
            rows,
            wide,
            pltpu.VMEM((width, feed), BF16),
            rows,
            turned,
            turned,
            turned,
            pltpu.VMEM((length, 4 * dq.shape[1]), BF16),
            rows,
            pltpu.VMEM((2, 3, TURN, width), BF16),
            pltpu.VMEM((2, width, GRAD), BF16),
            pltpu.SemaphoreType.DMA((7,)),
            pltpu.SemaphoreType.DMA((2, 3)),
            pltpu.SemaphoreType.DMA((2,)),
        ]
        + scatter_scratch(length, peers)
        + flow_scratch(length, width),
        60_000_000_000,
    )


def input_kernel(
    n,
    peers,
    dq_ref,
    dk_ref,
    dv_ref,
    weight_hbm,
    source_hbm,
    back_hbm,
    gain,
    rows_ref,
    out_hbm,
    small_ref,
    weight,
    source,
    back,
    own,
    result,
    small_own,
    small_got,
    load_sems,
    small_send,
    small_recv,
    send_sems,
    recv_sems,
    home_sems,
    *flows,
):
    length, width = own.shape
    band = dq_ref.shape[1]
    mine = lax.axis_index("fsdp")
    share = width // peers
    strips = length // STRIP
    scatter_sems = (send_sems, recv_sems, home_sems)
    loads = [
        pltpu.make_async_copy(weight_hbm.at[:, pl.ds(0, 3 * band)], weight, load_sems.at[0]),
        pltpu.make_async_copy(source_hbm, source, load_sems.at[1]),
        pltpu.make_async_copy(back_hbm, back, load_sems.at[2]),
    ]
    for load in loads:
        load.start()
    greet(n, peers)
    small_own[...] = rows_ref[...]
    small_own[0:1, :] = jnp.zeros((1, width), F32)
    loads[0].wait()
    halves = [
        (lambda rows, ref=ref: ref[rows, :], lambda cols, k=k: weight[cols, k * band : (k + 1) * band])
        for k, ref in enumerate((dq_ref, dk_ref, dv_ref))
    ]
    send, drain, shift = scatter(length, peers, result, out_hbm, scatter_sems)

    def make(group):
        product_nt(own, wide_rows(group), halves)

    def work(s):
        on_shifted_groups(s, shift, strips, make)

        @pl.when(s == 0)
        def _():
            loads[1].wait()
            loads[2].wait()

    def finish(strip, rows, total):
        here = source[rows, :].astype(F32)
        scale = lax.rsqrt(row_mean(here * here) + EPS)
        scaled = total * gain[...]
        inner = row_mean(scaled * here)
        result[rows, :] = (
            back[rows, :].astype(F32) + scale * (scaled - here * (scale * scale * inner))
        ).astype(BF16)
        small_own[0:1, :] += col_sum(total * here * scale)

        send(strip)

    line_sum(n, own, flows, work, finish, shift)

    def small(ahead):
        peer = lax.rem(mine + ahead, peers)
        cols = pl.ds(pl.multiple_of(peer * share, share), share)
        return pltpu.make_async_remote_copy(
            src_ref=small_own.at[:, cols],
            dst_ref=small_got.at[mine],
            send_sem=small_send.at[ahead],
            recv_sem=small_recv.at[mine],
            device_id={"fsdp": peer},
            device_id_type=MESH,
        )

    for ahead in range(1, peers):
        small(ahead).start()
    total = small_own[:, pl.ds(pl.multiple_of(mine * share, share), share)]
    for ahead in range(1, peers):
        peer = lax.rem(mine + ahead, peers)
        pltpu.make_async_remote_copy(
            src_ref=small_own.at[:, pl.ds(0, share)],
            dst_ref=small_got.at[peer],
            send_sem=small_send.at[ahead],
            recv_sem=small_recv.at[peer],
            device_id={"fsdp": peer},
            device_id_type=MESH,
        ).wait_recv()
        total = total + small_got[peer]
        small(ahead).wait_send()
    drain()
    small_ref[...] = total


def input_sum(n, peers, dq, dk, dv, weights, source, back, gain, small_rows):
    length, width = source.shape
    band = dq.shape[1]
    rows = pltpu.VMEM((length, width), BF16)
    share = width // peers
    return line_call(
        lambda count, *refs: input_kernel(count, peers, *refs),
        n,
        "input_sum",
        4,
        (dq, dk, dv, weights, source, back, gain, small_rows),
        [VM, VM, VM, ANY, ANY, ANY, VM, VM],
        [
            jax.ShapeDtypeStruct((peers, length // peers, width), BF16),
            jax.ShapeDtypeStruct((8, share), F32),
        ],
        [ANY, VM],
        [
            pltpu.VMEM((width, 3 * band), BF16),
            rows,
            rows,
            rows,
            rows,
            pltpu.VMEM((8, width), F32),
            pltpu.VMEM((peers, 8, share), F32),
            pltpu.SemaphoreType.DMA((3,)),
            pltpu.SemaphoreType.DMA((peers,)),
            pltpu.SemaphoreType.DMA((peers,)),
        ]
        + scatter_scratch(length, peers)
        + flow_scratch(length, width),
        50_000_000_000,
    )
def per_device(
    mesh_sizes,
    inputs,
    cotangent,
    piece_start,
    piece_image,
    valid_mask,
    query_weight,
    key_weight,
    value_weight,
    output_weight,
    attn_gain,
    gate_weight,
    up_weight,
    down_weight,
    mlp_gain,
):
    spread, line = mesh_sizes
    seqs, local, width = inputs.shape
    length = valid_mask.shape[1]
    band = query_weight.shape[1]
    feed = gate_weight.shape[1]
    mine = lax.axis_index("fsdp")

    def swap(values):
        return lax.all_to_all(values, "fsdp", split_axis=0, concat_axis=0, tiled=True)

    def shares(terms):
        return lax.psum_scatter(terms, "fsdp", scatter_dimension=0, tiled=True)

    gains = lax.all_gather(jnp.stack([attn_gain, mlp_gain]), "fsdp", axis=1, tiled=True)
    gains, inputs = lax.optimization_barrier((gains, inputs))
    gains = gains.astype(F32)
    attn_g, mlp_g = gains[0:1], gains[1:2]
    attn_w = lax.all_gather(
        jnp.concatenate([query_weight, key_weight, value_weight, output_weight.T], axis=1),
        "fsdp",
        axis=0,
        tiled=True,
    )
    mlp_w = lax.all_gather(
        jnp.concatenate([gate_weight, up_weight, down_weight.T], axis=1),
        "fsdp",
        axis=0,
        tiled=True,
    )
    source = swap(inputs).reshape(length, width)
    source, cotangent = lax.optimization_barrier((source, cotangent))
    upstream = swap(cotangent).reshape(length, width)

    places = jnp.arange(length, dtype=jnp.int32)
    cosine, sine = rope_tables(places, HD)
    signs = jnp.where(jnp.arange(HD) < HD // 2, -1.0, 1.0).astype(F32)
    cosine = jnp.concatenate([cosine, cosine], axis=1)
    sine = jnp.concatenate([sine * signs, sine * signs], axis=1)
    valid_row = lax.dynamic_index_in_dim(valid_mask, mine, 0, keepdims=False)
    valid = valid_row.astype(F32)[:, None]
    bias = jnp.where(valid_row > 0, 0.0, NEG).astype(F32)[:, None]
    starts = lax.dynamic_index_in_dim(piece_start, mine, 0, keepdims=False)
    images = lax.dynamic_index_in_dim(piece_image, mine, 0, keepdims=False)
    image = image_of(jnp.arange(length // TILE, dtype=jnp.int32) * TILE, starts, images).astype(
        jnp.int32
    )

    residual = source.astype(F32)
    scale_one = lax.rsqrt(jnp.mean(residual * residual, axis=1, keepdims=True) + EPS)
    normed_one = (residual * scale_one * attn_g).astype(BF16)
    qkv = mm(normed_one, attn_w[:, : 3 * band])
    queries, keys, values, mixed, lse = attend(qkv, cosine, sine, bias, image)
    middle, normed_two, stats = middle_sum(line, mixed, attn_w, source, mlp_g, valid)
    act, _, _, front_terms, middle_low, mlp_gain_sum = mlp_sum(
        line, normed_two, upstream, middle, mlp_g, mlp_w
    )
    front_grads = shares(front_terms)
    mixed_back = mm(middle_low, attn_w[:, 3 * band :]).astype(BF16)
    dq, dk, dv = attend_back(
        queries, keys, values, mixed_back, mixed, lse, cosine, sine, bias, image
    )
    output, mlp_stats, late_terms = output_sum(
        line,
        spread,
        act,
        mlp_w,
        middle,
        upstream,
        normed_one,
        middle_low,
        dq,
        dk,
        dv,
        mixed,
        valid,
    )
    late_terms, front_grads = lax.optimization_barrier((late_terms, front_grads))
    late_grads = shares(late_terms)
    sums = jnp.stack([jnp.sum(stats[0]), jnp.sum(stats[1]), jnp.sum(mlp_stats[0])])
    small_rows = jnp.concatenate(
        [
            jnp.zeros((1, width), F32),
            mlp_gain_sum[0:1],
            jnp.broadcast_to(sums[:, None], (3, width)),
            jnp.zeros((3, width), F32),
        ]
    )
    input_grad, small = input_sum(
        line, spread, dq, dk, dv, attn_w, source, middle_low, attn_g, small_rows
    )
    late_grads = late_grads.astype(F32)
    attn_grads = late_grads[:, feed:]
    count = jnp.sum(valid_mask).astype(F32) * width
    roots = jnp.sqrt(small[2:5, 0] / count)
    return (
        output,
        input_grad,
        attn_grads[:, :band],
        attn_grads[:, band : 2 * band],
        attn_grads[:, 2 * band : 3 * band],
        attn_grads[:, 3 * band :].T,
        small[0],
        front_grads[:, :feed].astype(F32),
        front_grads[:, feed:].astype(F32),
        late_grads[:, :feed].T,
        small[1],
        roots[0],
        roots[1],
        roots[2],
    )


def solution(mesh):
    placed = (
        P(None, "fsdp", None),
        P(None, "fsdp", None),
        P(),
        P(),
        P(),
        P("fsdp", "dp"),
        P("fsdp", "dp"),
        P("fsdp", "dp"),
        P("dp", "fsdp"),
        P("fsdp"),
        P("fsdp", "dp"),
        P("fsdp", "dp"),
        P("dp", "fsdp"),
        P("fsdp"),
    )
    spread, line = mesh.shape["fsdp"], mesh.shape["dp"]

    def whole(*arrays):
        seqs, length, _ = arrays[0].shape
        own_sequence = seqs == spread and length % (2 * TILE) == 0 and line > 1
        each = functools.partial(per_device, (spread, line)) if own_sequence else per_device_gather
        return jax.shard_map(
            each,
            mesh=mesh,
            in_specs=placed,
            out_specs=(
                P(None, "fsdp", None),
                P(None, "fsdp", None),
                P("fsdp", "dp"),
                P("fsdp", "dp"),
                P("fsdp", "dp"),
                P("dp", "fsdp"),
                P("fsdp"),
                P("fsdp", "dp"),
                P("fsdp", "dp"),
                P("dp", "fsdp"),
                P("fsdp"),
                P(),
                P(),
                P(),
            ),
            check_vma=False,
        )(*arrays)

    return whole
```

```python
import functools

import jax
import jax.numpy as jnp
from jax import lax
from jax.experimental import pallas as pl
from jax.experimental.pallas import tpu as pltpu
from jax.sharding import PartitionSpec as P


HD = 64
PIECE = 256


EPS = 1e-05
THETA = 130000.0
NEG = -1e30


def rope_tables(positions, head_size):
    half = head_size // 2
    rates = THETA ** (-(jnp.arange(half, dtype=jnp.float32) * 2.0 / head_size))
    angle = positions.astype(jnp.float32)[:, None] * rates[None, :]
    cosine = jnp.concatenate([jnp.cos(angle), jnp.cos(angle)], axis=-1)
    sine = jnp.concatenate([jnp.sin(angle), jnp.sin(angle)], axis=-1)
    return (cosine, sine)


def rotate(values, cosine, sine):
    half = values.shape[-1] // 2
    turned = jnp.concatenate([-values[..., half:], values[..., :half]], axis=-1)
    return values * cosine[:, None, :] + turned * sine[:, None, :]


def unrotate(grads, cosine, sine):
    half = grads.shape[-1] // 2
    scaled = grads * sine[:, None, :]
    turned = jnp.concatenate([scaled[..., half:], -scaled[..., :half]], axis=-1)
    return grads * cosine[:, None, :] + turned


def image_of(positions, starts, images):
    inside = (positions[:, None] >= starts[None, :]) & (
        positions[:, None] < starts[None, :] + PIECE
    )
    return jnp.sum(jnp.where(inside, images[None, :] + 1, 0), axis=1) - 1


def allowed_mask(query_pos, key_pos, query_image, key_image, key_valid):
    causal = key_pos[None, :] <= query_pos[:, None]
    same = (query_image[:, None] >= 0) & (query_image[:, None] == key_image[None, :])
    return (causal | same) & (key_valid[None, :] > 0)


def project(values, weight):
    return jnp.einsum("std,de->ste", values, weight, preferred_element_type=jnp.float32)


def project_back(grads, weight):
    return jnp.einsum("ste,de->std", grads, weight, preferred_element_type=jnp.float32)


def weight_term(values, grads):
    return jnp.einsum("std,ste->de", values, grads, preferred_element_type=jnp.float32)


def masked_scores(queries, key_heads, allowed):
    raw = jnp.einsum(
        "qhd,khd->hqk", queries, key_heads, preferred_element_type=jnp.float32
    ) * HD ** (-0.5)
    return jnp.where(allowed[None, :, :], raw, NEG)


def norm_back(grad, source, scale, gain):
    scaled = grad * gain.astype(jnp.float32)
    inner = jnp.mean(scaled * source, axis=2, keepdims=True)
    return scale * (scaled - source * scale * scale * inner)


def blocked(step, items):
    total = items[0].shape[0]
    block_size = max((candidate for candidate in range(1, 9) if total % candidate == 0))
    groups = total // block_size
    shaped = tuple((item.reshape((groups, block_size) + item.shape[1:]) for item in items))
    results = lax.map(lambda group: jax.vmap(step)(*group), shaped)
    return jax.tree.map(
        lambda result: result.reshape((groups * block_size,) + result.shape[2:]), results
    )


def per_device_gather(
    inputs,
    cotangent,
    piece_start,
    piece_image,
    valid_mask,
    query_weight,
    key_weight,
    value_weight,
    output_weight,
    attn_gain,
    gate_weight,
    up_weight,
    down_weight,
    mlp_gain,
):
    seqs, local, width = inputs.shape
    length = valid_mask.shape[1]
    band = query_weight.shape[1]
    heads_here = band // HD
    offset = lax.axis_index("fsdp") * local
    positions = offset + jnp.arange(local, dtype=jnp.int32)
    key_places = jnp.arange(length, dtype=jnp.int32)
    cosine, sine = rope_tables(positions, HD)
    local_valid = lax.dynamic_slice_in_dim(valid_mask, offset, local, 1).astype(jnp.float32)

    def sequence_mask(starts, images, valid_row):
        query_image = image_of(positions, starts, images)
        key_image = image_of(key_places, starts, images)
        return allowed_mask(positions, key_places, query_image, key_image, valid_row)

    attn_set = (
        lax.all_gather(query_weight, "fsdp", axis=0, tiled=True),
        lax.all_gather(key_weight, "fsdp", axis=0, tiled=True),
        lax.all_gather(value_weight, "fsdp", axis=0, tiled=True),
        lax.all_gather(output_weight, "fsdp", axis=1, tiled=True),
        lax.all_gather(attn_gain, "fsdp", axis=0, tiled=True),
    )
    residual = inputs.astype(jnp.float32)
    scale_one = lax.rsqrt(jnp.mean(residual * residual, axis=2, keepdims=True) + EPS)
    normed_one = (residual * scale_one * attn_set[4].astype(jnp.float32)).astype(jnp.bfloat16)
    queries = rotate(
        project(normed_one, attn_set[0]).reshape(seqs, local, heads_here, HD), cosine, sine
    ).astype(jnp.bfloat16)
    keys_here = (
        rotate(project(normed_one, attn_set[1]).reshape(seqs, local, heads_here, HD), cosine, sine)
        .astype(jnp.bfloat16)
        .reshape(seqs, local, band)
    )
    values_here = project(normed_one, attn_set[2]).astype(jnp.bfloat16)
    keys_all, values_all = (
        lax.all_gather(keys_here, "fsdp", axis=1, tiled=True),
        lax.all_gather(values_here, "fsdp", axis=1, tiled=True),
    )

    def attend(query_one, key_one, value_one, starts, images, valid_row):
        allowed = sequence_mask(starts, images, valid_row)
        scores = masked_scores(query_one, key_one.reshape(length, heads_here, HD), allowed)
        highest = jnp.max(scores, axis=2, keepdims=True)
        log_total = highest + jnp.log(jnp.sum(jnp.exp(scores - highest), axis=2, keepdims=True))
        probs = jnp.exp(scores - log_total).astype(jnp.bfloat16)
        mixed_one = jnp.einsum(
            "hqk,khd->qhd",
            probs,
            value_one.reshape(length, heads_here, HD),
            preferred_element_type=jnp.float32,
        )
        return (mixed_one.reshape(local, band).astype(jnp.bfloat16), log_total)

    mixed, log_totals = blocked(
        attend, (queries, keys_all, values_all, piece_start, piece_image, valid_mask)
    )
    attn_out = lax.psum(project(mixed, attn_set[3]).astype(jnp.bfloat16), "dp").astype(jnp.float32)
    middle = residual + attn_out
    scale_two = lax.rsqrt(jnp.mean(middle * middle, axis=2, keepdims=True) + EPS)
    mlp_set = (
        lax.all_gather(gate_weight, "fsdp", axis=0, tiled=True),
        lax.all_gather(up_weight, "fsdp", axis=0, tiled=True),
        lax.all_gather(down_weight, "fsdp", axis=1, tiled=True),
        lax.all_gather(mlp_gain, "fsdp", axis=0, tiled=True),
    )
    normed_two = (middle * scale_two * mlp_set[3].astype(jnp.float32)).astype(jnp.bfloat16)
    gate = project(normed_two, mlp_set[0])
    up = project(normed_two, mlp_set[1])
    sigmoid_gate = jax.nn.sigmoid(gate)
    activated = (gate * sigmoid_gate * up).astype(jnp.bfloat16)
    mlp_out = lax.psum(project(activated, mlp_set[2]).astype(jnp.bfloat16), "dp").astype(
        jnp.float32
    )
    output = (middle + mlp_out).astype(jnp.bfloat16)
    row_weight = local_valid[:, :, None]
    totals = lax.psum(
        (
            jnp.sum(middle * middle * row_weight),
            jnp.sum(attn_out * attn_out * row_weight),
            jnp.sum(mlp_out * mlp_out * row_weight),
        ),
        "fsdp",
    )
    count = jnp.sum(valid_mask).astype(jnp.float32) * width
    mlp_back = (
        lax.all_gather(gate_weight, "fsdp", axis=0, tiled=True),
        lax.all_gather(up_weight, "fsdp", axis=0, tiled=True),
        lax.all_gather(down_weight, "fsdp", axis=1, tiled=True),
        lax.all_gather(mlp_gain, "fsdp", axis=0, tiled=True),
    )
    upstream = cotangent.astype(jnp.float32)
    act_grad = project_back(cotangent, mlp_back[2])
    gate_back = (
        act_grad * up * (sigmoid_gate + gate * sigmoid_gate * (1.0 - sigmoid_gate))
    ).astype(jnp.bfloat16)
    up_back = (act_grad * gate * sigmoid_gate).astype(jnp.bfloat16)
    normed_two_back = lax.psum(
        (project_back(gate_back, mlp_back[0]) + project_back(up_back, mlp_back[1])).astype(
            jnp.bfloat16
        ),
        "dp",
    ).astype(jnp.float32)
    middle_back = upstream + norm_back(normed_two_back, middle, scale_two, mlp_back[3])
    mlp_gain_term = jnp.sum(normed_two_back * middle * scale_two, axis=(0, 1))
    mlp_parts = lax.psum_scatter(
        jnp.concatenate(
            [
                weight_term(normed_two, gate_back),
                weight_term(normed_two, up_back),
                weight_term(cotangent, activated),
            ],
            axis=1,
        ).astype(jnp.bfloat16),
        "fsdp",
        scatter_dimension=0,
        tiled=True,
    ).astype(jnp.float32)
    feed = gate_weight.shape[1]
    gate_part = mlp_parts[:, :feed]
    up_part = mlp_parts[:, feed : 2 * feed]
    down_part = mlp_parts[:, 2 * feed :].T
    attn_back = (
        lax.all_gather(query_weight, "fsdp", axis=0, tiled=True),
        lax.all_gather(key_weight, "fsdp", axis=0, tiled=True),
        lax.all_gather(value_weight, "fsdp", axis=0, tiled=True),
        lax.all_gather(output_weight, "fsdp", axis=1, tiled=True),
        lax.all_gather(attn_gain, "fsdp", axis=0, tiled=True),
    )
    middle_low = middle_back.astype(jnp.bfloat16)
    mixed_back = project_back(middle_low, attn_back[3]).astype(jnp.bfloat16)

    def query_grads(query_one, key_heads, value_heads, grad_heads, log_total, allowed):
        scores = masked_scores(query_one, key_heads, allowed)
        weights = jnp.exp(scores - log_total)
        prob_back = jnp.einsum(
            "qhd,khd->hqk", grad_heads, value_heads, preferred_element_type=jnp.float32
        )
        inner = jnp.sum(weights * prob_back, axis=2, keepdims=True)
        score_back = (weights * (prob_back - inner)).astype(jnp.bfloat16)
        query_back = jnp.einsum(
            "hqk,khd->qhd", score_back, key_heads, preferred_element_type=jnp.float32
        ) * HD ** (-0.5)
        return (query_back, weights, score_back, inner)

    def attend_back(query_one, key_one, value_one, grad_one, log_total, starts, images, valid_row):
        allowed = sequence_mask(starts, images, valid_row)
        grad_heads = grad_one.reshape(local, heads_here, HD)
        query_back, weights, score_back, inner = query_grads(
            query_one,
            key_one.reshape(length, heads_here, HD),
            value_one.reshape(length, heads_here, HD),
            grad_heads,
            log_total,
            allowed,
        )
        key_back = jnp.einsum(
            "hqk,qhd->khd", score_back, query_one, preferred_element_type=jnp.float32
        ) * HD ** (-0.5)
        value_back = jnp.einsum(
            "hqk,qhd->khd",
            weights.astype(jnp.bfloat16),
            grad_heads,
            preferred_element_type=jnp.float32,
        )
        return (query_back, key_back.reshape(length, band), value_back.reshape(length, band))

    query_backs, key_parts, value_parts = blocked(
        attend_back,
        (
            queries,
            keys_all,
            values_all,
            mixed_back,
            log_totals,
            piece_start,
            piece_image,
            valid_mask,
        ),
    )
    key_backs, value_backs = (
        lax.psum_scatter(
            key_parts.astype(jnp.bfloat16), "fsdp", scatter_dimension=1, tiled=True
        ).astype(jnp.float32),
        lax.psum_scatter(
            value_parts.astype(jnp.bfloat16), "fsdp", scatter_dimension=1, tiled=True
        ).astype(jnp.float32),
    )
    query_low = unrotate(query_backs, cosine, sine).reshape(seqs, local, band).astype(jnp.bfloat16)
    key_low = (
        unrotate(key_backs.reshape(seqs, local, heads_here, HD), cosine, sine)
        .reshape(seqs, local, band)
        .astype(jnp.bfloat16)
    )
    value_low = value_backs.astype(jnp.bfloat16)
    partial_back = (
        project_back(query_low, attn_back[0])
        + project_back(key_low, attn_back[1])
        + project_back(value_low, attn_back[2])
    )
    normed_one_back = lax.psum(partial_back.astype(jnp.bfloat16), "dp").astype(jnp.float32)
    input_grad = (
        middle_back + norm_back(normed_one_back, residual, scale_one, attn_back[4])
    ).astype(jnp.bfloat16)
    query_part, key_part, value_part, output_term, attn_gain_part, mlp_gain_part = (
        lax.psum_scatter(
            weight_term(normed_one, query_low).astype(jnp.bfloat16),
            "fsdp",
            scatter_dimension=0,
            tiled=True,
        ).astype(jnp.float32),
        lax.psum_scatter(
            weight_term(normed_one, key_low).astype(jnp.bfloat16),
            "fsdp",
            scatter_dimension=0,
            tiled=True,
        ).astype(jnp.float32),
        lax.psum_scatter(
            weight_term(normed_one, value_low).astype(jnp.bfloat16),
            "fsdp",
            scatter_dimension=0,
            tiled=True,
        ).astype(jnp.float32),
        lax.psum_scatter(
            weight_term(middle_low, mixed).astype(jnp.bfloat16),
            "fsdp",
            scatter_dimension=0,
            tiled=True,
        ).astype(jnp.float32),
        lax.psum_scatter(
            jnp.sum(normed_one_back * residual * scale_one, axis=(0, 1)).astype(jnp.bfloat16),
            "fsdp",
            scatter_dimension=0,
            tiled=True,
        ).astype(jnp.float32),
        lax.psum_scatter(
            mlp_gain_term.astype(jnp.bfloat16), "fsdp", scatter_dimension=0, tiled=True
        ).astype(jnp.float32),
    )
    output_part = output_term.T
    return (
        output,
        input_grad,
        query_part,
        key_part,
        value_part,
        output_part,
        attn_gain_part,
        gate_part,
        up_part,
        down_part,
        mlp_gain_part,
        jnp.sqrt(totals[0] / count),
        jnp.sqrt(totals[1] / count),
        jnp.sqrt(totals[2] / count),
    )


VMEM_MOST = 66_000_000
MESH = pl.DeviceIdType.MESH
BF16 = jnp.bfloat16
F32 = jnp.float32
PAIR = 2 * HD
TILE = 256
STRIP = 32
SLAB = 512
HOP = 2

NT = (((1,), (1,)), ((), ()))
TN = (((0,), (0,)), ((), ()))


def mm(a, b):
    return jnp.dot(a, b, preferred_element_type=F32)


def mm_nt(a, b):
    return lax.dot_general(a, b, NT, preferred_element_type=F32)


def mm_tn(a, b):
    return lax.dot_general(a, b, TN, preferred_element_type=F32)


def half_swap(values):
    lane = lax.broadcasted_iota(jnp.int32, values.shape, 1) % HD
    ahead = pltpu.roll(values, PAIR - HD // 2, 1)
    behind = pltpu.roll(values, HD // 2, 1)
    return jnp.where(lane < HD // 2, ahead, behind)


def head_lanes(values, head):
    lane = lax.broadcasted_iota(jnp.int32, values.shape, 1) // HD
    return jnp.where(lane == head, values, jnp.zeros_like(values))


def diagonal_bias(is_piece):
    key = lax.broadcasted_iota(jnp.int32, (TILE, TILE), 0)
    query = lax.broadcasted_iota(jnp.int32, (TILE, TILE), 1)
    return jnp.where((key <= query) | is_piece, 0.0, NEG).astype(F32)


def attend_kernel(
    image_ref,
    q_in,
    k_in,
    v_in,
    cos_ref,
    sin_ref,
    bias_ref,
    q_ref,
    k_ref,
    v_ref,
    mixed_ref,
    lse_ref,
    top,
    total,
    acc,
    outs,
):
    length = q_in.shape[0]
    tiles = length // TILE
    cosine, sine = cos_ref[...], sin_ref[...]
    raw = q_in[...]
    q_ref[...] = ((raw * cosine + half_swap(raw) * sine) * HD ** (-0.5)).astype(BF16)
    raw = k_in[...]
    k_ref[...] = (raw * cosine + half_swap(raw) * sine).astype(BF16)
    v_ref[...] = v_in[...].astype(BF16)
    lse_ref[...] = jnp.zeros_like(lse_ref)
    for tile in range(tiles):
        here = slice(tile * TILE, (tile + 1) * TILE)
        upto = (tile + 1) * TILE
        corner = diagonal_bias(image_ref[tile] >= 0)
        for head in range(2):
            query = head_lanes(q_ref[here, :], head)
            scores = mm_nt(k_ref[:upto, :], query) + bias_ref[:upto, :]
            diag = scores[upto - TILE :, :] + corner
            highest = jnp.max(diag, axis=0, keepdims=True)
            if tile:
                before = scores[: upto - TILE, :]
                highest = jnp.maximum(highest, jnp.max(before, axis=0, keepdims=True))
                weight_low = jnp.exp(before - highest)
                weight_diag = jnp.exp(diag - highest)
                summed = jnp.sum(weight_low, axis=0, keepdims=True) + jnp.sum(
                    weight_diag, axis=0, keepdims=True
                )
                mixed = mm_tn(v_ref[: upto - TILE, :], weight_low.astype(BF16)) + mm_tn(
                    v_ref[upto - TILE : upto, :], weight_diag.astype(BF16)
                )
            else:
                weight_diag = jnp.exp(diag - highest)
                summed = jnp.sum(weight_diag, axis=0, keepdims=True)
                mixed = mm_tn(v_ref[:upto, :], weight_diag.astype(BF16))
            top[...] = highest
            total[...] = summed
            acc[...] = mixed
            for other in range(tile + 1, tiles):

                @pl.when((image_ref[tile] >= 0) & (image_ref[tile] == image_ref[other]))
                def _(other=other, query=query):
                    there = slice(other * TILE, (other + 1) * TILE)
                    extra = mm_nt(k_ref[there, :], query) + bias_ref[there, :]
                    newest = jnp.maximum(top[...], jnp.max(extra, axis=0, keepdims=True))
                    shrink = jnp.exp(top[...] - newest)
                    weight = jnp.exp(extra - newest)
                    total[...] = total[...] * shrink + jnp.sum(weight, axis=0, keepdims=True)
                    acc[...] = acc[...] * shrink + mm_tn(v_ref[there, :], weight.astype(BF16))
                    top[...] = newest

            rows = slice(head * HD, (head + 1) * HD)
            outs[rows, :] = acc[rows, :] / total[...]
            lse_ref[0, head : head + 1, here] = top[...] + jnp.log(total[...])
        mixed_ref[here, :] = outs[...].T.astype(BF16)


def attend(qkv, cosine, sine, bias, image):
    length, wide = qkv.shape
    band = wide // 3
    pairs = band // PAIR
    column = lambda shift: pl.BlockSpec((length, PAIR), lambda g, img: (0, g + shift))
    fixed = lambda cols: pl.BlockSpec((length, cols), lambda g, img: (0, 0))
    low = jax.ShapeDtypeStruct((length, band), BF16)
    return pl.pallas_call(
        attend_kernel,
        grid_spec=pltpu.PrefetchScalarGridSpec(
            num_scalar_prefetch=1,
            grid=(pairs,),
            in_specs=[
                column(0),
                column(pairs),
                column(2 * pairs),
                fixed(PAIR),
                fixed(PAIR),
                fixed(1),
            ],
            out_specs=[column(0)] * 4 + [pl.BlockSpec((1, 8, length), lambda g, img: (g, 0, 0))],
            scratch_shapes=[
                pltpu.VMEM((1, TILE), F32),
                pltpu.VMEM((1, TILE), F32),
                pltpu.VMEM((PAIR, TILE), F32),
                pltpu.VMEM((PAIR, TILE), F32),
            ],
        ),
        out_shape=[low] * 4 + [jax.ShapeDtypeStruct((pairs, 8, length), F32)],
        compiler_params=pltpu.CompilerParams(vmem_limit_bytes=VMEM_MOST),
        cost_estimate=pl.CostEstimate(
            flops=12_000_000_000, bytes_accessed=12_000_000, transcendentals=6_000_000
        ),
        name="attend",
    )(image, qkv, qkv, qkv, cosine, sine, bias)


def attend_back_kernel(
    image_ref,
    q_ref,
    k_ref,
    v_ref,
    g_ref,
    mixed_ref,
    lse_ref,
    cos_ref,
    sin_ref,
    bias_ref,
    dq_ref,
    dk_ref,
    dv_ref,
    dk_acc,
    dv_acc,
    dq_acc,
):
    length = q_ref.shape[0]
    tiles = length // TILE
    dk_acc[...] = jnp.zeros_like(dk_acc)
    dv_acc[...] = jnp.zeros_like(dv_acc)
    pick_row = lax.broadcasted_iota(jnp.int32, (8, PAIR), 0)
    pick_lane = lax.broadcasted_iota(jnp.int32, (8, PAIR), 1) // HD
    picker = (pick_row == pick_lane).astype(F32)
    for tile in range(tiles):
        here = slice(tile * TILE, (tile + 1) * TILE)
        corner = diagonal_bias(image_ref[tile] >= 0)
        product = mixed_ref[here, :].astype(F32) * g_ref[here, :].astype(F32)
        inners = lax.dot_general(
            picker, product, NT, precision=lax.Precision.HIGHEST, preferred_element_type=F32
        )
        for head in range(2):
            query = head_lanes(q_ref[here, :], head)
            grad = head_lanes(g_ref[here, :], head)
            inner = inners[head : head + 1, :]
            lse = lse_ref[0, head : head + 1, here]
            rows = slice(head * HD, (head + 1) * HD)

            def block(there, extra, first):
                scores = mm_nt(k_ref[there, :], query) + bias_ref[there, :]
                if extra is not None:
                    scores = scores + extra
                weight = jnp.exp(scores - lse)
                back = mm_nt(v_ref[there, :], grad)
                score_back = (weight * (back - inner)).astype(BF16)
                dv_acc[there, :] += mm(weight.astype(BF16), grad)
                dk_acc[there, :] += mm(score_back, query)
                part = mm_tn(k_ref[there, :], score_back)
                if first:
                    dq_acc[rows, :] = part[rows, :]
                else:
                    dq_acc[rows, :] += part[rows, :]

            block(here, corner, True)
            for other in range(tile):
                block(slice(other * TILE, (other + 1) * TILE), None, False)
            for other in range(tile + 1, tiles):

                @pl.when((image_ref[tile] >= 0) & (image_ref[tile] == image_ref[other]))
                def _(other=other):
                    block(slice(other * TILE, (other + 1) * TILE), None, False)

        turned = dq_acc[...].T * HD ** (-0.5)
        dq_ref[here, :] = (
            turned * cos_ref[here, :] - half_swap(turned) * sin_ref[here, :]
        ).astype(BF16)
    turned = dk_acc[...]
    dk_ref[...] = (turned * cos_ref[...] - half_swap(turned) * sin_ref[...]).astype(BF16)
    dv_ref[...] = dv_acc[...].astype(BF16)


def attend_back(queries, keys, values, grads, mixed, lse, cosine, sine, bias, image):
    length, band = queries.shape
    pairs = band // PAIR
    column = pl.BlockSpec((length, PAIR), lambda g, img: (0, g))
    fixed = lambda cols: pl.BlockSpec((length, cols), lambda g, img: (0, 0))
    low = jax.ShapeDtypeStruct((length, band), BF16)
    return pl.pallas_call(
        attend_back_kernel,
        grid_spec=pltpu.PrefetchScalarGridSpec(
            num_scalar_prefetch=1,
            grid=(pairs,),
            in_specs=[column] * 5
            + [
                pl.BlockSpec((1, 8, length), lambda g, img: (g, 0, 0)),
                fixed(PAIR),
                fixed(PAIR),
                fixed(1),
            ],
            out_specs=[column] * 3,
            scratch_shapes=[
                pltpu.VMEM((length, PAIR), F32),
                pltpu.VMEM((length, PAIR), F32),
                pltpu.VMEM((PAIR, TILE), F32),
            ],
        ),
        out_shape=[low] * 3,
        compiler_params=pltpu.CompilerParams(vmem_limit_bytes=VMEM_MOST),
        cost_estimate=pl.CostEstimate(
            flops=30_000_000_000, bytes_accessed=12_000_000, transcendentals=6_000_000
        ),
        name="attend_back",
    )(image, queries, keys, values, grads, mixed, lse, cosine, sine, bias)


VM = pl.BlockSpec(memory_space=pltpu.VMEM)
ANY = pl.BlockSpec(memory_space=pl.ANY)


def row_mean(values):
    return jnp.mean(values, axis=1, keepdims=True)


def col_sum(values):
    return jnp.sum(values, axis=0, keepdims=True)


def greet(n, peers=0):
    rank = lax.axis_index("dp")
    has_low, has_high = rank > 0, rank < n - 1
    barrier = pltpu.get_barrier_semaphore()

    @pl.when(has_low)
    def _():
        pl.semaphore_signal(
            barrier, inc=1, device_id={"dp": lax.rem(rank + n - 1, n)}, device_id_type=MESH
        )

    @pl.when(has_high)
    def _():
        pl.semaphore_signal(
            barrier, inc=1, device_id={"dp": lax.rem(rank + 1, n)}, device_id_type=MESH
        )

    mine = lax.axis_index("fsdp")
    for ahead in range(1, peers):
        pl.semaphore_signal(
            barrier, inc=1, device_id={"fsdp": lax.rem(mine + ahead, peers)}, device_id_type=MESH
        )
    both = has_low.astype(jnp.int32) + has_high.astype(jnp.int32)
    pl.semaphore_wait(barrier, both + max(peers - 1, 0))


def line_sum(n, own, flows, work, finish, shift=0):
    prefix, suffix, sems = flows
    send_high, send_low, got_low, got_high = (sems.at[k] for k in range(4))
    rank = lax.axis_index("dp")
    strips = own.shape[0] // STRIP
    has_low, has_high = rank > 0, rank < n - 1
    higher, lower = lax.rem(rank + 1, n), lax.rem(rank + n - 1, n)

    def rows_of(strip):
        at = strip if isinstance(shift, int) else lax.rem(strip + shift, strips)
        return pl.ds(pl.multiple_of(at * STRIP, STRIP), STRIP)

    def up(strip):
        rows = rows_of(strip)
        return pltpu.make_async_remote_copy(
            src_ref=prefix.at[rows],
            dst_ref=prefix.at[rows],
            send_sem=send_high.at[strip],
            recv_sem=got_low.at[strip],
            device_id={"dp": higher},
            device_id_type=MESH,
        )

    def down(strip):
        rows = rows_of(strip)
        return pltpu.make_async_remote_copy(
            src_ref=suffix.at[rows],
            dst_ref=suffix.at[rows],
            send_sem=send_low.at[strip],
            recv_sem=got_high.at[strip],
            device_id={"dp": lower},
            device_id_type=MESH,
        )

    late = jnp.maximum(rank, n - 1 - rank)

    def step(s, carry):
        work(s)
        a = s - rank * HOP

        @pl.when((a >= 0) & (a < strips))
        def _():
            rows = rows_of(a)

            @pl.when(has_low)
            def _():
                up(a).wait_recv()
                prefix[rows, :] = (
                    own[rows, :].astype(F32) + prefix[rows, :].astype(F32)
                ).astype(BF16)

            @pl.when(jnp.logical_not(has_low))
            def _():
                prefix[rows, :] = own[rows, :]

            @pl.when(has_high)
            def _():
                up(a).start()

        b = s - (n - 1 - rank) * HOP

        @pl.when((b >= 0) & (b < strips))
        def _():
            rows = rows_of(b)

            @pl.when(has_high)
            def _():
                down(b).wait_recv()
                suffix[rows, :] = (
                    own[rows, :].astype(F32) + suffix[rows, :].astype(F32)
                ).astype(BF16)

            @pl.when(jnp.logical_not(has_high))
            def _():
                suffix[rows, :] = own[rows, :]

            @pl.when(has_low)
            def _():
                down(b).start()

        c = s - late * HOP

        @pl.when((c >= 0) & (c < strips))
        def _():
            rows = rows_of(c)
            finish(
                c,
                rows,
                prefix[rows, :].astype(F32)
                + suffix[rows, :].astype(F32)
                - own[rows, :].astype(F32),
            )

        return carry

    lax.fori_loop(0, strips + (n - 1) * HOP, step, 0)

    def drain(s, carry):
        @pl.when(has_high)
        def _():
            up(s).wait_send()

        @pl.when(has_low)
        def _():
            down(s).wait_send()

        return carry

    lax.fori_loop(0, strips, drain, 0)


def flow_scratch(length, width):
    whole = pltpu.VMEM((length, width), BF16)
    return [whole] * 2 + [pltpu.SemaphoreType.DMA((4, length // STRIP))]


def line_call(kernel, n, name, collective_id, args, specs, outs, out_specs, scratch, flops):
    return pl.pallas_call(
        functools.partial(kernel, n),
        in_specs=specs,
        out_specs=out_specs,
        out_shape=outs,
        scratch_shapes=scratch,
        compiler_params=pltpu.CompilerParams(
            collective_id=collective_id, has_side_effects=True, vmem_limit_bytes=VMEM_MOST
        ),
        cost_estimate=pl.CostEstimate(
            flops=flops, bytes_accessed=300_000_000, transcendentals=0
        ),
        name=name,
    )(*args)


def wide_rows(group):
    return pl.ds(pl.multiple_of(group * TILE, TILE), TILE)


def product_nt(own, rows, pairs):
    width = own.shape[1]

    def piece(p, carry):
        cols = pl.ds(pl.multiple_of(p * SLAB, SLAB), SLAB)
        total = None
        for left, right in pairs:
            term = mm_nt(left(rows), right(cols))
            total = term if total is None else total + term
        own[rows, cols] = total.astype(BF16)
        return carry

    lax.fori_loop(0, width // SLAB, piece, 0)


def on_groups(s, length, make):
    per = TILE // STRIP

    @pl.when((lax.rem(s, per) == 0) & (s < length // STRIP))
    def _():
        make(lax.div(s, per))


def middle_kernel(
    n,
    mixed_ref,
    out_weight,
    source_hbm,
    gain,
    valid,
    middle_ref,
    normed_ref,
    stats_ref,
    weight,
    source,
    own,
    load_sems,
    *flows,
):
    band = weight.shape[1]
    length = own.shape[0]
    loads = [
        pltpu.make_async_copy(
            out_weight.at[:, pl.ds(out_weight.shape[1] - band, band)], weight, load_sems.at[0]
        ),
        pltpu.make_async_copy(source_hbm, source, load_sems.at[1]),
    ]
    for load in loads:
        load.start()
    greet(n)
    stats_ref[...] = jnp.zeros_like(stats_ref)
    for load in loads:
        load.wait()

    def make(group):
        product_nt(
            own,
            wide_rows(group),
            [(lambda rows: mixed_ref[rows, :], lambda cols: weight[cols, :])],
        )

    def finish(strip, rows, total):
        middle = source[rows, :].astype(F32) + total
        middle_ref[rows, :] = middle.astype(BF16)
        square = middle * middle
        scale = lax.rsqrt(row_mean(square) + EPS)
        normed_ref[rows, :] = (middle * scale * gain[...]).astype(BF16)
        stats_ref[0:1, :] += col_sum(square * valid[rows, :])
        stats_ref[1:2, :] += col_sum(total * total * valid[rows, :])

    line_sum(n, own, flows, lambda s: on_groups(s, length, make), finish)


def middle_sum(n, mixed, gathered, source, gain, valid):
    length, width = source.shape
    band = mixed.shape[1]
    rows = pltpu.VMEM((length, width), BF16)
    return line_call(
        middle_kernel,
        n,
        "middle_sum",
        1,
        (mixed, gathered, source, gain, valid),
        [VM, ANY, ANY, VM, VM],
        [
            jax.ShapeDtypeStruct((length, width), BF16),
            jax.ShapeDtypeStruct((length, width), BF16),
            jax.ShapeDtypeStruct((8, width), F32),
        ],
        [VM] * 3,
        [
            pltpu.VMEM((width, band), BF16),
            rows,
            rows,
            pltpu.SemaphoreType.DMA((2,)),
        ]
        + flow_scratch(length, width),
        50_000_000_000,
    )
TURN = 128
GRAD = 256


def mlp_kernel(
    n,
    normed_hbm,
    upstream_hbm,
    middle_hbm,
    gain,
    weight_hbm,
    act_hbm,
    gate_back_hbm,
    up_back_hbm,
    grads_hbm,
    low_ref,
    gain_ref,
    weight,
    normed,
    upstream,
    middle_in,
    own,
    acc,
    stage,
    load_sems,
    weight_sems,
    stage_sems,
    right_sems,
    grad_sems,
    *flows,
):
    width, feed = weight.shape[0], weight.shape[1] // 3
    length = own.shape[0]
    blocks = feed // SLAB
    chunks = length // TILE
    loads = [
        pltpu.make_async_copy(normed_hbm, normed, load_sems.at[0]),
        pltpu.make_async_copy(upstream_hbm, upstream, load_sems.at[1]),
        pltpu.make_async_copy(middle_hbm, middle_in, load_sems.at[2]),
    ]

    def columns(kind, block):
        return pl.ds(pl.multiple_of(kind * feed + block * SLAB, SLAB), SLAB)

    def weight_load(kind, block):
        return pltpu.make_async_copy(
            weight_hbm.at[:, columns(kind, block)],
            weight.at[:, columns(kind, block)],
            weight_sems.at[kind, block],
        )

    loads[0].start()
    for kind in range(3):
        weight_load(kind, 0).start()
    loads[1].start()
    for block in range(1, blocks):
        for kind in range(3):
            weight_load(kind, block).start()
    loads[2].start()
    greet(n)
    gain_ref[...] = jnp.zeros_like(gain_ref)
    loads[0].wait()
    loads[1].wait()
    backs = (act_hbm, gate_back_hbm, up_back_hbm)

    def store(kind, unit):
        slot = lax.rem(unit, 2)
        rows = pl.ds(pl.multiple_of(lax.div(unit, blocks) * TILE, TILE), TILE)
        cols = pl.ds(pl.multiple_of(lax.rem(unit, blocks) * SLAB, SLAB), SLAB)
        return pltpu.make_async_copy(
            stage.at[slot, kind], backs[kind].at[rows, cols], stage_sems.at[slot, kind]
        )

    def unit_work(unit):
        block = lax.rem(unit, blocks)
        rows = pl.ds(pl.multiple_of(lax.div(unit, blocks) * TILE, TILE), TILE)
        slot = lax.rem(unit, 2)

        @pl.when(unit < blocks)
        def _():
            for kind in range(3):
                weight_load(kind, block).wait()

        @pl.when(unit >= 2)
        def _():
            for kind in range(3):
                store(kind, unit - 2).wait()

        here = normed[rows, :]
        gate_w = weight[:, columns(0, block)]
        up_w = weight[:, columns(1, block)]
        gate = mm(here, gate_w)
        up = mm(here, up_w)
        act_grad = mm(upstream[rows, :], weight[:, columns(2, block)])
        sig = jax.nn.sigmoid(gate)
        gate_sig = gate * sig
        stage[slot, 0] = (gate_sig * up).astype(BF16)
        gate_back = (act_grad * up * (sig + gate_sig * (1.0 - sig))).astype(BF16)
        up_back = (act_grad * gate_sig).astype(BF16)
        stage[slot, 1] = gate_back
        stage[slot, 2] = up_back
        for kind in range(3):
            store(kind, unit).start()
        part = mm_nt(gate_back, gate_w) + mm_nt(up_back, up_w)

        @pl.when(block == 0)
        def _():
            acc[...] = part

        @pl.when(block > 0)
        def _():
            acc[...] += part

        @pl.when(block == blocks - 1)
        def _():
            own[rows, :] = acc[...].astype(BF16)

    units = chunks * blocks

    def first(unit, carry):
        unit_work(unit)
        return carry

    lax.fori_loop(0, blocks, first, 0)
    loads[2].wait()
    per = (length // STRIP) // chunks
    stride = per // blocks
    last = (units - blocks - 1) * stride

    turned = weight.at[:, pl.ds(0, length)]
    each = feed // GRAD
    grads = 2 * each
    turn_steps = 4
    turns = length // TURN // turn_steps
    begin = last + 1 + turn_steps
    at_once = -(-grads // (length // STRIP + (n - 1) * HOP - begin))

    def right(unit):
        return weight.at[
            pl.ds(0, length),
            pl.ds(pl.multiple_of(length + lax.rem(unit, 2) * GRAD, GRAD), GRAD),
        ]

    def made(unit):
        return weight.at[
            :, pl.ds(pl.multiple_of(length + (2 + lax.rem(unit, 2)) * GRAD, GRAD), GRAD)
        ]

    def right_load(unit, kind):
        cols = pl.ds(pl.multiple_of(lax.rem(unit, each) * GRAD, GRAD), GRAD)
        return pltpu.make_async_copy(
            backs[1 + kind].at[:, cols], right(unit), right_sems.at[lax.rem(unit, 2)]
        )

    def fetch(unit):
        for kind in range(2):

            @pl.when(lax.div(unit, each) == kind)
            def _(kind=kind):
                right_load(unit, kind).start()

    def grad_store(unit):
        cols = pl.ds(pl.multiple_of(unit * GRAD, GRAD), GRAD)
        return pltpu.make_async_copy(
            made(unit), grads_hbm.at[:, cols], grad_sems.at[lax.rem(unit, 2)]
        )

    def grad_work(unit):
        right_load(unit, 0).wait()

        @pl.when(unit >= 2)
        def _():
            grad_store(unit - 2).wait()

        here, there = right(unit), made(unit)

        def piece(p, carry):
            rows = pl.ds(pl.multiple_of(p * SLAB, SLAB), SLAB)
            there[rows, :] = mm(turned[rows, :], here[...]).astype(BF16)
            return carry

        lax.fori_loop(0, width // SLAB, piece, 0)
        grad_store(unit).start()

        @pl.when(unit + 2 < grads)
        def _():
            fetch(unit + 2)

    def work(s):
        @pl.when((s <= last) & (lax.rem(s, stride) == 0))
        def _():
            unit_work(blocks + lax.div(s, stride))

        @pl.when(s == last + 1)
        def _():
            for kind in range(3):
                store(kind, units - 2).wait()
                store(kind, units - 1).wait()
            fetch(0)
            fetch(1)

        @pl.when((s > last) & (s < begin))
        def _():
            for k in range(turns):
                at = pl.multiple_of(((s - last - 1) * turns + k) * TURN, TURN)
                turned[:, pl.ds(at, TURN)] = normed[pl.ds(at, TURN), :].T

        @pl.when(s >= begin)
        def _():
            def some(k, carry):
                unit = (s - begin) * at_once + k

                @pl.when(unit < grads)
                def _():
                    grad_work(unit)

                return carry

            lax.fori_loop(0, at_once, some, 0)

    def finish(strip, rows, total):
        middle = middle_in[rows, :].astype(F32)
        scale = lax.rsqrt(row_mean(middle * middle) + EPS)
        scaled = total * gain[...]
        inner = row_mean(scaled * middle)
        back = upstream[rows, :].astype(F32) + scale * (scaled - middle * (scale * scale * inner))
        low_ref[rows, :] = back.astype(BF16)
        gain_ref[0:1, :] += col_sum(total * middle * scale)

    line_sum(n, own, flows, work, finish)
    grad_store(grads - 2).wait()
    grad_store(grads - 1).wait()


def mlp_sum(n, normed, upstream, middle, gain, weights):
    length, width = normed.shape
    feed = weights.shape[1] // 3
    rows = pltpu.VMEM((length, width), BF16)
    low = jax.ShapeDtypeStruct((length, feed), BF16)
    return line_call(
        mlp_kernel,
        n,
        "mlp_sum",
        2,
        (normed, upstream, middle, gain, weights),
        [ANY, ANY, ANY, VM, ANY],
        [low] * 3
        + [
            jax.ShapeDtypeStruct((width, 2 * feed), BF16),
            jax.ShapeDtypeStruct((length, width), BF16),
            jax.ShapeDtypeStruct((8, width), F32),
        ],
        [ANY] * 4 + [VM] * 2,
        [
            pltpu.VMEM((width, 3 * feed), BF16),
            rows,
            rows,
            rows,
            rows,
            pltpu.VMEM((TILE, width), F32),
            pltpu.VMEM((2, 3, TILE, SLAB), BF16),
            pltpu.SemaphoreType.DMA((3,)),
            pltpu.SemaphoreType.DMA((3, feed // SLAB)),
            pltpu.SemaphoreType.DMA((2, 3)),
            pltpu.SemaphoreType.DMA((2,)),
            pltpu.SemaphoreType.DMA((2,)),
        ]
        + flow_scratch(length, width),
        60_000_000_000,
    )
def scatter(length, peers, result, out_hbm, sems):
    send_sems, recv_sems, home_sems = sems
    mine = lax.axis_index("fsdp")
    strips, local = length // STRIP, length // peers
    per = local // STRIP
    shift = mine * per

    def place(strip):
        at = lax.rem(strip + shift, strips)
        inside = pl.ds(pl.multiple_of(lax.rem(at, per) * STRIP, STRIP), STRIP)
        rows = pl.ds(pl.multiple_of(at * STRIP, STRIP), STRIP)
        return lax.div(at, per), rows, inside

    def away(strip):
        owner, rows, inside = place(strip)
        return pltpu.make_async_remote_copy(
            src_ref=result.at[rows],
            dst_ref=out_hbm.at[mine, inside],
            send_sem=send_sems.at[strip],
            recv_sem=recv_sems.at[mine],
            device_id={"fsdp": owner},
            device_id_type=MESH,
        )

    def home(strip):
        _, rows, inside = place(strip)
        return pltpu.make_async_copy(
            result.at[rows], out_hbm.at[mine, inside], home_sems.at[lax.rem(strip, per)]
        )

    def send(strip):
        @pl.when(strip < per)
        def _():
            home(strip).start()

        @pl.when(strip >= per)
        def _():
            away(strip).start()

    def drain():
        for strip in range(per):
            home(strip).wait()

        def sent(strip, carry):
            away(strip).wait_send()
            return carry

        lax.fori_loop(per, strips, sent, 0)
        for ahead in range(1, peers):
            peer = lax.rem(mine + ahead, peers)
            pltpu.make_async_remote_copy(
                src_ref=result.at[pl.ds(0, local)],
                dst_ref=out_hbm.at[peer],
                send_sem=send_sems.at[0],
                recv_sem=recv_sems.at[peer],
                device_id={"fsdp": peer},
                device_id_type=MESH,
            ).wait_recv()

    return send, drain, shift


def scatter_scratch(length, peers):
    return [
        pltpu.SemaphoreType.DMA((length // STRIP,)),
        pltpu.SemaphoreType.DMA((peers,)),
        pltpu.SemaphoreType.DMA((length // peers // STRIP,)),
    ]


def on_shifted_groups(s, shift, strips, make):
    full = TILE // STRIP
    base = lax.rem(s + shift, strips)

    @pl.when((s == 0) | ((lax.rem(base, full) == 0) & (s <= strips - full)))
    def _():
        make(lax.div(base, full))


def output_kernel(
    n,
    peers,
    act_hbm,
    weight_hbm,
    middle_hbm,
    upstream_hbm,
    source_hbm,
    low_hbm,
    dq_hbm,
    dk_hbm,
    dv_hbm,
    mixed_hbm,
    gain,
    valid,
    out_hbm,
    stats_ref,
    grads_hbm,
    result,
    act,
    down,
    middle,
    upstream_t,
    normed_t,
    low_t,
    rights,
    own,
    slices,
    stage,
    load_sems,
    slice_sems,
    stage_sems,
    send_sems,
    recv_sems,
    home_sems,
    *flows,
):
    length, width = own.shape
    feed = act.shape[1]
    loads = [
        pltpu.make_async_copy(act_hbm, act, load_sems.at[0]),
        pltpu.make_async_copy(weight_hbm.at[:, pl.ds(2 * feed, feed)], down, load_sems.at[1]),
        pltpu.make_async_copy(middle_hbm, middle, load_sems.at[2]),
    ]
    band = dq_hbm.shape[1]
    for k, ref in enumerate((dq_hbm, dk_hbm, dv_hbm, mixed_hbm)):
        loads.append(
            pltpu.make_async_copy(
                ref, rights.at[:, k * band : (k + 1) * band], load_sems.at[3 + k]
            )
        )
    turned = (upstream_t, normed_t, low_t)
    turns = length // TURN

    def slice_load(kind, turn):
        rows = pl.ds(pl.multiple_of(turn * TURN, TURN), TURN)
        slot = lax.rem(turn, 2)
        return pltpu.make_async_copy(
            (upstream_hbm, source_hbm, low_hbm)[kind].at[rows],
            slices.at[slot, kind],
            slice_sems.at[slot, kind],
        )

    loads[0].start()
    loads[1].start()
    for turn in range(2):
        for kind in range(3):
            slice_load(kind, turn).start()
    for load in loads[2:]:
        load.start()
    greet(n, peers)
    stats_ref[...] = jnp.zeros_like(stats_ref)
    loads[0].wait()
    loads[1].wait()

    def make(group):
        product_nt(
            own, wide_rows(group), [(lambda rows: act[rows, :], lambda cols: down[cols, :])]
        )

    edges = (0, feed // GRAD, (feed + 3 * band) // GRAD, (feed + 4 * band) // GRAD)
    units = edges[3]

    def store(unit):
        cols = pl.ds(pl.multiple_of(unit * GRAD, GRAD), GRAD)
        slot = lax.rem(unit, 2)
        return pltpu.make_async_copy(stage.at[slot], grads_hbm.at[:, cols], stage_sems.at[slot])

    def grad_unit(unit):
        slot = lax.rem(unit, 2)

        @pl.when(unit >= 2)
        def _():
            store(unit - 2).wait()

        for kind, (left, right) in enumerate(
            ((upstream_t, act), (normed_t, rights), (low_t, rights))
        ):
            first = 0 if kind == 0 else edges[1]

            @pl.when((unit >= edges[kind]) & (unit < edges[kind + 1]))
            def _(left=left, right=right, first=first):
                cols = pl.ds(pl.multiple_of((unit - first) * GRAD, GRAD), GRAD)

                def piece(p, carry):
                    rows = pl.ds(pl.multiple_of(p * SLAB, SLAB), SLAB)
                    stage[slot, rows, :] = mm(left[rows, :], right[:, cols]).astype(BF16)
                    return carry

                lax.fori_loop(0, width // SLAB, piece, 0)

        store(unit).start()

    send, drain, shift = scatter(
        length, peers, result, out_hbm, (send_sems, recv_sems, home_sems)
    )

    def work(s):
        on_shifted_groups(s, shift, length // STRIP, make)

        @pl.when(s < turns)
        def _():
            slot = lax.rem(s, 2)
            cols = pl.ds(pl.multiple_of(s * TURN, TURN), TURN)
            for kind in range(3):
                slice_load(kind, s).wait()
                here = slices[slot, kind]
                if kind == 1:
                    here = here.astype(F32)
                    scale = lax.rsqrt(row_mean(here * here) + EPS)
                    here = (here * scale * gain[...]).astype(BF16)
                turned[kind][:, cols] = here.T

                @pl.when(s + 2 < turns)
                def _(kind=kind):
                    slice_load(kind, s + 2).start()

        @pl.when(s == turns)
        def _():
            for load in loads[3:]:
                load.wait()

        @pl.when((s >= turns) & (s < turns + units))
        def _():
            grad_unit(s - turns)

        @pl.when(s == 0)
        def _():
            loads[2].wait()

    def finish(strip, rows, total):
        result[rows, :] = (middle[rows, :].astype(F32) + total).astype(BF16)
        send(strip)
        stats_ref[0:1, :] += col_sum(total * total * valid[rows, :])

    line_sum(n, own, flows, work, finish, shift)
    drain()
    store(units - 2).wait()
    store(units - 1).wait()


def output_sum(
    n, peers, act, weights, middle, upstream, source, low, dq, dk, dv, mixed, gain, valid
):
    length, width = middle.shape
    feed = act.shape[1]
    rows = pltpu.VMEM((length, width), BF16)
    wide = pltpu.VMEM((length, feed), BF16)
    turned = pltpu.VMEM((width, length), BF16)
    return line_call(
        lambda count, *refs: output_kernel(count, peers, *refs),
        n,
        "output_sum",
        3,
        (act, weights, middle, upstream, source, low, dq, dk, dv, mixed, gain, valid),
        [ANY] * 10 + [VM] * 2,
        [
            jax.ShapeDtypeStruct((peers, length // peers, width), BF16),
            jax.ShapeDtypeStruct((8, width), F32),
            jax.ShapeDtypeStruct((width, feed + 4 * dq.shape[1]), BF16),
        ],
        [ANY, VM, ANY],
        [
            rows,
            wide,
            pltpu.VMEM((width, feed), BF16),
            rows,
            turned,
            turned,
            turned,
            pltpu.VMEM((length, 4 * dq.shape[1]), BF16),
            rows,
            pltpu.VMEM((2, 3, TURN, width), BF16),
            pltpu.VMEM((2, width, GRAD), BF16),
            pltpu.SemaphoreType.DMA((7,)),
            pltpu.SemaphoreType.DMA((2, 3)),
            pltpu.SemaphoreType.DMA((2,)),
        ]
        + scatter_scratch(length, peers)
        + flow_scratch(length, width),
        60_000_000_000,
    )


def input_kernel(
    n,
    peers,
    dq_ref,
    dk_ref,
    dv_ref,
    weight_hbm,
    source_hbm,
    back_hbm,
    gain,
    rows_ref,
    out_hbm,
    small_ref,
    weight,
    source,
    back,
    own,
    result,
    small_own,
    small_got,
    load_sems,
    small_send,
    small_recv,
    send_sems,
    recv_sems,
    home_sems,
    *flows,
):
    length, width = own.shape
    band = dq_ref.shape[1]
    mine = lax.axis_index("fsdp")
    share = width // peers
    strips = length // STRIP
    scatter_sems = (send_sems, recv_sems, home_sems)
    loads = [
        pltpu.make_async_copy(weight_hbm.at[:, pl.ds(0, 3 * band)], weight, load_sems.at[0]),
        pltpu.make_async_copy(source_hbm, source, load_sems.at[1]),
        pltpu.make_async_copy(back_hbm, back, load_sems.at[2]),
    ]
    for load in loads:
        load.start()
    greet(n, peers)
    small_own[...] = rows_ref[...]
    small_own[0:1, :] = jnp.zeros((1, width), F32)
    loads[0].wait()
    halves = [
        (lambda rows, ref=ref: ref[rows, :], lambda cols, k=k: weight[cols, k * band : (k + 1) * band])
        for k, ref in enumerate((dq_ref, dk_ref, dv_ref))
    ]
    send, drain, shift = scatter(length, peers, result, out_hbm, scatter_sems)

    def make(group):
        product_nt(own, wide_rows(group), halves)

    def work(s):
        on_shifted_groups(s, shift, strips, make)

        @pl.when(s == 0)
        def _():
            loads[1].wait()
            loads[2].wait()

    def finish(strip, rows, total):
        here = source[rows, :].astype(F32)
        scale = lax.rsqrt(row_mean(here * here) + EPS)
        scaled = total * gain[...]
        inner = row_mean(scaled * here)
        result[rows, :] = (
            back[rows, :].astype(F32) + scale * (scaled - here * (scale * scale * inner))
        ).astype(BF16)
        small_own[0:1, :] += col_sum(total * here * scale)

        send(strip)

    line_sum(n, own, flows, work, finish, shift)

    def small(ahead):
        peer = lax.rem(mine + ahead, peers)
        cols = pl.ds(pl.multiple_of(peer * share, share), share)
        return pltpu.make_async_remote_copy(
            src_ref=small_own.at[:, cols],
            dst_ref=small_got.at[mine],
            send_sem=small_send.at[ahead],
            recv_sem=small_recv.at[mine],
            device_id={"fsdp": peer},
            device_id_type=MESH,
        )

    for ahead in range(1, peers):
        small(ahead).start()
    total = small_own[:, pl.ds(pl.multiple_of(mine * share, share), share)]
    for ahead in range(1, peers):
        peer = lax.rem(mine + ahead, peers)
        pltpu.make_async_remote_copy(
            src_ref=small_own.at[:, pl.ds(0, share)],
            dst_ref=small_got.at[peer],
            send_sem=small_send.at[ahead],
            recv_sem=small_recv.at[peer],
            device_id={"fsdp": peer},
            device_id_type=MESH,
        ).wait_recv()
        total = total + small_got[peer]
        small(ahead).wait_send()
    drain()
    small_ref[...] = total


def input_sum(n, peers, dq, dk, dv, weights, source, back, gain, small_rows):
    length, width = source.shape
    band = dq.shape[1]
    rows = pltpu.VMEM((length, width), BF16)
    share = width // peers
    return line_call(
        lambda count, *refs: input_kernel(count, peers, *refs),
        n,
        "input_sum",
        4,
        (dq, dk, dv, weights, source, back, gain, small_rows),
        [VM, VM, VM, ANY, ANY, ANY, VM, VM],
        [
            jax.ShapeDtypeStruct((peers, length // peers, width), BF16),
            jax.ShapeDtypeStruct((8, share), F32),
        ],
        [ANY, VM],
        [
            pltpu.VMEM((width, 3 * band), BF16),
            rows,
            rows,
            rows,
            rows,
            pltpu.VMEM((8, width), F32),
            pltpu.VMEM((peers, 8, share), F32),
            pltpu.SemaphoreType.DMA((3,)),
            pltpu.SemaphoreType.DMA((peers,)),
            pltpu.SemaphoreType.DMA((peers,)),
        ]
        + scatter_scratch(length, peers)
        + flow_scratch(length, width),
        50_000_000_000,
    )
def settle_kernel(in_ref, out_ref):
    out_ref[...] = in_ref[...]


def settle(values):
    block = pl.BlockSpec((1,) + values.shape[1:], lambda i: (i, 0, 0))
    return pl.pallas_call(
        settle_kernel,
        grid=(values.shape[0],),
        in_specs=[block],
        out_specs=block,
        out_shape=jax.ShapeDtypeStruct(values.shape, values.dtype),
        name="settle",
    )(values)


def per_device(
    mesh_sizes,
    inputs,
    cotangent,
    piece_start,
    piece_image,
    valid_mask,
    query_weight,
    key_weight,
    value_weight,
    output_weight,
    attn_gain,
    gate_weight,
    up_weight,
    down_weight,
    mlp_gain,
):
    spread, line = mesh_sizes
    seqs, local, width = inputs.shape
    length = valid_mask.shape[1]
    band = query_weight.shape[1]
    feed = gate_weight.shape[1]
    mine = lax.axis_index("fsdp")

    def swap(values):
        return lax.all_to_all(values, "fsdp", split_axis=0, concat_axis=0, tiled=True)

    def shares(terms):
        return lax.psum_scatter(terms, "fsdp", scatter_dimension=0, tiled=True)

    gains = lax.all_gather(jnp.stack([attn_gain, mlp_gain]), "fsdp", axis=1, tiled=True)
    gains, inputs = lax.optimization_barrier((gains, inputs))
    gains = gains.astype(F32)
    attn_g, mlp_g = gains[0:1], gains[1:2]
    attn_w = lax.all_gather(
        jnp.concatenate([query_weight, key_weight, value_weight, output_weight.T], axis=1),
        "fsdp",
        axis=0,
        tiled=True,
    )
    mlp_w = lax.all_gather(
        jnp.concatenate([gate_weight, up_weight, down_weight.T], axis=1),
        "fsdp",
        axis=0,
        tiled=True,
    )
    source = swap(inputs).reshape(length, width)
    source, cotangent = lax.optimization_barrier((source, cotangent))
    upstream = swap(cotangent).reshape(length, width)

    places = jnp.arange(length, dtype=jnp.int32)
    cosine, sine = rope_tables(places, HD)
    signs = jnp.where(jnp.arange(HD) < HD // 2, -1.0, 1.0).astype(F32)
    cosine = jnp.concatenate([cosine, cosine], axis=1)
    sine = jnp.concatenate([sine * signs, sine * signs], axis=1)
    valid_row = lax.dynamic_index_in_dim(valid_mask, mine, 0, keepdims=False)
    valid = valid_row.astype(F32)[:, None]
    bias = jnp.where(valid_row > 0, 0.0, NEG).astype(F32)[:, None]
    starts = lax.dynamic_index_in_dim(piece_start, mine, 0, keepdims=False)
    images = lax.dynamic_index_in_dim(piece_image, mine, 0, keepdims=False)
    image = image_of(jnp.arange(length // TILE, dtype=jnp.int32) * TILE, starts, images).astype(
        jnp.int32
    )

    residual = source.astype(F32)
    scale_one = lax.rsqrt(jnp.mean(residual * residual, axis=1, keepdims=True) + EPS)
    normed_one = (residual * scale_one * attn_g).astype(BF16)
    qkv = mm(normed_one, attn_w[:, : 3 * band])
    queries, keys, values, mixed, lse = attend(qkv, cosine, sine, bias, image)
    middle, normed_two, stats = middle_sum(line, mixed, attn_w, source, mlp_g, valid)
    act, _, _, front_terms, middle_low, mlp_gain_sum = mlp_sum(
        line, normed_two, upstream, middle, mlp_g, mlp_w
    )
    front_grads = shares(front_terms)
    mixed_back = mm(middle_low, attn_w[:, 3 * band :]).astype(BF16)
    dq, dk, dv = attend_back(
        queries, keys, values, mixed_back, mixed, lse, cosine, sine, bias, image
    )
    output, mlp_stats, late_terms = output_sum(
        line,
        spread,
        act,
        mlp_w,
        middle,
        upstream,
        source,
        middle_low,
        dq,
        dk,
        dv,
        mixed,
        attn_g,
        valid,
    )
    late_terms, front_grads = lax.optimization_barrier((late_terms, front_grads))
    late_grads = shares(late_terms)
    output = settle(output)
    sums = jnp.stack([jnp.sum(stats[0]), jnp.sum(stats[1]), jnp.sum(mlp_stats[0])])
    small_rows = jnp.concatenate(
        [
            jnp.zeros((1, width), F32),
            mlp_gain_sum[0:1],
            jnp.broadcast_to(sums[:, None], (3, width)),
            jnp.zeros((3, width), F32),
        ]
    )
    input_grad, small = input_sum(
        line, spread, dq, dk, dv, attn_w, source, middle_low, attn_g, small_rows
    )
    input_grad = settle(input_grad)
    late_grads, output, input_grad = lax.optimization_barrier((late_grads, output, input_grad))
    late_grads = late_grads.astype(F32)
    attn_grads = late_grads[:, feed:]
    count = jnp.sum(valid_mask).astype(F32) * width
    roots = jnp.sqrt(small[2:5, 0] / count)
    return (
        output,
        input_grad,
        attn_grads[:, :band],
        attn_grads[:, band : 2 * band],
        attn_grads[:, 2 * band : 3 * band],
        attn_grads[:, 3 * band :].T,
        small[0],
        front_grads[:, :feed].astype(F32),
        front_grads[:, feed:].astype(F32),
        late_grads[:, :feed].T,
        small[1],
        roots[0],
        roots[1],
        roots[2],
    )


def solution(mesh):
    placed = (
        P(None, "fsdp", None),
        P(None, "fsdp", None),
        P(),
        P(),
        P(),
        P("fsdp", "dp"),
        P("fsdp", "dp"),
        P("fsdp", "dp"),
        P("dp", "fsdp"),
        P("fsdp"),
        P("fsdp", "dp"),
        P("fsdp", "dp"),
        P("dp", "fsdp"),
        P("fsdp"),
    )
    spread, line = mesh.shape["fsdp"], mesh.shape["dp"]

    def whole(*arrays):
        seqs, length, _ = arrays[0].shape
        own_sequence = seqs == spread and length % (2 * TILE) == 0 and line > 1
        each = functools.partial(per_device, (spread, line)) if own_sequence else per_device_gather
        return jax.shard_map(
            each,
            mesh=mesh,
            in_specs=placed,
            out_specs=(
                P(None, "fsdp", None),
                P(None, "fsdp", None),
                P("fsdp", "dp"),
                P("fsdp", "dp"),
                P("fsdp", "dp"),
                P("dp", "fsdp"),
                P("fsdp"),
                P("fsdp", "dp"),
                P("fsdp", "dp"),
                P("dp", "fsdp"),
                P("fsdp"),
                P(),
                P(),
                P(),
            ),
            check_vma=False,
        )(*arrays)

    return whole
```
